256 devices in a mesh: seq: 32 (over x, y, core), tp: 8 (over z).
Axes of the slice: x: 4, y: 4, z: 8, core: 2. Of those that a mesh axis runs over, the one named last changes fastest.
Arguments:
- queries: bfloat16 [16384, 8192], P('seq', 'tp'), may hold values from -6 to 6
- keys: bfloat16 [16384, 8192], P('seq', 'tp'), may hold values from -0.5 to 0.5
- values: bfloat16 [16384, 8192], P('seq', 'tp'), may hold values from -6 to 6
- gate: bfloat16 [16384, 8192], P('seq', 'tp'), may hold values from -6 to 6
- log_decay: float32 [16384, 64], P('seq', 'tp'), may hold values from -0.8 to 0
- out_grad: bfloat16 [16384, 8192], P('seq', 'tp'), may hold values from -6 to 6
Outputs:
- output: bfloat16 [16384, 8192], P('seq', 'tp')
- query_grad: bfloat16 [16384, 8192], P('seq', 'tp')
- key_grad: bfloat16 [16384, 8192], P('seq', 'tp')
- value_grad: bfloat16 [16384, 8192], P('seq', 'tp')
- gate_grad: bfloat16 [16384, 8192], P('seq', 'tp')
The draws below stay inside these ranges and needn't reach their ends.
All inputs are finite; a program needn't handle non-finite values.
Results may differ from the reference program's by a relative error of at most 0.0051.
Values sent between devices are 32-bit elements; how exact they have to be, the bound alone decides.
No kernel may reach another device: no remote copies, remote signals or barrier semaphores. Data moves between devices by JAX's collectives and lax.ppermute only.
A program may use at most 128 MiB of HBM per device.

```python
import jax
import jax.numpy as jnp
from jax import lax

HEAD_COUNT = 64
HEAD = 128
TOK_DEV = 512
TOKEN_COUNT = 16384
N_SEQ = 32


def draw_log_decay(key, part):
    every_key = jax.random.split(jax.random.fold_in(key, 7), 6)
    share = 0.5
    slow = jax.random.uniform(every_key[0], (HEAD_COUNT,)) < share
    slow_rate = jnp.exp(jax.random.uniform(every_key[1], (HEAD_COUNT,), jnp.float32, jnp.log(0.05), jnp.log(0.5))) / TOKEN_COUNT
    fast_rate = jax.random.uniform(every_key[2], (HEAD_COUNT,), jnp.float32, 1.0 / 50.0, 1.0 / 30.0)
    decay_rate = jnp.where(slow, slow_rate, fast_rate)
    random_noise = jax.random.uniform(every_key[3], (TOKEN_COUNT, HEAD_COUNT), jnp.float32, 0.5, 1.5)
    decay_spike = jax.random.uniform(every_key[4], (TOKEN_COUNT, HEAD_COUNT)) < 3.0 / TOKEN_COUNT
    decay_falloff = jnp.log(jax.random.uniform(every_key[5], (TOKEN_COUNT, HEAD_COUNT), jnp.float32, 0.5, 0.8))
    return (-decay_rate[None, :] * random_noise + jnp.where(decay_spike, decay_falloff, 0.0)).astype(jnp.float32)


def steps_of(key, shape, cuts, smallest, top_value):
    def one(position, parts):
        draws = jax.random.uniform(jax.random.fold_in(jax.random.fold_in(key, 6), position), (parts,), jnp.float32, smallest / len(cuts), top_value / len(cuts))
        return jnp.repeat(jnp.exp(draws), shape[position] // parts).reshape((-1,) + (1,) * (len(shape) - position - 1))

    loudness = one(*cuts[0])
    for cut in cuts[1:]:
        loudness = loudness * one(*cut)
    return loudness


def scatter_about(own_key, extent, scale, reach, cuts=(), dtype=jnp.bfloat16):
    drawn = scale * jax.random.normal(own_key, extent, jnp.float32)
    if cuts:
        drawn = drawn * steps_of(own_key, extent, cuts, -0.22, 0.18)
    return jnp.clip(drawn, -reach, reach).astype(dtype)


def setup_inputs(seed: int = 0) -> dict:
    key_of = jax.random.split(jax.random.key(seed), 7)
    queries = scatter_about(key_of[0], (TOKEN_COUNT, HEAD_COUNT * HEAD), 1.0, 6.0, ((0, 32), (1, 8)))
    keys = scatter_about(key_of[1], (TOKEN_COUNT, HEAD_COUNT * HEAD), HEAD ** -0.5, 0.5, ((0, 32), (1, 8)))
    values = scatter_about(key_of[2], (TOKEN_COUNT, HEAD_COUNT * HEAD), 1.0, 6.0, ((0, 32), (1, 8)))
    gate = scatter_about(key_of[3], (TOKEN_COUNT, HEAD_COUNT * HEAD), 1.0, 6.0, ((0, 32), (1, 8)))
    log_decay = draw_log_decay(jax.random.fold_in(key_of[6], 71), 0)
    out_grad = scatter_about(key_of[5], (TOKEN_COUNT, HEAD_COUNT * HEAD), 1.0, 6.0, ((0, 32), (1, 8)))
    return {"queries": queries, "keys": keys, "values": values, "gate": gate, "log_decay": log_decay, "out_grad": out_grad}


HIGH = lax.Precision.HIGHEST

def decay_table(within):
    gap = within.T[:, :, None] - within.T[:, None, :]
    rows = lax.broadcasted_iota(jnp.int32, gap.shape, 1)
    cols = lax.broadcasted_iota(jnp.int32, gap.shape, 2)
    return jnp.where(rows >= cols, jnp.exp(jnp.minimum(gap, 0.0)), 0.0)

def block_probs(qh, kh, decay):
    scores = jnp.einsum('thd,shd->hts', qh.astype(jnp.float32), kh.astype(jnp.float32))
    return (scores * decay).astype(jnp.bfloat16)

def forward_block(state, pieces):
    qh, kh, vh, rates = pieces
    within = jnp.cumsum(rates, axis=0)
    last = within[-1]
    decay = decay_table(within)
    probs = block_probs(qh, kh, decay)
    qf = qh.astype(jnp.float32)
    kf = kh.astype(jnp.float32)
    vf = vh.astype(jnp.float32)
    intra = jnp.einsum('hts,shd->thd', probs.astype(jnp.float32), vf)
    inter = jnp.exp(within)[:, :, None] * jnp.einsum('thd,hde->the', qf, state, precision=HIGH)
    tail = jnp.exp(last[None, :] - within)
    local = jnp.einsum('thd,the->hde', kf * tail[:, :, None], vf, precision=HIGH)
    fresh = jnp.exp(last)[:, None, None] * state + local
    return (fresh, (intra + inter, state))

def backward_block(grad_state, pieces):
    qh, kh, vh, rates, grad_b, state = pieces
    within = jnp.cumsum(rates, axis=0)
    last = within[-1]
    decay = decay_table(within)
    probs = block_probs(qh, kh, decay)
    qf = qh.astype(jnp.float32)
    kf = kh.astype(jnp.float32)
    vf = vh.astype(jnp.float32)
    gradf = grad_b.astype(jnp.float32)
    pgrad = (jnp.einsum('thd,shd->hts', gradf, vf) * decay).astype(jnp.bfloat16).astype(jnp.float32)
    grow = jnp.exp(within)[:, :, None]
    tail = jnp.exp(last[None, :] - within)[:, :, None]
    query_grad = jnp.einsum('hts,shd->thd', pgrad, kf) + grow * jnp.einsum('the,hde->thd', gradf, state, precision=HIGH)
    key_grad = jnp.einsum('hts,thd->shd', pgrad, qf) + tail * jnp.einsum('the,hde->thd', vf, grad_state, precision=HIGH)
    value_grad = jnp.einsum('hts,thd->shd', probs.astype(jnp.float32), gradf) + tail * jnp.einsum('thd,hde->the', kf, grad_state, precision=HIGH)
    weighted = jnp.einsum('thd,the->hde', qf * grow, gradf, precision=HIGH)
    fresh = weighted + jnp.exp(last)[:, None, None] * grad_state
    return (fresh, (query_grad.astype(jnp.bfloat16), key_grad.astype(jnp.bfloat16), value_grad.astype(jnp.bfloat16)))

def reference(queries, keys, values, gate, log_decay, out_grad):
    blocks = N_SEQ
    width = HEAD_COUNT * HEAD
    qb = queries.reshape(blocks, TOK_DEV, HEAD_COUNT, HEAD)
    kb = keys.reshape(blocks, TOK_DEV, HEAD_COUNT, HEAD)
    vb = values.reshape(blocks, TOK_DEV, HEAD_COUNT, HEAD)
    rb = log_decay.reshape(blocks, TOK_DEV, HEAD_COUNT)
    start = jnp.zeros((HEAD_COUNT, HEAD, HEAD), jnp.float32)
    unused, (attn_blocks, states) = lax.scan(forward_block, start, (qb, kb, vb, rb))
    attn = attn_blocks.reshape(TOKEN_COUNT, width)
    scale = lax.rsqrt(lax.optimization_barrier(jnp.sum(attn * attn, axis=1)) / width + 1e-06)
    normed = attn * scale[:, None]
    sig = jax.nn.sigmoid(gate.astype(jnp.float32))
    output = (normed * sig).astype(jnp.bfloat16)
    upstream = out_grad.astype(jnp.float32)
    dnorm = upstream * sig
    gate_grad = (upstream * normed * sig * (1.0 - sig)).astype(jnp.bfloat16)
    center = lax.optimization_barrier(jnp.sum(dnorm * normed, axis=1)) / width
    attn_grad = (scale[:, None] * (dnorm - normed * center[:, None])).astype(jnp.bfloat16)
    gb = attn_grad.reshape(blocks, TOK_DEV, HEAD_COUNT, HEAD)
    unused2, (dq, dk, dv) = lax.scan(backward_block, start, (qb, kb, vb, rb, gb, states), reverse=True)
    return (output, dq.reshape(TOKEN_COUNT, width), dk.reshape(TOKEN_COUNT, width), dv.reshape(TOKEN_COUNT, width), gate_grad)
```

```python
import jax
import jax.numpy as jnp
from jax import lax
from jax.experimental import pallas as pl
from jax.experimental.pallas import tpu as pltpu
from jax.sharding import Mesh
from jax.sharding import PartitionSpec as P

HEAD_COUNT = 64
HEAD = 128
SEQ = ("x", "y", "c")
CHIPS = ("x", "y")
HIGH = lax.Precision.HIGHEST
F32 = jnp.float32
BF16 = jnp.bfloat16
PAD = 8

NN = (((1,), (0,)), ((), ()))
NT = (((1,), (1,)), ((), ()))
TN = (((0,), (0,)), ((), ()))


def dot(a, b, dims, precision=None):
    return lax.dot_general(a, b, dims, precision=precision, preferred_element_type=F32)


def halves(x):
    high = x.astype(BF16)
    return high, (x - high.astype(F32)).astype(BF16)


def as_column(row):
    return jnp.transpose(jnp.broadcast_to(row, (HEAD, row.shape[1])))


def sigmoid(x):
    return 1.0 / (1.0 + jnp.exp(-x))


def params(mib=40):
    return pltpu.CompilerParams(
        dimension_semantics=("arbitrary",), vmem_limit_bytes=mib * 2**20
    )


def outer_state(wide, narrow):
    both = dot(narrow, jnp.concatenate(halves(wide), axis=1), TN)
    return both[:, :HEAD] + both[:, HEAD:]


def put_state(ref, i, state, factor):
    ref[i, 0:HEAD, :] = state
    ref[i, HEAD : HEAD + PAD, :] = jnp.broadcast_to(factor, (PAD, HEAD))


def local_kernel(core_ref, rate_ref, k_ref, v_ref, within_ref, theirs_ref, mine_ref):
    step = pl.program_id(0)
    tokens = rate_ref.shape[0]
    group = k_ref.shape[1] // HEAD

    @pl.when(step == 0)
    def _():
        early = lax.broadcasted_iota(jnp.int32, (tokens, tokens), 0)
        late = lax.broadcasted_iota(jnp.int32, (tokens, tokens), 1)
        upto = (early <= late).astype(F32)
        within_ref[...] = dot(rate_ref[...], upto, TN, HIGH)

    first = (core_ref[0] ^ (1 - step)) * group

    def part(out_ref):
        for i in range(group):
            within = within_ref[pl.ds(first + i, 1), :]
            last = within[:, tokens - 1 :]
            tail = as_column(jnp.exp(last - within))
            cols = slice(i * HEAD, (i + 1) * HEAD)
            scaled = k_ref[:, cols].astype(F32) * tail
            put_state(out_ref, i, outer_state(scaled, v_ref[:, cols]), jnp.exp(last))

    @pl.when(step == 0)
    def _():
        part(theirs_ref)

    @pl.when(step == 1)
    def _():
        part(mine_ref)


def combine_kernel(lead_ref, mine_ref, other_ref, out_ref):
    lead = lead_ref[0] == 1
    group = mine_ref.shape[0]
    rows = HEAD // 4
    for i in range(group):
        own = mine_ref[i, HEAD : HEAD + PAD, :]
        far = other_ref[i, HEAD : HEAD + PAD, :]
        mine = mine_ref[i, 0:HEAD, :]
        other = other_ref[i, 0:HEAD, :]
        both = jnp.where(lead, far[0:1] * mine + other, own[0:1] * other + mine)
        for j in range(4):
            out_ref[4 * i + j, 0:rows, :] = both[j * rows : (j + 1) * rows]
            out_ref[4 * i + j, rows : rows + PAD, :] = own * far


def scan_kernel(reverse, in_ref, out_ref):
    chips, rows = out_ref.shape[0], out_ref.shape[1]
    state = jnp.zeros(out_ref.shape[1:], F32)
    for n in reversed(range(chips)) if reverse else range(chips):
        out_ref[n] = state
        state = in_ref[n, rows : rows + 1, :] * state + in_ref[n, 0:rows, :]


def decay_block(within, column, start, size, width):
    gap = jnp.concatenate([column[start : start + size]] * (width // HEAD), axis=1)
    gap = gap - within[:, :width]
    rows = start + lax.broadcasted_iota(jnp.int32, gap.shape, 0)
    cols = lax.broadcasted_iota(jnp.int32, gap.shape, 1)
    return jnp.where(rows >= cols, jnp.exp(jnp.minimum(gap, 0.0)), 0.0)


def inside_kernel(within_ref, q_ref, k_ref, v_ref, probs_ref, intra_ref):
    within = within_ref[pl.ds(pl.program_id(0), 1), :]
    column = as_column(within)
    tokens = q_ref.shape[0]
    size = tokens // 2
    for start in (0, size):
        width = start + size
        scores = dot(q_ref[start:width, :], k_ref[0:width, :], NT)
        probs = (scores * decay_block(within, column, start, size, width)).astype(BF16)
        probs_ref[0, start:width, 0:width] = probs
        intra_ref[start:width, :] = dot(probs, v_ref[0:width, :], NN)


def pick_state(follows, chip_ref, lead_ref, i):
    chip = chip_ref[i]
    return jnp.where(
        follows, lead_ref[i, HEAD : HEAD + 1, :] * chip + lead_ref[i, 0:HEAD, :], chip
    )


def attn_kernel(
    core_ref, within_ref, q_ref, intra_ref, gate_ref, up_ref,
    chip_mine_ref, chip_other_ref, lead_mine_ref, lead_other_ref,
    attn_ref, state_ref, sums_ref, square_ref, inner_ref,
):
    step = pl.program_id(0)
    group = chip_mine_ref.shape[0]
    first = (core_ref[0] ^ step) * group

    @pl.when(step == 0)
    def _():
        square_ref[...] = jnp.zeros_like(square_ref)
        inner_ref[...] = jnp.zeros_like(inner_ref)

    def part(chip_ref, lead_ref):
        for i in range(group):
            cols = slice(i * HEAD, (i + 1) * HEAD)
            state = pick_state(core_ref[0] == 1, chip_ref, lead_ref, i)
            state_ref[i] = state
            grow = as_column(jnp.exp(within_ref[pl.ds(first + i, 1), :]))
            q = q_ref[:, cols]
            inter = dot(
                jnp.concatenate([q, q], axis=1), jnp.concatenate(halves(state), axis=1), NT
            )
            attn = intra_ref[:, cols] + grow * inter
            attn_ref[:, cols] = attn
            dnorm = up_ref[:, cols].astype(F32) * sigmoid(gate_ref[:, cols].astype(F32))
            square_ref[...] += attn * attn
            inner_ref[...] += dnorm * attn

    @pl.when(step == 0)
    def _():
        part(chip_mine_ref, lead_mine_ref)

    @pl.when(step == 1)
    def _():
        part(chip_other_ref, lead_other_ref)
        ones = jnp.ones((8, HEAD), F32)
        square = dot(ones, square_ref[...], NT, HIGH)
        inner = dot(ones, inner_ref[...], NT, HIGH)
        rows = lax.broadcasted_iota(jnp.int32, (8, HEAD), 0)
        packed = jnp.zeros((8, HEAD), F32)
        for i in range(4):
            cols = slice(i * HEAD, (i + 1) * HEAD)
            packed = jnp.where(rows == i, square[:, cols], packed)
            packed = jnp.where(rows == i + 4, inner[:, cols], packed)
        sums_ref[...] = jnp.broadcast_to(packed[None], sums_ref.shape)


def token_columns(table):
    def column(first):
        return jnp.concatenate([as_column(table[i : i + 1]) for i in range(first, first + 4)], axis=0)

    return column(0), column(4)


def grad_kernel(
    core_ref, sums_ref, within_ref, q_ref, attn_ref, gate_ref, up_ref,
    grad_ref, theirs_ref, mine_ref, table_ref,
):
    step = pl.program_id(0)
    tokens = q_ref.shape[0]
    group = q_ref.shape[1] // HEAD
    first = (core_ref[0] ^ (1 - step)) * group

    @pl.when(step == 0)
    def _():
        total = jnp.sum(sums_ref[...], axis=0) / (HEAD_COUNT * HEAD)
        scale = lax.rsqrt(total[0:4] + 1e-06)
        table_ref[0:4] = scale
        table_ref[4:8] = scale * total[4:8]

    scale, center = token_columns(table_ref[...])

    def part(out_ref):
        for i in range(group):
            cols = slice(i * HEAD, (i + 1) * HEAD)
            dnorm = up_ref[:, cols].astype(F32) * sigmoid(gate_ref[:, cols].astype(F32))
            normed = attn_ref[:, cols] * scale
            grad = (scale * (dnorm - normed * center)).astype(BF16)
            grad_ref[:, cols] = grad
            within = within_ref[pl.ds(first + i, 1), :]
            grown = q_ref[:, cols].astype(F32) * as_column(jnp.exp(within))
            put_state(out_ref, i, outer_state(grown, grad), jnp.exp(within[:, tokens - 1 :]))

    @pl.when(step == 0)
    def _():
        part(theirs_ref)

    @pl.when(step == 1)
    def _():
        part(mine_ref)


def gate_kernel(table_ref, attn_ref, gate_ref, up_ref, output_ref, gate_grad_ref):
    scale, _ = token_columns(table_ref[...])
    for i in range(attn_ref.shape[1] // HEAD):
        cols = slice(i * HEAD, (i + 1) * HEAD)
        normed = attn_ref[:, cols] * scale
        sig = sigmoid(gate_ref[:, cols].astype(F32))
        output_ref[:, cols] = (normed * sig).astype(BF16)
        gate_grad_ref[:, cols] = (
            up_ref[:, cols].astype(F32) * normed * sig * (1.0 - sig)
        ).astype(BF16)


def back_kernel(
    within_ref, q_ref, k_ref, v_ref, grad_ref, probs_ref, state_ref,
    query_grad_ref, key_ref, value_ref,
):
    within = within_ref[pl.ds(pl.program_id(0), 1), :]
    column = as_column(within)
    grow = jnp.exp(column)
    tokens = q_ref.shape[0]
    size = tokens // 2
    state = jnp.concatenate(halves(state_ref[0]), axis=0)
    for start in (0, size):
        width = start + size
        grad = grad_ref[start:width, :]
        pgrad = dot(grad, v_ref[0:width, :], NT)
        pgrad = (pgrad * decay_block(within, column, start, size, width)).astype(BF16)
        inter = dot(jnp.concatenate([grad, grad], axis=1), state, NN)
        query_grad_ref[start:width, :] = (
            dot(pgrad, k_ref[0:width, :], NN) + grow[start:width] * inter
        ).astype(BF16)
        key_part = dot(pgrad, q_ref[start:width, :], TN)
        value_part = dot(probs_ref[0, start:width, 0:width], grad, TN)
        if start == 0:
            key_ref[0:width, :] = key_part
            value_ref[0:width, :] = value_part
        else:
            key_ref[0:start, :] += key_part[0:start]
            value_ref[0:start, :] += value_part[0:start]
            key_ref[start:width, :] = key_part[start:width]
            value_ref[start:width, :] = value_part[start:width]


def final_kernel(
    core_ref, within_ref, k_ref, v_ref, key_part_ref, value_part_ref,
    chip_mine_ref, chip_other_ref, lead_mine_ref, lead_other_ref,
    key_grad_ref, value_grad_ref,
):
    step = pl.program_id(0)
    group = chip_mine_ref.shape[0]
    tokens = k_ref.shape[0]
    first = (core_ref[0] ^ step) * group

    def part(chip_ref, lead_ref):
        for i in range(group):
            cols = slice(i * HEAD, (i + 1) * HEAD)
            state = halves(pick_state(core_ref[0] == 0, chip_ref, lead_ref, i))
            within = within_ref[pl.ds(first + i, 1), :]
            tail = as_column(jnp.exp(within[:, tokens - 1 :] - within))
            k, v = k_ref[:, cols], v_ref[:, cols]
            key_inter = dot(
                jnp.concatenate([v, v], axis=1), jnp.concatenate(state, axis=0), NN
            )
            value_inter = dot(
                jnp.concatenate([k, k], axis=1), jnp.concatenate(state, axis=1), NT
            )
            key_grad_ref[:, cols] = (key_part_ref[:, cols] + tail * key_inter).astype(BF16)
            value_grad_ref[:, cols] = (
                value_part_ref[:, cols] + tail * value_inter
            ).astype(BF16)

    @pl.when(step == 0)
    def _():
        part(chip_mine_ref, lead_mine_ref)

    @pl.when(step == 1)
    def _():
        part(chip_other_ref, lead_other_ref)


def shape(dims, dtype=F32):
    return jax.ShapeDtypeStruct(dims, dtype)


def whole(dims):
    return pl.BlockSpec(dims, lambda *_: (0,) * len(dims))


def swap(x):
    return lax.ppermute(x, "c", [(0, 1), (1, 0)])


def spread(x):
    return lax.all_to_all(x, CHIPS, split_axis=0, concat_axis=0, tiled=True)


def shards(queries, keys, values, gate, log_decay, out_grad):
    tokens, flat = queries.shape
    heads = log_decay.shape[1]
    group = heads // 2
    half = group * HEAD
    chips = lax.axis_size("x") * lax.axis_size("y")
    rows = group * HEAD // chips
    core = lax.axis_index("c").astype(jnp.int32).reshape(1)
    packed = (group, HEAD + PAD, HEAD)
    states = (group, HEAD, HEAD)

    other_first = pl.BlockSpec((tokens, half), lambda s, c: (0, c[0] ^ (1 - s)))
    mine_first = pl.BlockSpec((tokens, half), lambda s, c: (0, c[0] ^ s))
    by_head = pl.BlockSpec((tokens, HEAD), lambda h: (0, h))

    def grid_of(inputs, outputs, scratch=()):
        return pltpu.PrefetchScalarGridSpec(
            num_scalar_prefetch=1,
            grid=(2,),
            in_specs=inputs,
            out_specs=outputs,
            scratch_shapes=list(scratch),
        )

    def combined(lead, mine, other):
        return pl.pallas_call(
            combine_kernel,
            grid_spec=pltpu.PrefetchScalarGridSpec(
                num_scalar_prefetch=1,
                grid=(1,),
                in_specs=[whole(packed)] * 2,
                out_specs=whole((chips, rows + PAD, HEAD)),
            ),
            out_shape=shape((chips, rows + PAD, HEAD)),
            compiler_params=params(),
            name="combine",
        )(lead, mine, other)

    def scanned(x, reverse):
        return pl.pallas_call(
            lambda i, o: scan_kernel(reverse, i, o),
            out_shape=shape((chips, rows, HEAD)),
            name="scan",
        )(x)

    within, theirs, mine = pl.pallas_call(
        local_kernel,
        grid_spec=grid_of(
            [whole((tokens, heads)), other_first, other_first],
            [whole((heads, tokens)), whole(packed), whole(packed)],
        ),
        out_shape=[shape((heads, tokens)), shape(packed), shape(packed)],
        compiler_params=params(),
        name="local",
    )(core, log_decay, keys, values)
    lead_mine = swap(theirs)
    chip_state = spread(combined(1 - core, mine, lead_mine))
    lead_other = swap(mine)
    probs, intra = pl.pallas_call(
        inside_kernel,
        grid=(heads,),
        in_specs=[whole((heads, tokens)), by_head, by_head, by_head],
        out_specs=[pl.BlockSpec((1, tokens, tokens), lambda h: (h, 0, 0)), by_head],
        out_shape=[shape((heads, tokens, tokens), BF16), shape((tokens, flat))],
        compiler_params=params(),
        name="inside",
    )(within, queries, keys, values)
    chip_mine = spread(scanned(chip_state, False)).reshape(states)
    chip_other = swap(chip_mine)
    attn, state, sums = pl.pallas_call(
        attn_kernel,
        grid_spec=grid_of(
            [whole((heads, tokens))] + [mine_first] * 4 + [whole(states)] * 2 + [whole(packed)] * 2,
            [
                mine_first,
                pl.BlockSpec(states, lambda s, c: (c[0] ^ s, 0, 0)),
                whole((8, 8, HEAD)),
            ],
            [pltpu.VMEM((tokens, HEAD), F32)] * 2,
        ),
        out_shape=[shape((tokens, flat)), shape((heads, HEAD, HEAD)), shape((8, 8, HEAD))],
        compiler_params=params(),
        name="attn",
    )(core, within, queries, intra, gate, out_grad, chip_mine, chip_other, lead_mine, lead_other)
    sums = lax.all_to_all(sums, "tp", split_axis=0, concat_axis=0, tiled=True)
    grad, theirs, mine, table = pl.pallas_call(
        grad_kernel,
        grid_spec=grid_of(
            [whole((8, 8, HEAD)), whole((heads, tokens))] + [other_first] * 4,
            [other_first, whole(packed), whole(packed), whole((8, HEAD))],
        ),
        out_shape=[shape((tokens, flat), BF16), shape(packed), shape(packed), shape((8, HEAD))],
        compiler_params=params(),
        name="grad",
    )(core, sums, within, queries, attn, gate, out_grad)
    lead_mine = swap(theirs)
    chip_state = spread(combined(core, mine, lead_mine))
    lead_other = swap(mine)
    query_grad, key_part, value_part = pl.pallas_call(
        back_kernel,
        grid=(heads,),
        in_specs=[whole((heads, tokens))]
        + [by_head] * 4
        + [
            pl.BlockSpec((1, tokens, tokens), lambda h: (h, 0, 0)),
            pl.BlockSpec((1, HEAD, HEAD), lambda h: (h, 0, 0)),
        ],
        out_specs=[by_head] * 3,
        out_shape=[shape((tokens, flat), BF16), shape((tokens, flat)), shape((tokens, flat))],
        compiler_params=params(),
        name="back",
    )(within, queries, keys, values, grad, probs, state)
    by_half = pl.BlockSpec((tokens, half), lambda s: (0, s))
    output, gate_grad = pl.pallas_call(
        gate_kernel,
        grid=(2,),
        in_specs=[whole((8, HEAD))] + [by_half] * 3,
        out_specs=[by_half] * 2,
        out_shape=[shape((tokens, flat), BF16)] * 2,
        compiler_params=params(),
        name="gate",
    )(table, attn, gate, out_grad)
    chip_mine = spread(scanned(chip_state, True)).reshape(states)
    chip_other = swap(chip_mine)
    key_grad, value_grad = pl.pallas_call(
        final_kernel,
        grid_spec=grid_of(
            [whole((heads, tokens))] + [mine_first] * 4 + [whole(states)] * 2 + [whole(packed)] * 2,
            [mine_first] * 2,
        ),
        out_shape=[shape((tokens, flat), BF16)] * 2,
        compiler_params=params(),
        name="final",
    )(core, within, keys, values, key_part, value_part, chip_mine, chip_other, lead_mine, lead_other)
    return output, query_grad, key_grad, value_grad, gate_grad


def solution(mesh):
    split = Mesh(mesh.devices.reshape(4, 4, 2, mesh.shape["tp"]), ("x", "y", "c", "tp"))
    return jax.shard_map(
        shards,
        mesh=split,
        in_specs=(P(SEQ, "tp"),) * 6,
        out_specs=(P(SEQ, "tp"),) * 5,
        check_vma=False,
    )
```

```python
import jax
import jax.numpy as jnp
from jax import lax
from jax.experimental import pallas as pl
from jax.experimental.pallas import tpu as pltpu
from jax.sharding import Mesh
from jax.sharding import PartitionSpec as P

HEAD_COUNT = 64
HEAD = 128
SEQ = ("x", "y", "c")
CHIPS = ("x", "y")
HIGH = lax.Precision.HIGHEST
F32 = jnp.float32
BF16 = jnp.bfloat16
PAD = 8

NN = (((1,), (0,)), ((), ()))
NT = (((1,), (1,)), ((), ()))
TN = (((0,), (0,)), ((), ()))


def dot(a, b, dims, precision=None):
    return lax.dot_general(a, b, dims, precision=precision, preferred_element_type=F32)


def halves(x):
    high = x.astype(BF16)
    return high, (x - high.astype(F32)).astype(BF16)


def as_column(row):
    return jnp.transpose(jnp.broadcast_to(row, (HEAD, row.shape[1])))


def sigmoid(x):
    return 1.0 / (1.0 + jnp.exp(-x))


def lanes(head, count=1):
    return pl.ds(pl.multiple_of(head * (count * HEAD), HEAD), count * HEAD)


def put_state(ref, i, state, factor):
    ref[i, 0:HEAD, :] = state
    ref[i, HEAD : HEAD + PAD, :] = jnp.broadcast_to(factor, (PAD, HEAD))


def outer_state(wide, narrow):
    both = dot(narrow, wide, TN)
    return both[:, :HEAD] + both[:, HEAD:]


def sum_kernel(rate_ref, within_ref):
    heads, tokens = rate_ref.shape
    early = lax.broadcasted_iota(jnp.int32, (tokens, tokens), 0)
    late = lax.broadcasted_iota(jnp.int32, (tokens, tokens), 1)
    upto = (early <= late).astype(F32).astype(BF16)
    rate = rate_ref[...]
    high, rest = halves(rate)
    low = (rate - high.astype(F32) - rest.astype(F32)).astype(BF16)
    parts = jnp.concatenate([x.astype(F32) for x in (high, rest, low)], axis=0).astype(BF16)
    sums = dot(parts, upto, NN)
    within_ref[...] = sums[0:heads] + sums[heads : 2 * heads] + sums[2 * heads :]


def local_part(first, step, within_ref, k_ref, v_ref, out_ref):
    count = k_ref.shape[1] // HEAD
    tokens = k_ref.shape[0]
    for i in range(count):
        within = within_ref[pl.ds(first + step * count + i, 1), :]
        last = within[:, tokens - 1 :]
        tail = as_column(jnp.exp(last - within))
        cols = slice(i * HEAD, (i + 1) * HEAD)
        scaled = jnp.concatenate(halves(k_ref[:, cols].astype(F32) * tail), axis=1)
        put_state(out_ref, step * count + i, outer_state(scaled, v_ref[:, cols]), jnp.exp(last))


def local_other_kernel(core_ref, rate_ref, k_ref, v_ref, within_ref, out_ref):
    step = pl.program_id(0)

    @pl.when(step == 0)
    def _():
        sum_kernel(rate_ref, within_ref)

    first = (1 - core_ref[0]) * out_ref.shape[0]
    local_part(first, step, within_ref, k_ref, v_ref, out_ref)


def copy_pair(step, count, from_ref, to_ref):
    for i in range(count):
        to_ref[i] = from_ref[step * count + i]


def local_mine_kernel(core_ref, within_ref, k_ref, v_ref, out_ref, copy_ref):
    first = core_ref[0] * out_ref.shape[0]
    step = pl.program_id(0)
    local_part(first, step, within_ref, k_ref, v_ref, out_ref)
    copy_pair(step, copy_ref.shape[0], out_ref, copy_ref)


def combine_kernel(lead_ref, mine_ref, other_ref, out_ref, copy_ref):
    copy_ref[...] = other_ref[...]
    lead = lead_ref[0] == 1
    group = mine_ref.shape[0]
    rows = HEAD // 4
    for i in range(group):
        own = mine_ref[i, HEAD : HEAD + PAD, :]
        far = other_ref[i, HEAD : HEAD + PAD, :]
        mine = mine_ref[i, 0:HEAD, :]
        other = other_ref[i, 0:HEAD, :]
        both = jnp.where(lead, far[0:1] * mine + other, own[0:1] * other + mine)
        for j in range(4):
            out_ref[4 * i + j, 0:rows, :] = both[j * rows : (j + 1) * rows]
            out_ref[4 * i + j, rows : rows + PAD, :] = own * far


def scan_kernel(reverse, in_ref, out_ref):
    chips, rows = out_ref.shape[0], out_ref.shape[1]
    state = jnp.zeros(out_ref.shape[1:], F32)
    for n in reversed(range(chips)) if reverse else range(chips):
        out_ref[n] = state
        state = in_ref[n, rows : rows + 1, :] * state + in_ref[n, 0:rows, :]


def decay_block(within, column, start, size, width):
    gap = jnp.concatenate([column[start : start + size]] * (width // HEAD), axis=1)
    gap = gap - within[:, :width]
    rows = start + lax.broadcasted_iota(jnp.int32, gap.shape, 0)
    cols = lax.broadcasted_iota(jnp.int32, gap.shape, 1)
    return jnp.where(rows >= cols, jnp.exp(jnp.minimum(gap, 0.0)), 0.0)


def inside_kernel(within_ref, q_ref, k_ref, v_ref, probs_ref, intra_ref):
    head = pl.program_id(0)
    within = within_ref[pl.ds(head, 1), :]
    column = as_column(within)
    tokens = q_ref.shape[0]
    size = tokens // 2
    for start in (0, size):
        width = start + size
        scores = dot(q_ref[start:width, :], k_ref[0:width, :], NT)
        probs = (scores * decay_block(within, column, start, size, width)).astype(BF16)
        probs_ref[0, start:width, 0:width] = probs
        intra_ref[start:width, :] = dot(probs, v_ref[0:width, :], NN)


def pick_state(follows, chip_ref, lead_ref, i):
    chip = chip_ref[i]
    return jnp.where(
        follows, lead_ref[i, HEAD : HEAD + 1, :] * chip + lead_ref[i, 0:HEAD, :], chip
    )


def attn_part(core_ref, head, own, at, within_ref, q_ref, gate_ref, up_ref, intra_ref, chip_ref, lead_ref, outs):
    attn_ref, dnorm_ref, grown_ref, state_ref = outs
    state = pick_state(core_ref[0] == 1, chip_ref, lead_ref, own)
    state_ref[head] = state
    high, low = halves(state)
    grown = q_ref[:, at].astype(F32) * as_column(jnp.exp(within_ref[pl.ds(head, 1), :]))
    grown = jnp.concatenate(halves(grown), axis=1)
    grown_ref[:, lanes(head, 2)] = grown
    attn = intra_ref[:, at] + dot(
        jnp.concatenate([grown, grown[:, :HEAD]], axis=1),
        jnp.concatenate([high, high, low], axis=1),
        NT,
    )
    attn_ref[:, lanes(head)] = attn
    dnorm = up_ref[:, at].astype(F32) * sigmoid(gate_ref[:, at].astype(F32))
    dnorm_ref[:, lanes(head)] = dnorm
    return attn * attn, dnorm * attn


def fetches(core_ref, sources, targets, sems):
    half = targets[0].shape[1]
    cols = pl.ds(pl.multiple_of((1 - core_ref[0]) * half, HEAD), half)
    return [
        pltpu.make_async_copy(source.at[:, cols], target, sems.at[i])
        for i, (source, target) in enumerate(zip(sources, targets))
    ]


def attn_mine_kernel(
    core_ref, within_ref, q_ref, gate_ref, up_ref, intra_ref, chip_ref, lead_ref,
    q_hbm, gate_hbm, up_hbm, intra_hbm,
    attn_ref, dnorm_ref, grown_ref, state_ref, square_ref, inner_ref,
    q_far, gate_far, up_far, intra_far, sems,
):
    step = pl.program_id(0)
    count = q_ref.shape[1] // HEAD
    copies = fetches(
        core_ref, (q_hbm, gate_hbm, up_hbm, intra_hbm), (q_far, gate_far, up_far, intra_far), sems
    )

    @pl.when(step == 0)
    def _():
        for copy in copies:
            copy.start()
        square_ref[...] = jnp.zeros_like(square_ref)
        inner_ref[...] = jnp.zeros_like(inner_ref)

    for i in range(count):
        own = step * count + i
        square, inner = attn_part(
            core_ref, core_ref[0] * chip_ref.shape[0] + own, own, slice(i * HEAD, (i + 1) * HEAD),
            within_ref, q_ref, gate_ref, up_ref, intra_ref, chip_ref, lead_ref,
            (attn_ref, dnorm_ref, grown_ref, state_ref),
        )
        square_ref[...] += square
        inner_ref[...] += inner

    @pl.when(step == pl.num_programs(0) - 1)
    def _():
        for copy in copies:
            copy.wait()


def attn_other_kernel(
    core_ref, within_ref, q_ref, gate_ref, up_ref, intra_ref, chip_ref, lead_ref,
    square_ref, inner_ref, attn_in, dnorm_in, grown_in, state_in,
    attn_ref, dnorm_ref, grown_ref, state_ref, sums_ref,
):
    total_square, total_inner = square_ref[...], inner_ref[...]
    for i in range(chip_ref.shape[0]):
        square, inner = attn_part(
            core_ref, (1 - core_ref[0]) * chip_ref.shape[0] + i, i, slice(i * HEAD, (i + 1) * HEAD),
            within_ref, q_ref, gate_ref, up_ref, intra_ref, chip_ref, lead_ref,
            (attn_ref, dnorm_ref, grown_ref, state_ref),
        )
        total_square = total_square + square
        total_inner = total_inner + inner
    ones = jnp.ones((8, HEAD), F32)
    square = dot(ones, total_square, NT, HIGH)
    inner = dot(ones, total_inner, NT, HIGH)
    rows = lax.broadcasted_iota(jnp.int32, (8, HEAD), 0)
    packed = jnp.zeros((8, HEAD), F32)
    for i in range(4):
        cols = slice(i * HEAD, (i + 1) * HEAD)
        packed = jnp.where(rows == i, square[:, cols], packed)
        packed = jnp.where(rows == i + 4, inner[:, cols], packed)
    sums_ref[...] = jnp.broadcast_to(packed[None], sums_ref.shape)


def grad_part(half, grown_ref, attn_ref, dnorm_ref, within_ref, scale_ref, center_ref, grad_ref, out_ref):
    step = pl.program_id(0)
    tokens = attn_ref.shape[0]
    count = grad_ref.shape[1] // HEAD
    for i in range(count):
        own = step * count + i
        head = half * out_ref.shape[0] + own
        scale = scale_ref[...]
        normed = attn_ref[:, lanes(head)] * scale
        grad = (scale * (dnorm_ref[:, lanes(head)] - normed * center_ref[...])).astype(BF16)
        grad_ref[:, i * HEAD : (i + 1) * HEAD] = grad
        last = within_ref[pl.ds(head, 1), :][:, tokens - 1 :]
        put_state(out_ref, own, outer_state(grown_ref[:, lanes(head, 2)], grad), jnp.exp(last))


def grad_other_kernel(
    core_ref, sums_ref, within_ref, grown_ref, attn_ref, dnorm_ref,
    grad_ref, out_ref, scale_ref, center_ref, table_ref,
):
    @pl.when(pl.program_id(0) == 0)
    def _():
        total = jnp.sum(sums_ref[...], axis=0) / (HEAD_COUNT * HEAD)
        scale = lax.rsqrt(total[0:4] + 1e-06)
        center = scale * total[4:8]
        table_ref[0:4] = scale
        table_ref[4:8] = center
        for i in range(4):
            rows = slice(i * HEAD, (i + 1) * HEAD)
            scale_ref[rows] = as_column(scale[i : i + 1])
            center_ref[rows] = as_column(center[i : i + 1])

    grad_part(
        1 - core_ref[0], grown_ref, attn_ref, dnorm_ref, within_ref, scale_ref, center_ref,
        grad_ref, out_ref,
    )


def grad_mine_kernel(
    core_ref, scale_ref, center_ref, within_ref, grown_ref, attn_ref, dnorm_ref, grad_in_ref,
    grad_ref, out_ref, copy_ref,
):
    grad_part(
        core_ref[0], grown_ref, attn_ref, dnorm_ref, within_ref, scale_ref, center_ref,
        grad_ref, out_ref,
    )
    copy_pair(pl.program_id(0), copy_ref.shape[0], out_ref, copy_ref)


def gate_kernel(table_ref, attn_ref, gate_ref, up_ref, output_ref, gate_grad_ref):
    table = table_ref[...]
    scale = jnp.concatenate([as_column(table[i : i + 1]) for i in range(4)], axis=0)
    count = gate_ref.shape[1] // HEAD
    for i in range(count):
        cols = slice(i * HEAD, (i + 1) * HEAD)
        normed = attn_ref[:, cols] * scale
        sig = sigmoid(gate_ref[:, cols].astype(F32))
        output_ref[:, cols] = (normed * sig).astype(BF16)
        gate_grad_ref[:, cols] = (
            up_ref[:, cols].astype(F32) * normed * sig * (1.0 - sig)
        ).astype(BF16)


def back_kernel(within_ref, q_ref, k_ref, v_ref, grad_ref, state_ref, query_grad_ref, key_ref):
    head = pl.program_id(0)
    within = within_ref[pl.ds(head, 1), :]
    column = as_column(within)
    grow = jnp.exp(column)
    tokens = q_ref.shape[0]
    size = tokens // 2
    state = jnp.concatenate(halves(state_ref[0]), axis=0)
    for start in (0, size):
        width = start + size
        grad = grad_ref[start:width, :]
        pgrad = dot(grad, v_ref[0:width, :], NT)
        pgrad = (pgrad * decay_block(within, column, start, size, width)).astype(BF16)
        inter = dot(jnp.concatenate([grad, grad], axis=1), state, NN)
        query_grad_ref[start:width, :] = (
            dot(pgrad, k_ref[0:width, :], NN) + grow[start:width] * inter
        ).astype(BF16)
        key_part = dot(pgrad, q_ref[start:width, :], TN)
        if start == 0:
            key_ref[0:width, :] = key_part
        else:
            key_ref[0:start, :] += key_part[0:start]
            key_ref[start:width, :] = key_part[start:width]


def value_kernel(grad_ref, probs_ref, value_ref):
    tokens = grad_ref.shape[0]
    size = tokens // 2
    late = dot(probs_ref[0, size:tokens, :], grad_ref[size:tokens, :], TN)
    early = dot(probs_ref[0, 0:size, 0:size], grad_ref[0:size, :], TN)
    value_ref[0:size, :] = late[0:size] + early
    value_ref[size:tokens, :] = late[size:tokens]


def final_part(
    core_ref, head, own, at, within_ref, k_ref, v_ref, key_part_ref, value_part_ref,
    chip_ref, lead_ref, key_grad_ref, value_grad_ref, to,
):
    tokens = k_ref.shape[0]
    state = halves(pick_state(core_ref[0] == 0, chip_ref, lead_ref, own))
    within = within_ref[pl.ds(head, 1), :]
    tail = as_column(jnp.exp(within[:, tokens - 1 :] - within))
    k, v = k_ref[:, at], v_ref[:, at]
    key_inter = dot(jnp.concatenate([v, v], axis=1), jnp.concatenate(state, axis=0), NN)
    value_inter = dot(jnp.concatenate([k, k], axis=1), jnp.concatenate(state, axis=1), NT)
    key_grad_ref[:, to] = (key_part_ref[:, at] + tail * key_inter).astype(BF16)
    value_grad_ref[:, to] = (value_part_ref[:, at] + tail * value_inter).astype(BF16)


def final_mine_kernel(
    core_ref, within_ref, k_ref, v_ref, key_part_ref, value_part_ref, chip_ref, lead_ref,
    k_hbm, v_hbm, key_part_hbm, value_part_hbm,
    key_grad_ref, value_grad_ref, k_far, v_far, key_part_far, value_part_far, sems,
):
    step = pl.program_id(0)
    count = k_ref.shape[1] // HEAD
    copies = fetches(
        core_ref, (k_hbm, v_hbm, key_part_hbm, value_part_hbm),
        (k_far, v_far, key_part_far, value_part_far), sems,
    )

    @pl.when(step == 0)
    def _():
        for copy in copies:
            copy.start()

    for i in range(count):
        own = step * count + i
        cols = slice(i * HEAD, (i + 1) * HEAD)
        final_part(
            core_ref, core_ref[0] * chip_ref.shape[0] + own, own, cols, within_ref, k_ref, v_ref,
            key_part_ref, value_part_ref, chip_ref, lead_ref, key_grad_ref, value_grad_ref, cols,
        )

    @pl.when(step == pl.num_programs(0) - 1)
    def _():
        for copy in copies:
            copy.wait()


def final_other_kernel(
    core_ref, within_ref, k_ref, v_ref, key_part_ref, value_part_ref, chip_ref, lead_ref,
    key_grad_in, value_grad_in, key_grad_ref, value_grad_ref,
):
    step = pl.program_id(0)
    count = key_grad_ref.shape[1] // HEAD
    for i in range(count):
        own = step * count + i
        final_part(
            core_ref, (1 - core_ref[0]) * chip_ref.shape[0] + own, own, lanes(own), within_ref,
            k_ref, v_ref, key_part_ref, value_part_ref, chip_ref, lead_ref,
            key_grad_ref, value_grad_ref, slice(i * HEAD, (i + 1) * HEAD),
        )


def shape(dims, dtype=F32):
    return jax.ShapeDtypeStruct(dims, dtype)


def swap(x):
    return lax.ppermute(x, "c", [(0, 1), (1, 0)])


def spread(x):
    return lax.all_to_all(x, CHIPS, split_axis=0, concat_axis=0, tiled=True)


VMEM = pl.BlockSpec(memory_space=pltpu.VMEM)
HBM = pl.BlockSpec(memory_space=pl.ANY)


def call(kernel, name, grid, inputs, outputs, core=None, aliases=(), scratch=(), mib=12):
    def place(x, spec):
        return x if spec is VMEM else pltpu.with_memory_space_constraint(x, pltpu.HBM)

    scalars = () if core is None else (core,)
    return pl.pallas_call(
        kernel,
        grid_spec=pltpu.PrefetchScalarGridSpec(
            num_scalar_prefetch=len(scalars),
            grid=grid,
            in_specs=[spec for _, spec in inputs],
            out_specs=[spec for _, spec in outputs],
            scratch_shapes=list(scratch),
        ),
        out_shape=[
            (pltpu.VMEM if spec is VMEM else pltpu.HBM)(x.shape, x.dtype) for x, spec in outputs
        ],
        input_output_aliases=dict(aliases),
        compiler_params=pltpu.CompilerParams(
            dimension_semantics=("arbitrary",) * len(grid), vmem_limit_bytes=mib * 2**20
        ),
        name=name,
    )(*scalars, *(place(x, spec) for x, spec in inputs))


def shards(queries, keys, values, gate, log_decay, out_grad):
    tokens, flat = queries.shape
    heads = log_decay.shape[1]
    group = heads // 2
    chips = lax.axis_size("x") * lax.axis_size("y")
    rows = group * HEAD // chips
    core = lax.axis_index("c").astype(jnp.int32).reshape(1)
    packed = shape((group, HEAD + PAD, HEAD))
    states = shape((group, HEAD, HEAD))
    sliced = shape((chips, rows, HEAD))
    wide = shape((tokens, flat))
    narrow = shape((tokens, flat), BF16)
    column = shape((tokens, HEAD))

    half = shape((tokens, flat // 2))
    half_narrow = shape((tokens, flat // 2), BF16)
    full = shape((heads, HEAD, HEAD))

    by_head = pl.BlockSpec((tokens, HEAD), lambda h: (0, h))
    by_pair = pl.BlockSpec((tokens, 2 * HEAD), lambda s: (0, s))
    state_by_head = pl.BlockSpec((1, HEAD, HEAD), lambda h: (h, 0, 0))
    probs_by_head = pl.BlockSpec((1, tokens, tokens), lambda h: (h, 0, 0))
    pairs = group // 2
    mine_pair = pl.BlockSpec((tokens, 2 * HEAD), lambda s, c: (0, c[0] * pairs + s))
    other_pair = pl.BlockSpec((tokens, 2 * HEAD), lambda s, c: (0, (1 - c[0]) * pairs + s))
    packed_pair = pl.BlockSpec((2, HEAD + PAD, HEAD), lambda s, c: (s, 0, 0))

    def in_vmem(*xs):
        return [(x, VMEM) for x in xs]

    def in_hbm(*xs):
        return [(x, pl.BlockSpec(x.shape, lambda *_: (0,) * len(x.shape))) for x in xs]

    def combined(lead, mine, other):
        return call(
            combine_kernel, "combine", (1,), in_vmem(mine, other),
            in_hbm(shape((chips, rows + PAD, HEAD)), packed), lead,
        )

    def scanned(x, reverse):
        return call(
            lambda i, o: scan_kernel(reverse, i, o), "scan", (1,), in_vmem(x), in_hbm(sliced)
        )[0]

    within, theirs = call(
        local_other_kernel, "local_other", (pairs,),
        [(log_decay.T, VMEM), (keys, other_pair), (values, other_pair)],
        in_vmem(shape((heads, tokens)), packed), core,
    )
    lead_mine = swap(theirs)
    mine, mine_copy = call(
        local_mine_kernel, "local_mine", (pairs,),
        [(within, VMEM), (keys, mine_pair), (values, mine_pair)],
        in_vmem(packed) + [(packed, packed_pair)], core,
    )
    chip_state, lead_mine = combined(1 - core, mine, lead_mine)
    chip_state = spread(chip_state)
    probs, intra = call(
        inside_kernel, "inside", (heads,),
        in_hbm(within) + [(queries, by_head), (keys, by_head), (values, by_head)],
        [(shape((heads, tokens, tokens), BF16), probs_by_head), (wide, by_head)],
    )
    chip_state, probs, intra, mine_copy = lax.optimization_barrier(
        (chip_state, probs, intra, mine_copy)
    )
    chip_mine = spread(scanned(chip_state, False))
    lead_other = swap(mine_copy)
    chip_mine, lead_other, intra, within = lax.optimization_barrier(
        (chip_mine, lead_other, intra, within)
    )
    chip_mine = chip_mine.reshape(states.shape)
    chip_other = swap(chip_mine)
    attn, dnorm, grown, state, square, inner, *far = call(
        attn_mine_kernel, "attn_mine", (pairs,),
        in_hbm(within)
        + [(queries, mine_pair), (gate, mine_pair), (out_grad, mine_pair), (intra, mine_pair)]
        + in_vmem(chip_mine) + in_hbm(lead_mine)
        + [(queries, HBM), (gate, HBM), (out_grad, HBM), (intra, HBM)],
        in_vmem(
            wide, wide, shape((tokens, 2 * flat), BF16), full, column, column,
            half_narrow, half_narrow, half_narrow, half,
        ),
        core, scratch=[pltpu.SemaphoreType.DMA((4,))],
    )
    attn, dnorm, grown, state, sums = call(
        attn_other_kernel, "attn_other", (1,),
        in_hbm(within) + in_vmem(*far, chip_other, lead_other)
        + in_vmem(square, inner, attn, dnorm, grown, state),
        in_vmem(wide, wide, shape((tokens, 2 * flat), BF16), full, shape((8, 8, HEAD))),
        core, {10: 0, 11: 1, 12: 2, 13: 3},
    )
    sums = lax.all_to_all(sums, "tp", split_axis=0, concat_axis=0, tiled=True)
    grad, theirs, scale, center, table = call(
        grad_other_kernel, "grad_other", (pairs,),
        in_vmem(sums) + in_hbm(within) + in_vmem(grown, attn, dnorm),
        [(narrow, other_pair)] + in_vmem(packed, column, column) + in_hbm(shape((8, HEAD))), core,
    )
    lead_mine = swap(theirs)
    grad, mine, mine_copy = call(
        grad_mine_kernel, "grad_mine", (pairs,),
        in_vmem(scale, center) + in_hbm(within) + in_vmem(grown, attn, dnorm) + [(grad, HBM)],
        [(narrow, mine_pair)] + in_vmem(packed) + [(packed, packed_pair)], core, {7: 0},
    )
    chip_state, lead_mine = combined(core, mine, lead_mine)
    chip_state = spread(chip_state)
    query_grad, key_part = call(
        back_kernel, "back", (heads,),
        in_hbm(within)
        + [(queries, by_head), (keys, by_head), (values, by_head), (grad, by_head), (state, state_by_head)],
        [(narrow, by_head), (wide, by_head)],
    )
    chip_state, key_part, mine_copy, grad, table = lax.optimization_barrier(
        (chip_state, key_part, mine_copy, grad, table)
    )
    chip_mine = spread(scanned(chip_state, True))
    lead_other = swap(mine_copy)
    (value_part,) = call(
        value_kernel, "value", (heads,), [(grad, by_head), (probs, probs_by_head)],
        [(wide, by_head)],
    )
    output, gate_grad = call(
        gate_kernel, "gate", (heads // 2,),
        in_hbm(table) + [(attn, by_pair), (gate, by_pair), (out_grad, by_pair)],
        [(narrow, by_pair)] * 2,
    )
    chip_mine, value_part, output, gate_grad, lead_other = lax.optimization_barrier(
        (chip_mine, value_part, output, gate_grad, lead_other)
    )
    chip_mine = chip_mine.reshape(states.shape)
    chip_other = swap(chip_mine)
    key_grad, value_grad, *far = call(
        final_mine_kernel, "final_mine", (pairs,),
        in_hbm(within)
        + [(keys, mine_pair), (values, mine_pair), (key_part, mine_pair), (value_part, mine_pair)]
        + in_vmem(chip_mine) + in_hbm(lead_mine)
        + [(keys, HBM), (values, HBM), (key_part, HBM), (value_part, HBM)],
        [(narrow, mine_pair)] * 2 + in_vmem(half_narrow, half_narrow, half, half),
        core, scratch=[pltpu.SemaphoreType.DMA((4,))],
    )
    key_grad, value_grad = call(
        final_other_kernel, "final_other", (pairs,),
        in_hbm(within) + in_vmem(*far, chip_other, lead_other)
        + [(key_grad, HBM), (value_grad, HBM)],
        [(narrow, other_pair)] * 2, core, {8: 0, 9: 1},
    )
    return output, query_grad, key_grad, value_grad, gate_grad


def solution(mesh):
    split = Mesh(mesh.devices.reshape(4, 4, 2, mesh.shape["tp"]), ("x", "y", "c", "tp"))
    return jax.shard_map(
        shards,
        mesh=split,
        in_specs=(P(SEQ, "tp"),) * 6,
        out_specs=(P(SEQ, "tp"),) * 5,
        check_vma=False,
    )
```

```python
import jax
import jax.numpy as jnp
from jax import lax
from jax.experimental import pallas as pl
from jax.experimental.pallas import tpu as pltpu
from jax.sharding import Mesh
from jax.sharding import PartitionSpec as P

HEAD_COUNT = 64
HEAD = 128
SEQ = ("x", "y", "c")
CHIPS = ("x", "y")
HIGH = lax.Precision.HIGHEST
F32 = jnp.float32
BF16 = jnp.bfloat16
PAD = 8

NN = (((1,), (0,)), ((), ()))
NT = (((1,), (1,)), ((), ()))
TN = (((0,), (0,)), ((), ()))


def dot(a, b, dims, precision=None):
    return lax.dot_general(a, b, dims, precision=precision, preferred_element_type=F32)


def halves(x):
    high = x.astype(BF16)
    return high, (x - high.astype(F32)).astype(BF16)


def as_column(row):
    return jnp.transpose(jnp.broadcast_to(row, (HEAD, row.shape[1])))


def sigmoid(x):
    return 1.0 / (1.0 + jnp.exp(-x))


def lanes(head, count=1):
    return pl.ds(pl.multiple_of(head * (count * HEAD), HEAD), count * HEAD)


def put_state(ref, i, state, factor):
    ref[i, 0:HEAD, :] = state
    ref[i, HEAD : HEAD + PAD, :] = jnp.broadcast_to(factor, (PAD, HEAD))


def outer_state(wide, narrow):
    both = dot(narrow, wide, TN)
    return both[:, :HEAD] + both[:, HEAD:]


def sum_kernel(rate_ref, within_ref):
    heads, tokens = rate_ref.shape
    early = lax.broadcasted_iota(jnp.int32, (tokens, tokens), 0)
    late = lax.broadcasted_iota(jnp.int32, (tokens, tokens), 1)
    upto = (early <= late).astype(F32).astype(BF16)
    rate = rate_ref[...]
    high, rest = halves(rate)
    low = (rate - high.astype(F32) - rest.astype(F32)).astype(BF16)
    parts = jnp.concatenate([x.astype(F32) for x in (high, rest, low)], axis=0).astype(BF16)
    sums = dot(parts, upto, NN)
    within_ref[...] = sums[0:heads] + sums[heads : 2 * heads] + sums[2 * heads :]


def half_of(half, group, count=1):
    width = group * count * HEAD
    return pl.ds(pl.multiple_of(half * width, HEAD), width)


def copies(pairs, sems):
    return [pltpu.make_async_copy(a, b, sems.at[i]) for i, (a, b) in enumerate(pairs)]


def start(group):
    for copy in group:
        copy.start()


def wait(group):
    for copy in group:
        copy.wait()


def each_head(heads, body):
    def step(head, carry):
        body(head)
        return carry

    lax.fori_loop(0, heads, step, 0)


def head_copies(arrays, sems, head):
    made = []
    for i, (a, b, count) in enumerate(arrays):
        at = (head,) if count == 0 else (slice(None), lanes(head, count))
        made.append(pltpu.make_async_copy(a.at[at], b.at[at], sems.at[i, head]))
    return made


def local_state(head, cols, within_ref, k_ref, v_ref, out_ref, i):
    tokens = k_ref.shape[0]
    within = within_ref[pl.ds(head, 1), :]
    last = within[:, tokens - 1 :]
    tail = as_column(jnp.exp(last - within))
    scaled = jnp.concatenate(halves(k_ref[:, cols].astype(F32) * tail), axis=1)
    put_state(out_ref, i, outer_state(scaled, v_ref[:, cols]), jnp.exp(last))


def local_other_kernel(
    core_ref, rate_hbm, k_hbm, v_hbm, within_ref, out_ref, k_near, v_near, rate_ref, k_ref, v_ref, sems
):
    group = out_ref.shape[0]
    core = core_ref[0]
    far, near = half_of(1 - core, group), half_of(core, group)
    made = copies(
        [
            (rate_hbm, rate_ref),
            (v_hbm.at[:, far], v_ref),
            (k_hbm.at[:, far], k_ref),
            (v_hbm.at[:, near], v_near),
            (k_hbm.at[:, near], k_near),
        ],
        sems,
    )
    start(made)
    made[0].wait()
    sum_kernel(rate_ref, within_ref)
    wait(made[1:3])
    for i in range(group):
        cols = slice(i * HEAD, (i + 1) * HEAD)
        local_state((1 - core) * group + i, cols, within_ref, k_ref, v_ref, out_ref, i)
    wait(made[3:])


def local_mine_kernel(core_ref, within_ref, k_ref, v_ref, out_ref):
    group = out_ref.shape[0]
    for i in range(group):
        cols = slice(i * HEAD, (i + 1) * HEAD)
        local_state(core_ref[0] * group + i, cols, within_ref, k_ref, v_ref, out_ref, i)


def combine_kernel(
    lead_ref, mine_ref, other_ref, out_hbm, mine_hbm, other_hbm, out_ref, sems
):
    made = copies([(mine_ref, mine_hbm), (other_ref, other_hbm), (out_ref, out_hbm)], sems)
    start(made[:2])
    lead = lead_ref[0] == 1
    group = mine_ref.shape[0]
    rows = HEAD // 4
    for i in range(group):
        own = mine_ref[i, HEAD : HEAD + PAD, :]
        far = other_ref[i, HEAD : HEAD + PAD, :]
        mine = mine_ref[i, 0:HEAD, :]
        other = other_ref[i, 0:HEAD, :]
        both = jnp.where(lead, far[0:1] * mine + other, own[0:1] * other + mine)
        for j in range(4):
            out_ref[4 * i + j, 0:rows, :] = both[j * rows : (j + 1) * rows]
            out_ref[4 * i + j, rows : rows + PAD, :] = own * far
    made[2].start()
    wait(made)


def scan_kernel(reverse, in_ref, out_hbm, out_ref, sems):
    chips, rows = out_ref.shape[0], out_ref.shape[1]
    state = jnp.zeros(out_ref.shape[1:], F32)
    made = []
    for n in reversed(range(chips)) if reverse else range(chips):
        out_ref[n] = state
        state = in_ref[n, rows : rows + 1, :] * state + in_ref[n, 0:rows, :]
    made = copies([(out_ref, out_hbm)], sems)
    start(made)
    wait(made)


def decay_block(within, column, first, size, width):
    gap = jnp.concatenate([column[first : first + size]] * (width // HEAD), axis=1)
    gap = gap - within[:, :width]
    rows = first + lax.broadcasted_iota(jnp.int32, gap.shape, 0)
    cols = lax.broadcasted_iota(jnp.int32, gap.shape, 1)
    return jnp.where(rows >= cols, jnp.exp(jnp.minimum(gap, 0.0)), 0.0)


def inside_kernel(
    within_hbm, q_hbm, k_hbm, v_hbm, probs_hbm, intra_hbm,
    within_ref, q_ref, k_ref, v_ref, probs_ref, intra_ref, sem, in_sems, out_sems,
):
    heads = within_ref.shape[0]
    tokens = q_ref.shape[0]
    size = tokens // 2
    small = copies([(within_hbm, within_ref)], sem)
    start(small)
    loads = [(q_hbm, q_ref, 1), (k_hbm, k_ref, 1), (v_hbm, v_ref, 1)]
    each_head(heads, lambda h: start(head_copies(loads, in_sems, h)))
    wait(small)

    def results(h):
        upper, lower = pl.ds(0, size), pl.ds(size, size)
        pairs = [
            (probs_ref.at[h, upper, upper], probs_hbm.at[h, upper, upper]),
            (probs_ref.at[h, lower], probs_hbm.at[h, lower]),
            (intra_ref.at[:, lanes(h)], intra_hbm.at[:, lanes(h)]),
        ]
        return [pltpu.make_async_copy(a, b, out_sems.at[i, h]) for i, (a, b) in enumerate(pairs)]

    def one(h):
        within = within_ref[pl.ds(h, 1), :]
        column = as_column(within)
        wait(head_copies(loads, in_sems, h))
        q, k, v = q_ref[:, lanes(h)], k_ref[:, lanes(h)], v_ref[:, lanes(h)]
        for first in (0, size):
            width = first + size
            scores = dot(q[first:width], k[0:width], NT)
            probs = (scores * decay_block(within, column, first, size, width)).astype(BF16)
            probs_ref[h, first:width, 0:width] = probs
            intra_ref[first:width, lanes(h)] = dot(probs, v[0:width], NN)
        start(results(h))

    each_head(heads, one)
    each_head(heads, lambda h: wait(results(h)))


def prepare_kernel(
    within_hbm, q_hbm, gate_hbm, up_hbm, dnorm_hbm, grown_hbm,
    within_ref, q_ref, gate_ref, up_ref, dnorm_ref, grown_ref, sem, in_sems, out_sems,
):
    heads = within_ref.shape[0]
    small = copies([(within_hbm, within_ref)], sem)
    start(small)
    loads = [(q_hbm, q_ref, 1), (gate_hbm, gate_ref, 1), (up_hbm, up_ref, 1)]
    stores = [(dnorm_ref, dnorm_hbm, 1), (grown_ref, grown_hbm, 2)]
    each_head(heads, lambda h: start(head_copies(loads, in_sems, h)))
    wait(small)

    def one(h):
        grow = as_column(jnp.exp(within_ref[pl.ds(h, 1), :]))
        wait(head_copies(loads, in_sems, h))
        dnorm_ref[:, lanes(h)] = up_ref[:, lanes(h)].astype(F32) * sigmoid(
            gate_ref[:, lanes(h)].astype(F32)
        )
        grown = q_ref[:, lanes(h)].astype(F32) * grow
        grown_ref[:, lanes(h, 2)] = jnp.concatenate(halves(grown), axis=1)
        start(head_copies(stores, out_sems, h))

    each_head(heads, one)
    each_head(heads, lambda h: wait(head_copies(stores, out_sems, h)))


def pick_state(follows, chip_ref, lead_ref, i):
    chip = chip_ref[i]
    return jnp.where(
        follows, lead_ref[i, HEAD : HEAD + 1, :] * chip + lead_ref[i, 0:HEAD, :], chip
    )


def attn_head(core, head, i, at, grown_ref, intra_ref, dnorm_ref, chip_ref, lead_ref, attn_ref, state_ref):
    state = pick_state(core == 1, chip_ref, lead_ref, i)
    state_ref[head] = state
    high, low = halves(state)
    grown = grown_ref[:, lanes(head, 2)]
    attn = intra_ref[:, at] + dot(
        jnp.concatenate([grown, grown[:, :HEAD]], axis=1),
        jnp.concatenate([high, high, low], axis=1),
        NT,
    )
    attn_ref[:, lanes(head)] = attn
    return attn * attn, dnorm_ref[:, lanes(head)] * attn


def attn_mine_kernel(
    core_ref, chip_ref, within_hbm, lead_hbm, grown_hbm, intra_hbm, dnorm_hbm,
    attn_ref, dnorm_ref, grown_ref, state_ref, square_ref, inner_ref, intra_far, within_ref,
    lead_ref, intra_ref, sems,
):
    core = core_ref[0]
    group = chip_ref.shape[0]
    pairs = [(lead_hbm, lead_ref)]
    for half, target in ((core, intra_ref), (1 - core, intra_far)):
        wide, two = half_of(half, group), half_of(half, group, 2)
        pairs += [
            (grown_hbm.at[:, two], grown_ref.at[:, two]),
            (intra_hbm.at[:, wide], target),
            (dnorm_hbm.at[:, wide], dnorm_ref.at[:, wide]),
        ]
    made = copies(pairs + [(within_hbm, within_ref)], sems)
    start(made)
    wait(made[:4])
    square = inner = jnp.zeros(square_ref.shape, F32)
    for i in range(group):
        more = attn_head(
            core, core * group + i, i, slice(i * HEAD, (i + 1) * HEAD), grown_ref, intra_ref,
            dnorm_ref, chip_ref, lead_ref, attn_ref, state_ref,
        )
        square, inner = square + more[0], inner + more[1]
    square_ref[...] = square
    inner_ref[...] = inner
    wait(made[4:])


def attn_other_kernel(
    core_ref, chip_ref, lead_ref, intra_ref, square_ref, inner_ref, dnorm_ref, grown_ref, attn_in, state_in,
    attn_ref, state_ref, sums_ref,
):
    core = core_ref[0]
    group = chip_ref.shape[0]
    square, inner = square_ref[...], inner_ref[...]
    for i in range(group):
        more = attn_head(
            core, (1 - core) * group + i, i, slice(i * HEAD, (i + 1) * HEAD), grown_ref, intra_ref,
            dnorm_ref, chip_ref, lead_ref, attn_ref, state_ref,
        )
        square, inner = square + more[0], inner + more[1]
    ones = jnp.ones((8, HEAD), F32)
    square = dot(ones, square, NT, HIGH)
    inner = dot(ones, inner, NT, HIGH)
    rows = lax.broadcasted_iota(jnp.int32, (8, HEAD), 0)
    packed = jnp.zeros((8, HEAD), F32)
    for i in range(4):
        cols = slice(i * HEAD, (i + 1) * HEAD)
        packed = jnp.where(rows == i, square[:, cols], packed)
        packed = jnp.where(rows == i + 4, inner[:, cols], packed)
    sums_ref[...] = jnp.broadcast_to(packed[None], sums_ref.shape)


def grad_head(head, i, within_ref, grown_ref, attn_ref, dnorm_ref, scale_ref, center_ref, out_ref):
    tokens = attn_ref.shape[0]
    scale = scale_ref[...]
    normed = attn_ref[:, lanes(head)] * scale
    grad = (scale * (dnorm_ref[:, lanes(head)] - normed * center_ref[...])).astype(BF16)
    last = within_ref[pl.ds(head, 1), :][:, tokens - 1 :]
    put_state(out_ref, i, outer_state(grown_ref[:, lanes(head, 2)], grad), jnp.exp(last))
    return grad


def grad_other_kernel(
    core_ref, sums_ref, within_ref, grown_ref, attn_ref, dnorm_ref,
    grad_ref, out_ref, scale_ref, center_ref, table_ref,
):
    total = jnp.sum(sums_ref[...], axis=0) / (HEAD_COUNT * HEAD)
    scale = lax.rsqrt(total[0:4] + 1e-06)
    center = scale * total[4:8]
    table_ref[0:4] = scale
    table_ref[4:8] = center
    for i in range(4):
        rows = slice(i * HEAD, (i + 1) * HEAD)
        scale_ref[rows] = as_column(scale[i : i + 1])
        center_ref[rows] = as_column(center[i : i + 1])
    group = out_ref.shape[0]
    for i in range(group):
        grad_ref[:, i * HEAD : (i + 1) * HEAD] = grad_head(
            (1 - core_ref[0]) * group + i, i, within_ref, grown_ref, attn_ref, dnorm_ref,
            scale_ref, center_ref, out_ref,
        )


def grad_mine_kernel(
    core_ref, scale_ref, center_ref, table_ref, within_ref, grown_ref, attn_ref, dnorm_ref, grad_far,
    grad_hbm, table_hbm, out_ref, grad_ref, sems, far_sems,
):
    core = core_ref[0]
    group = out_ref.shape[0]
    made = copies(
        [(grad_far, grad_hbm.at[:, half_of(1 - core, group)]), (table_ref, table_hbm)], far_sems
    )
    start(made)
    stores = []
    for i in range(group):
        head = core * group + i
        cols = slice(i * HEAD, (i + 1) * HEAD)
        grad_ref[:, cols] = grad_head(
            head, i, within_ref, grown_ref, attn_ref, dnorm_ref, scale_ref, center_ref, out_ref
        )
        store = pltpu.make_async_copy(
            grad_ref.at[:, cols], grad_hbm.at[:, lanes(head)], sems.at[i]
        )
        store.start()
        stores.append(store)
    wait(made + stores)


def gate_kernel(
    table_hbm, attn_hbm, gate_hbm, up_hbm, output_hbm, gate_grad_hbm,
    table_ref, attn_ref, gate_ref, up_ref, output_ref, gate_grad_ref, scale_ref, sem, in_sems, out_sems,
):
    heads = in_sems.shape[1]
    small = copies([(table_hbm, table_ref)], sem)
    start(small)
    loads = [(attn_hbm, attn_ref, 1), (gate_hbm, gate_ref, 1), (up_hbm, up_ref, 1)]
    stores = [(output_ref, output_hbm, 1), (gate_grad_ref, gate_grad_hbm, 1)]
    each_head(heads, lambda h: start(head_copies(loads, in_sems, h)))
    wait(small)
    for i in range(4):
        scale_ref[i * HEAD : (i + 1) * HEAD] = as_column(table_ref[i : i + 1])

    def one(h):
        wait(head_copies(loads, in_sems, h))
        normed = attn_ref[:, lanes(h)] * scale_ref[...]
        sig = sigmoid(gate_ref[:, lanes(h)].astype(F32))
        output_ref[:, lanes(h)] = (normed * sig).astype(BF16)
        gate_grad_ref[:, lanes(h)] = (
            up_ref[:, lanes(h)].astype(F32) * normed * sig * (1.0 - sig)
        ).astype(BF16)
        start(head_copies(stores, out_sems, h))

    each_head(heads, one)
    each_head(heads, lambda h: wait(head_copies(stores, out_sems, h)))


def back_kernel(
    within_hbm, q_hbm, k_hbm, v_hbm, grad_hbm, state_hbm, query_grad_hbm, key_hbm,
    within_ref, q_ref, k_ref, v_ref, grad_ref, state_ref, query_grad_ref, key_ref, sem, in_sems, out_sems,
):
    heads = within_ref.shape[0]
    tokens = q_ref.shape[0]
    size = tokens // 2
    small = copies([(within_hbm, within_ref)], sem)
    start(small)
    loads = [
        (grad_hbm, grad_ref, 1), (v_hbm, v_ref, 1), (k_hbm, k_ref, 1), (q_hbm, q_ref, 1),
        (state_hbm, state_ref, 0),
    ]
    stores = [(query_grad_ref, query_grad_hbm, 1), (key_ref, key_hbm, 1)]
    each_head(heads, lambda h: start(head_copies(loads, in_sems, h)))
    wait(small)

    def one(h):
        within = within_ref[pl.ds(h, 1), :]
        column = as_column(within)
        grow = jnp.exp(column)
        wait(head_copies(loads, in_sems, h))
        at = lanes(h)
        q, k, v = q_ref[:, at], k_ref[:, at], v_ref[:, at]
        state = jnp.concatenate(halves(state_ref[h]), axis=0)
        for first in (0, size):
            width = first + size
            grad = grad_ref[first:width, at]
            pgrad = dot(grad, v[0:width], NT)
            pgrad = (pgrad * decay_block(within, column, first, size, width)).astype(BF16)
            inter = dot(jnp.concatenate([grad, grad], axis=1), state, NN)
            query_grad_ref[first:width, at] = (
                dot(pgrad, k[0:width], NN) + grow[first:width] * inter
            ).astype(BF16)
            key_part = dot(pgrad, q[first:width], TN)
            if first == 0:
                key_ref[0:width, at] = key_part
            else:
                key_ref[0:first, at] += key_part[0:first]
                key_ref[first:width, at] = key_part[first:width]
        start(head_copies(stores, out_sems, h))

    each_head(heads, one)
    each_head(heads, lambda h: wait(head_copies(stores, out_sems, h)))


def value_kernel(
    grad_hbm, probs_hbm, value_hbm, grad_ref, probs_ref, value_ref, in_sems, out_sems
):
    heads = probs_ref.shape[0]
    tokens = grad_ref.shape[0]
    size = tokens // 2

    def loads(h):
        upper, lower = pl.ds(0, size), pl.ds(size, size)
        pairs = [
            (grad_hbm.at[:, lanes(h)], grad_ref.at[:, lanes(h)]),
            (probs_hbm.at[h, upper, upper], probs_ref.at[h, upper, upper]),
            (probs_hbm.at[h, lower], probs_ref.at[h, lower]),
        ]
        return [pltpu.make_async_copy(a, b, in_sems.at[i, h]) for i, (a, b) in enumerate(pairs)]

    stores = [(value_ref, value_hbm, 1)]
    each_head(heads, lambda h: start(loads(h)))

    def one(h):
        wait(loads(h))
        at = lanes(h)
        late = dot(probs_ref[h, size:tokens, :], grad_ref[size:tokens, at], TN)
        early = dot(probs_ref[h, 0:size, 0:size], grad_ref[0:size, at], TN)
        value_ref[0:size, at] = late[0:size] + early
        value_ref[size:tokens, at] = late[size:tokens]
        start(head_copies(stores, out_sems, h))

    each_head(heads, one)
    each_head(heads, lambda h: wait(head_copies(stores, out_sems, h)))


def final_head(core, head, i, within_ref, k_ref, v_ref, key_part_ref, value_part_ref, chip_ref, lead_ref):
    tokens = k_ref.shape[0]
    at = slice(i * HEAD, (i + 1) * HEAD)
    state = halves(pick_state(core == 0, chip_ref, lead_ref, i))
    within = within_ref[pl.ds(head, 1), :]
    tail = as_column(jnp.exp(within[:, tokens - 1 :] - within))
    k, v = k_ref[:, at], v_ref[:, at]
    key_inter = dot(jnp.concatenate([v, v], axis=1), jnp.concatenate(state, axis=0), NN)
    value_inter = dot(jnp.concatenate([k, k], axis=1), jnp.concatenate(state, axis=1), NT)
    return (
        (key_part_ref[:, at] + tail * key_inter).astype(BF16),
        (value_part_ref[:, at] + tail * value_inter).astype(BF16),
    )


def final_mine_kernel(
    core_ref, chip_ref, within_hbm, lead_hbm, k_hbm, v_hbm, key_part_hbm, value_part_hbm,
    key_grad_ref, value_grad_ref, k_far, v_far, key_part_far, value_part_far, within_ref,
    lead_ref, k_ref, v_ref, key_part_ref, value_part_ref, sems,
):
    core = core_ref[0]
    group = chip_ref.shape[0]
    sources = (k_hbm, v_hbm, key_part_hbm, value_part_hbm)
    near, far = half_of(core, group), half_of(1 - core, group)
    pairs = [(within_hbm, within_ref), (lead_hbm, lead_ref)]
    pairs += [(a.at[:, near], b) for a, b in zip(sources, (k_ref, v_ref, key_part_ref, value_part_ref))]
    pairs += [(a.at[:, far], b) for a, b in zip(sources, (k_far, v_far, key_part_far, value_part_far))]
    made = copies(pairs, sems)
    start(made)
    wait(made[:6])
    for i in range(group):
        cols = slice(i * HEAD, (i + 1) * HEAD)
        key_grad_ref[:, cols], value_grad_ref[:, cols] = final_head(
            core, core * group + i, i, within_ref, k_ref, v_ref, key_part_ref, value_part_ref,
            chip_ref, lead_ref,
        )
    wait(made[6:])


def final_other_kernel(
    core_ref, chip_ref, lead_ref, within_ref, k_ref, v_ref, key_part_ref, value_part_ref, key_near, value_near,
    key_grad_hbm, value_grad_hbm, key_grad_ref, value_grad_ref, near_sems, sems,
):
    core = core_ref[0]
    group = chip_ref.shape[0]
    near = half_of(core, group)
    made = copies(
        [(key_near, key_grad_hbm.at[:, near]), (value_near, value_grad_hbm.at[:, near])], near_sems
    )
    start(made)
    for i in range(group):
        cols = slice(i * HEAD, (i + 1) * HEAD)
        head = (1 - core) * group + i
        key_grad_ref[:, cols], value_grad_ref[:, cols] = final_head(
            core, head, i, within_ref, k_ref, v_ref, key_part_ref, value_part_ref, chip_ref, lead_ref
        )
        stores = [
            pltpu.make_async_copy(a.at[:, cols], b.at[:, lanes(head)], sems.at[j, i])
            for j, (a, b) in enumerate(((key_grad_ref, key_grad_hbm), (value_grad_ref, value_grad_hbm)))
        ]
        start(stores)
        made = made + stores
    wait(made)


def shape(dims, dtype=F32):
    return jax.ShapeDtypeStruct(dims, dtype)


def swap(x):
    return lax.ppermute(x, "c", [(0, 1), (1, 0)])


def spread(x):
    return lax.all_to_all(x, CHIPS, split_axis=0, concat_axis=0, tiled=True)


def call(kernel, name, near, far, near_out, far_out, buffers, sems, core=None, aliases=(), mib=16):
    scalars = () if core is None else (core,)
    vmem = pl.BlockSpec(memory_space=pltpu.VMEM)
    hbm = pl.BlockSpec(memory_space=pl.ANY)
    return pl.pallas_call(
        kernel,
        grid_spec=pltpu.PrefetchScalarGridSpec(
            num_scalar_prefetch=len(scalars),
            grid=(1,),
            in_specs=[vmem] * len(near) + [hbm] * len(far),
            out_specs=[hbm] * len(far_out) + [vmem] * len(near_out),
            scratch_shapes=[pltpu.VMEM(x.shape, x.dtype) for x in buffers]
            + [pltpu.SemaphoreType.DMA(dims) for dims in sems],
        ),
        out_shape=[pltpu.HBM(x.shape, x.dtype) for x in far_out]
        + [pltpu.VMEM(x.shape, x.dtype) for x in near_out],
        input_output_aliases=dict(aliases),
        compiler_params=pltpu.CompilerParams(
            dimension_semantics=("arbitrary",), vmem_limit_bytes=mib * 2**20
        ),
        name=name,
    )(*scalars, *near, *(pltpu.with_memory_space_constraint(x, pltpu.HBM) for x in far))


def shards(queries, keys, values, gate, log_decay, out_grad):
    tokens, flat = queries.shape
    heads = log_decay.shape[1]
    group = heads // 2
    chips = lax.axis_size("x") * lax.axis_size("y")
    rows = group * HEAD // chips
    core = lax.axis_index("c").astype(jnp.int32).reshape(1)
    packed = shape((group, HEAD + PAD, HEAD))
    sliced = shape((chips, rows, HEAD))
    carried = shape((chips, rows + PAD, HEAD))
    wide = shape((tokens, flat))
    narrow = shape((tokens, flat), BF16)
    double = shape((tokens, 2 * flat), BF16)
    half = shape((tokens, flat // 2))
    half_narrow = shape((tokens, flat // 2), BF16)
    column = shape((tokens, HEAD))
    states = shape((heads, HEAD, HEAD))
    table_rows = shape((8, HEAD))
    sums_rows = shape((8, 8, HEAD))
    rates = shape((heads, tokens))
    table_of = shape((heads, tokens, tokens), BF16)

    def combined(lead, mine, other):
        return call(
            combine_kernel, "combine", (mine, other), (), (), (carried, packed, packed), (carried,), ((3,),),
            lead,
        )

    def scanned(x, reverse):
        (out,) = call(
            lambda *refs: scan_kernel(reverse, *refs), "scan", (x,), (), (), (sliced,), (sliced,), ((1,),)
        )
        return out

    within, theirs, k_near, v_near = call(
        local_other_kernel, "local_other", (), (log_decay.T, keys, values),
        (rates, packed, half_narrow, half_narrow), (), (rates, half_narrow, half_narrow), ((5,),), core,
    )
    lead_mine = swap(theirs)
    (mine,) = call(
        local_mine_kernel, "local_mine", (within, k_near, v_near), (), (packed,), (), (), (), core
    )
    chip_state, mine, lead_mine = combined(1 - core, mine, lead_mine)
    chip_state = spread(chip_state)
    probs, intra = call(
        inside_kernel, "inside", (), (within, queries, keys, values), (), (table_of, wide),
        (rates, narrow, narrow, narrow, table_of, wide), ((1,), (3, heads), (3, heads)),
    )
    chip_state, probs, intra, mine, within = lax.optimization_barrier(
        (chip_state, probs, intra, mine, within)
    )
    chip_state, within = lax.optimization_barrier((scanned(chip_state, False), within))
    chip_mine = spread(chip_state)
    dnorm, grown = call(
        prepare_kernel, "prepare", (), (within, queries, gate, out_grad), (), (wide, double),
        (rates, narrow, narrow, narrow, wide, double), ((1,), (3, heads), (2, heads)),
    )
    chip_mine, mine, dnorm, grown = lax.optimization_barrier((chip_mine, mine, dnorm, grown))
    chip_mine = chip_mine.reshape(group, HEAD, HEAD)
    chip_other, lead_other = swap(chip_mine), swap(mine)
    attn, dnorm, grown, state, square, inner, intra_far, within_near = call(
        attn_mine_kernel, "attn_mine", (chip_mine,), (within, lead_mine, grown, intra, dnorm),
        (wide, wide, double, states, column, column, half, rates), (), (packed, half), ((8,),), core,
    )
    attn, state, sums = call(
        attn_other_kernel, "attn_other",
        (chip_other, lead_other, intra_far, square, inner, dnorm, grown, attn, state), (),
        (wide, states, sums_rows), (), (), (), core, {8: 0, 9: 1},
    )
    sums = lax.all_to_all(sums, "tp", split_axis=0, concat_axis=0, tiled=True)
    grad_far, theirs, scale, center, table = call(
        grad_other_kernel, "grad_other", (sums, within_near, grown, attn, dnorm), (),
        (half_narrow, packed, column, column, table_rows), (), (), (), core,
    )
    lead_mine = swap(theirs)
    grad, table, mine = call(
        grad_mine_kernel, "grad_mine",
        (scale, center, table, within_near, grown, attn, dnorm, grad_far), (),
        (packed,), (narrow, table_rows), (half_narrow,), ((group,), (2,)), core,
    )
    chip_state, mine, lead_mine = combined(core, mine, lead_mine)
    chip_state = spread(chip_state)
    query_grad, key_part = call(
        back_kernel, "back", (), (within, queries, keys, values, grad, state), (), (narrow, wide),
        (rates, narrow, narrow, narrow, narrow, states, narrow, wide), ((1,), (5, heads), (2, heads)),
    )
    chip_state, key_part, mine, grad, table = lax.optimization_barrier(
        (chip_state, key_part, mine, grad, table)
    )
    chip_state, grad, table = lax.optimization_barrier((scanned(chip_state, True), grad, table))
    chip_mine = spread(chip_state)
    (value_part,) = call(
        value_kernel, "value", (), (grad, probs), (), (wide,), (narrow, table_of, wide), ((3, heads), (1, heads))
    )
    output, gate_grad = call(
        gate_kernel, "gate", (), (table, attn, gate, out_grad), (), (narrow, narrow),
        (table_rows, wide, narrow, narrow, narrow, narrow, column), ((1,), (3, heads), (2, heads)),
    )
    chip_mine, value_part, output, gate_grad, mine = lax.optimization_barrier(
        (chip_mine, value_part, output, gate_grad, mine)
    )
    chip_mine = chip_mine.reshape(group, HEAD, HEAD)
    chip_other, lead_other = swap(chip_mine), swap(mine)
    key_near, value_near, *far, within_near = call(
        final_mine_kernel, "final_mine", (chip_mine,), (within, lead_mine, keys, values, key_part, value_part),
        (half_narrow, half_narrow, half_narrow, half_narrow, half, half, rates), (),
        (packed, half_narrow, half_narrow, half, half), ((10,),), core,
    )
    key_grad, value_grad = call(
        final_other_kernel, "final_other", (chip_other, lead_other, within_near, *far, key_near, value_near), (),
        (), (narrow, narrow), (half_narrow, half_narrow), ((2,), (2, group)), core,
    )
    return output, query_grad, key_grad, value_grad, gate_grad


def solution(mesh):
    split = Mesh(mesh.devices.reshape(4, 4, 2, mesh.shape["tp"]), ("x", "y", "c", "tp"))
    return jax.shard_map(
        shards,
        mesh=split,
        in_specs=(P(SEQ, "tp"),) * 6,
        out_specs=(P(SEQ, "tp"),) * 5,
        check_vma=False,
    )
```

```python
import jax
import jax.numpy as jnp
from jax import lax
from jax.experimental import pallas as pl
from jax.experimental.pallas import tpu as pltpu
from jax.sharding import Mesh
from jax.sharding import PartitionSpec as P

HEAD_COUNT = 64
HEAD = 128
SEQ = ("x", "y", "c")
CHIPS = ("x", "y")
HIGH = lax.Precision.HIGHEST
F32 = jnp.float32
BF16 = jnp.bfloat16
PAD = 8

NN = (((1,), (0,)), ((), ()))
NT = (((1,), (1,)), ((), ()))
TN = (((0,), (0,)), ((), ()))


def dot(a, b, dims, precision=None):
    return lax.dot_general(a, b, dims, precision=precision, preferred_element_type=F32)


def halves(x):
    high = x.astype(BF16)
    return high, (x - high.astype(F32)).astype(BF16)


def as_column(row):
    return jnp.transpose(jnp.broadcast_to(row, (HEAD, row.shape[1])))


def sigmoid(x):
    return 1.0 / (1.0 + jnp.exp(-x))


def lanes(head, count=1):
    return pl.ds(pl.multiple_of(head * (count * HEAD), HEAD), count * HEAD)


def put_state(ref, i, state, factor):
    ref[i, 0:HEAD, :] = state
    ref[i, HEAD : HEAD + PAD, :] = jnp.broadcast_to(factor, (PAD, HEAD))


def outer_state(wide, narrow):
    both = dot(narrow, wide, TN)
    return both[:, :HEAD] + both[:, HEAD:]


def sum_kernel(rate_ref, within_ref):
    heads, tokens = rate_ref.shape
    early = lax.broadcasted_iota(jnp.int32, (tokens, tokens), 0)
    late = lax.broadcasted_iota(jnp.int32, (tokens, tokens), 1)
    upto = (early <= late).astype(F32).astype(BF16)
    rate = rate_ref[...]
    high, rest = halves(rate)
    low = (rate - high.astype(F32) - rest.astype(F32)).astype(BF16)
    parts = jnp.concatenate([x.astype(F32) for x in (high, rest, low)], axis=0).astype(BF16)
    sums = dot(parts, upto, NN)
    within_ref[...] = sums[0:heads] + sums[heads : 2 * heads] + sums[2 * heads :]


def half_of(half, group, count=1):
    width = group * count * HEAD
    return pl.ds(pl.multiple_of(half * width, HEAD), width)


def copies(pairs, sems):
    return [pltpu.make_async_copy(a, b, sems.at[i]) for i, (a, b) in enumerate(pairs)]


def start(group):
    for copy in group:
        copy.start()


def wait(group):
    for copy in group:
        copy.wait()


def each_head(heads, body):
    def step(head, carry):
        body(head)
        return carry

    lax.fori_loop(0, heads, step, 0)


def each_pair(heads, before, work, after):
    def step(pair, carry):
        both = (2 * pair, 2 * pair + 1)
        for stage in (before, work, after):
            for head in both:
                stage(head)
        return carry

    lax.fori_loop(0, heads // 2, step, 0)


def head_copies(arrays, sems, head):
    made = []
    for i, (a, b, count) in enumerate(arrays):
        at = (head,) if count == 0 else (slice(None), lanes(head, count))
        made.append(pltpu.make_async_copy(a.at[at], b.at[at], sems.at[i, head]))
    return made


def local_state(head, cols, within_ref, k_ref, v_ref, out_ref, i):
    tokens = k_ref.shape[0]
    within = within_ref[pl.ds(head, 1), :]
    last = within[:, tokens - 1 :]
    tail = as_column(jnp.exp(last - within))
    scaled = jnp.concatenate(halves(k_ref[:, cols].astype(F32) * tail), axis=1)
    put_state(out_ref, i, outer_state(scaled, v_ref[:, cols]), jnp.exp(last))


def local_other_kernel(
    core_ref, rate_hbm, k_hbm, v_hbm, within_ref, out_ref, k_near, v_near, rate_ref, k_ref, v_ref, sems
):
    group = out_ref.shape[0]
    core = core_ref[0]
    far, near = half_of(1 - core, group), half_of(core, group)
    made = copies(
        [
            (rate_hbm, rate_ref),
            (v_hbm.at[:, far], v_ref),
            (k_hbm.at[:, far], k_ref),
            (v_hbm.at[:, near], v_near),
            (k_hbm.at[:, near], k_near),
        ],
        sems,
    )
    start(made)
    made[0].wait()
    sum_kernel(rate_ref, within_ref)
    wait(made[1:3])
    for i in range(group):
        cols = slice(i * HEAD, (i + 1) * HEAD)
        local_state((1 - core) * group + i, cols, within_ref, k_ref, v_ref, out_ref, i)
    wait(made[3:])


def local_mine_kernel(core_ref, within_ref, k_ref, v_ref, out_ref):
    group = out_ref.shape[0]
    for i in range(group):
        cols = slice(i * HEAD, (i + 1) * HEAD)
        local_state(core_ref[0] * group + i, cols, within_ref, k_ref, v_ref, out_ref, i)


def combine_kernel(
    lead_ref, mine_ref, other_ref, out_hbm, mine_hbm, other_hbm, out_ref, sems
):
    made = copies([(mine_ref, mine_hbm), (other_ref, other_hbm), (out_ref, out_hbm)], sems)
    start(made[:2])
    lead = lead_ref[0] == 1
    group = mine_ref.shape[0]
    rows = HEAD // 4
    for i in range(group):
        own = mine_ref[i, HEAD : HEAD + PAD, :]
        far = other_ref[i, HEAD : HEAD + PAD, :]
        mine = mine_ref[i, 0:HEAD, :]
        other = other_ref[i, 0:HEAD, :]
        both = jnp.where(lead, far[0:1] * mine + other, own[0:1] * other + mine)
        for j in range(4):
            out_ref[4 * i + j, 0:rows, :] = both[j * rows : (j + 1) * rows]
            out_ref[4 * i + j, rows : rows + PAD, :] = own * far
    made[2].start()
    wait(made)


def scan_kernel(reverse, in_ref, out_hbm, out_ref, sems):
    chips, rows = out_ref.shape[0], out_ref.shape[1]
    state = jnp.zeros(out_ref.shape[1:], F32)
    made = []
    for n in reversed(range(chips)) if reverse else range(chips):
        out_ref[n] = state
        state = in_ref[n, rows : rows + 1, :] * state + in_ref[n, 0:rows, :]
    made = copies([(out_ref, out_hbm)], sems)
    start(made)
    wait(made)


def decayed(scores, first, within, column):
    width = scores.shape[1]
    rows = lax.broadcasted_iota(jnp.int32, (HEAD, HEAD), 0)
    cols = lax.broadcasted_iota(jnp.int32, (HEAD, HEAD), 1)
    bands = []
    for start_at in range(first, width, HEAD):
        band = scores[start_at - first : start_at - first + HEAD]
        own = column[start_at : start_at + HEAD]
        pieces = []
        if start_at:
            edge = within[:, start_at - 1 : start_at]
            grow = jnp.concatenate([jnp.exp(own - edge)] * (start_at // HEAD), axis=1)
            pieces.append(band[:, :start_at] * jnp.exp(edge - within[:, :start_at]) * grow)
        gap = own - within[:, start_at : start_at + HEAD]
        inside = jnp.where(rows >= cols, jnp.exp(jnp.minimum(gap, 0.0)), 0.0)
        pieces.append(band[:, start_at : start_at + HEAD] * inside)
        if start_at + HEAD < width:
            pieces.append(jnp.zeros((HEAD, width - start_at - HEAD), F32))
        bands.append(jnp.concatenate(pieces, axis=1).astype(BF16))
    return jnp.concatenate(bands, axis=0)


def inside_kernel(
    within_hbm, q_hbm, k_hbm, v_hbm, probs_hbm, intra_hbm,
    within_ref, q_ref, k_ref, v_ref, probs_ref, intra_ref, sem, in_sems, out_sems,
):
    heads = within_ref.shape[0]
    tokens = q_ref.shape[0]
    size = tokens // 2
    small = copies([(within_hbm, within_ref)], sem)
    start(small)
    loads = [(q_hbm, q_ref, 1), (k_hbm, k_ref, 1), (v_hbm, v_ref, 1)]
    each_head(heads, lambda h: start(head_copies(loads, in_sems, h)))
    wait(small)

    def results(h):
        upper, lower = pl.ds(0, size), pl.ds(size, size)
        pairs = [
            (probs_ref.at[h, upper, upper], probs_hbm.at[h, upper, upper]),
            (probs_ref.at[h, lower], probs_hbm.at[h, lower]),
            (intra_ref.at[:, lanes(h)], intra_hbm.at[:, lanes(h)]),
        ]
        return [pltpu.make_async_copy(a, b, out_sems.at[i, h]) for i, (a, b) in enumerate(pairs)]

    def one(h):
        within = within_ref[pl.ds(h, 1), :]
        column = as_column(within)
        q, k, v = q_ref[:, lanes(h)], k_ref[:, lanes(h)], v_ref[:, lanes(h)]
        for first in (0, size):
            width = first + size
            probs = decayed(dot(q[first:width], k[0:width], NT), first, within, column)
            probs_ref[h, first:width, 0:width] = probs
            intra_ref[first:width, lanes(h)] = dot(probs, v[0:width], NN)

    each_pair(heads, lambda h: wait(head_copies(loads, in_sems, h)), one, lambda h: start(results(h)))
    each_head(heads, lambda h: wait(results(h)))


def prepare_kernel(
    within_hbm, q_hbm, gate_hbm, up_hbm, dnorm_hbm, grown_hbm,
    within_ref, q_ref, gate_ref, up_ref, dnorm_ref, grown_ref, sem, in_sems, out_sems,
):
    heads = within_ref.shape[0]
    small = copies([(within_hbm, within_ref)], sem)
    start(small)
    loads = [(q_hbm, q_ref, 1), (gate_hbm, gate_ref, 1), (up_hbm, up_ref, 1)]
    stores = [(dnorm_ref, dnorm_hbm, 1), (grown_ref, grown_hbm, 2)]
    each_head(heads, lambda h: start(head_copies(loads, in_sems, h)))
    wait(small)

    def one(h):
        grow = as_column(jnp.exp(within_ref[pl.ds(h, 1), :]))
        dnorm_ref[:, lanes(h)] = up_ref[:, lanes(h)].astype(F32) * sigmoid(
            gate_ref[:, lanes(h)].astype(F32)
        )
        grown = q_ref[:, lanes(h)].astype(F32) * grow
        grown_ref[:, lanes(h, 2)] = jnp.concatenate(halves(grown), axis=1)

    each_pair(
        heads, lambda h: wait(head_copies(loads, in_sems, h)), one,
        lambda h: start(head_copies(stores, out_sems, h)),
    )
    each_head(heads, lambda h: wait(head_copies(stores, out_sems, h)))


def pick_state(follows, chip_ref, lead_ref, i):
    chip = chip_ref[i]
    return jnp.where(
        follows, lead_ref[i, HEAD : HEAD + 1, :] * chip + lead_ref[i, 0:HEAD, :], chip
    )


def attn_head(core, head, i, at, grown_ref, intra_ref, dnorm_ref, chip_ref, lead_ref, attn_ref, state_ref):
    state = pick_state(core == 1, chip_ref, lead_ref, i)
    state_ref[head] = state
    high, low = halves(state)
    grown = grown_ref[:, lanes(head, 2)]
    attn = intra_ref[:, at] + dot(
        jnp.concatenate([grown, grown[:, :HEAD]], axis=1),
        jnp.concatenate([high, high, low], axis=1),
        NT,
    )
    attn_ref[:, lanes(head)] = attn
    return attn * attn, dnorm_ref[:, lanes(head)] * attn


def attn_mine_kernel(
    core_ref, chip_ref, within_hbm, lead_hbm, grown_hbm, intra_hbm, dnorm_hbm,
    attn_ref, dnorm_ref, grown_ref, state_ref, square_ref, inner_ref, intra_far, within_ref,
    lead_ref, intra_ref, sems,
):
    core = core_ref[0]
    group = chip_ref.shape[0]
    pairs = [(lead_hbm, lead_ref)]
    for half, target in ((core, intra_ref), (1 - core, intra_far)):
        wide, two = half_of(half, group), half_of(half, group, 2)
        pairs += [
            (grown_hbm.at[:, two], grown_ref.at[:, two]),
            (intra_hbm.at[:, wide], target),
            (dnorm_hbm.at[:, wide], dnorm_ref.at[:, wide]),
        ]
    made = copies(pairs + [(within_hbm, within_ref)], sems)
    start(made)
    wait(made[:4])
    square = inner = jnp.zeros(square_ref.shape, F32)
    for i in range(group):
        more = attn_head(
            core, core * group + i, i, slice(i * HEAD, (i + 1) * HEAD), grown_ref, intra_ref,
            dnorm_ref, chip_ref, lead_ref, attn_ref, state_ref,
        )
        square, inner = square + more[0], inner + more[1]
    square_ref[...] = square
    inner_ref[...] = inner
    wait(made[4:])


def attn_other_kernel(
    core_ref, chip_ref, lead_ref, intra_ref, square_ref, inner_ref, dnorm_ref, grown_ref, attn_in, state_in,
    attn_ref, state_ref, sums_ref,
):
    core = core_ref[0]
    group = chip_ref.shape[0]
    square, inner = square_ref[...], inner_ref[...]
    for i in range(group):
        more = attn_head(
            core, (1 - core) * group + i, i, slice(i * HEAD, (i + 1) * HEAD), grown_ref, intra_ref,
            dnorm_ref, chip_ref, lead_ref, attn_ref, state_ref,
        )
        square, inner = square + more[0], inner + more[1]
    ones = jnp.ones((8, HEAD), F32)
    square = dot(ones, square, NT, HIGH)
    inner = dot(ones, inner, NT, HIGH)
    rows = lax.broadcasted_iota(jnp.int32, (8, HEAD), 0)
    packed = jnp.zeros((8, HEAD), F32)
    for i in range(4):
        cols = slice(i * HEAD, (i + 1) * HEAD)
        packed = jnp.where(rows == i, square[:, cols], packed)
        packed = jnp.where(rows == i + 4, inner[:, cols], packed)
    sums_ref[...] = jnp.broadcast_to(packed[None], sums_ref.shape)


def grad_head(head, i, within_ref, grown_ref, attn_ref, dnorm_ref, scale_ref, center_ref, out_ref):
    tokens = attn_ref.shape[0]
    scale = scale_ref[...]
    normed = attn_ref[:, lanes(head)] * scale
    grad = (scale * (dnorm_ref[:, lanes(head)] - normed * center_ref[...])).astype(BF16)
    last = within_ref[pl.ds(head, 1), :][:, tokens - 1 :]
    put_state(out_ref, i, outer_state(grown_ref[:, lanes(head, 2)], grad), jnp.exp(last))
    return grad


def grad_other_kernel(
    core_ref, sums_ref, within_ref, grown_ref, attn_ref, dnorm_ref,
    grad_ref, out_ref, scale_ref, center_ref, table_ref,
):
    total = jnp.sum(sums_ref[...], axis=0) / (HEAD_COUNT * HEAD)
    scale = lax.rsqrt(total[0:4] + 1e-06)
    center = scale * total[4:8]
    table_ref[0:4] = scale
    table_ref[4:8] = center
    for i in range(4):
        rows = slice(i * HEAD, (i + 1) * HEAD)
        scale_ref[rows] = as_column(scale[i : i + 1])
        center_ref[rows] = as_column(center[i : i + 1])
    group = out_ref.shape[0]
    for i in range(group):
        grad_ref[:, i * HEAD : (i + 1) * HEAD] = grad_head(
            (1 - core_ref[0]) * group + i, i, within_ref, grown_ref, attn_ref, dnorm_ref,
            scale_ref, center_ref, out_ref,
        )


def grad_mine_kernel(
    core_ref, scale_ref, center_ref, table_ref, within_ref, grown_ref, attn_ref, dnorm_ref, grad_far,
    grad_hbm, table_hbm, out_ref, grad_ref, sems, far_sems,
):
    core = core_ref[0]
    group = out_ref.shape[0]
    made = copies(
        [(grad_far, grad_hbm.at[:, half_of(1 - core, group)]), (table_ref, table_hbm)], far_sems
    )
    start(made)
    stores = []
    for i in range(group):
        head = core * group + i
        cols = slice(i * HEAD, (i + 1) * HEAD)
        grad_ref[:, cols] = grad_head(
            head, i, within_ref, grown_ref, attn_ref, dnorm_ref, scale_ref, center_ref, out_ref
        )
        store = pltpu.make_async_copy(
            grad_ref.at[:, cols], grad_hbm.at[:, lanes(head)], sems.at[i]
        )
        store.start()
        stores.append(store)
    wait(made + stores)


def back_kernel(
    within_hbm, q_hbm, k_hbm, v_hbm, grad_hbm, state_hbm, query_grad_hbm, key_hbm,
    within_ref, q_ref, k_ref, v_ref, grad_ref, state_ref, query_grad_ref, key_ref, sem, in_sems, out_sems,
):
    heads = within_ref.shape[0]
    tokens = q_ref.shape[0]
    size = tokens // 2
    small = copies([(within_hbm, within_ref)], sem)
    start(small)
    loads = [
        (grad_hbm, grad_ref, 1), (v_hbm, v_ref, 1), (k_hbm, k_ref, 1), (q_hbm, q_ref, 1),
        (state_hbm, state_ref, 0),
    ]
    stores = [(query_grad_ref, query_grad_hbm, 1), (key_ref, key_hbm, 1)]
    each_head(heads, lambda h: start(head_copies(loads, in_sems, h)))
    wait(small)

    def one(h):
        within = within_ref[pl.ds(h, 1), :]
        column = as_column(within)
        grow = jnp.exp(column)
        at = lanes(h)
        q, k, v = q_ref[:, at], k_ref[:, at], v_ref[:, at]
        state = jnp.concatenate(halves(state_ref[h]), axis=0)
        for first in (0, size):
            width = first + size
            grad = grad_ref[first:width, at]
            pgrad = decayed(dot(grad, v[0:width], NT), first, within, column)
            inter = dot(jnp.concatenate([grad, grad], axis=1), state, NN)
            query_grad_ref[first:width, at] = (
                dot(pgrad, k[0:width], NN) + grow[first:width] * inter
            ).astype(BF16)
            key_part = dot(pgrad, q[first:width], TN)
            if first == 0:
                key_ref[0:width, at] = key_part
            else:
                key_ref[0:first, at] += key_part[0:first]
                key_ref[first:width, at] = key_part[first:width]

    each_pair(
        heads, lambda h: wait(head_copies(loads, in_sems, h)), one,
        lambda h: start(head_copies(stores, out_sems, h)),
    )
    each_head(heads, lambda h: wait(head_copies(stores, out_sems, h)))


def value_gate_kernel(
    table_hbm, attn_hbm, gate_hbm, up_hbm, grad_hbm, probs_hbm, value_hbm, output_hbm, gate_grad_hbm,
    table_ref, attn_ref, gate_ref, up_ref, grad_ref, probs_ref, value_ref, output_ref, gate_grad_ref,
    scale_ref, sem, in_sems, out_sems,
):
    heads = probs_ref.shape[0]
    tokens = grad_ref.shape[0]
    size = tokens // 2
    small = copies([(table_hbm, table_ref)], sem)
    start(small)

    def loads(h):
        upper, lower = pl.ds(0, size), pl.ds(size, size)
        pairs = [
            (probs_hbm.at[h, upper, upper], probs_ref.at[h, upper, upper]),
            (probs_hbm.at[h, lower], probs_ref.at[h, lower]),
        ]
        pairs += [
            (a.at[:, lanes(h)], b.at[:, lanes(h)])
            for a, b in (
                (grad_hbm, grad_ref), (attn_hbm, attn_ref), (gate_hbm, gate_ref), (up_hbm, up_ref)
            )
        ]
        return [pltpu.make_async_copy(a, b, in_sems.at[i, h]) for i, (a, b) in enumerate(pairs)]

    stores = [(value_ref, value_hbm, 1), (output_ref, output_hbm, 1), (gate_grad_ref, gate_grad_hbm, 1)]
    each_head(heads, lambda h: start(loads(h)))
    wait(small)
    for i in range(4):
        scale_ref[i * HEAD : (i + 1) * HEAD] = as_column(table_ref[i : i + 1])

    def one(h):
        at = lanes(h)
        late = dot(probs_ref[h, size:tokens, :], grad_ref[size:tokens, at], TN)
        early = dot(probs_ref[h, 0:size, 0:size], grad_ref[0:size, at], TN)
        normed = attn_ref[:, at] * scale_ref[...]
        sig = sigmoid(gate_ref[:, at].astype(F32))
        output_ref[:, at] = (normed * sig).astype(BF16)
        gate_grad_ref[:, at] = (up_ref[:, at].astype(F32) * normed * sig * (1.0 - sig)).astype(BF16)
        value_ref[0:size, at] = late[0:size] + early
        value_ref[size:tokens, at] = late[size:tokens]

    each_pair(
        heads, lambda h: wait(loads(h)), one, lambda h: start(head_copies(stores, out_sems, h))
    )
    each_head(heads, lambda h: wait(head_copies(stores, out_sems, h)))


def final_head(core, head, i, within_ref, k_ref, v_ref, key_part_ref, value_part_ref, chip_ref, lead_ref):
    tokens = k_ref.shape[0]
    at = slice(i * HEAD, (i + 1) * HEAD)
    state = halves(pick_state(core == 0, chip_ref, lead_ref, i))
    within = within_ref[pl.ds(head, 1), :]
    tail = as_column(jnp.exp(within[:, tokens - 1 :] - within))
    k, v = k_ref[:, at], v_ref[:, at]
    key_inter = dot(jnp.concatenate([v, v], axis=1), jnp.concatenate(state, axis=0), NN)
    value_inter = dot(jnp.concatenate([k, k], axis=1), jnp.concatenate(state, axis=1), NT)
    return (
        (key_part_ref[:, at] + tail * key_inter).astype(BF16),
        (value_part_ref[:, at] + tail * value_inter).astype(BF16),
    )


def final_mine_kernel(
    core_ref, chip_ref, within_hbm, lead_hbm, k_hbm, v_hbm, key_part_hbm, value_part_hbm,
    key_grad_ref, value_grad_ref, k_far, v_far, key_part_far, value_part_far, within_ref,
    lead_ref, k_ref, v_ref, key_part_ref, value_part_ref, sems,
):
    core = core_ref[0]
    group = chip_ref.shape[0]
    sources = (k_hbm, v_hbm, key_part_hbm, value_part_hbm)
    near, far = half_of(core, group), half_of(1 - core, group)
    pairs = [(within_hbm, within_ref), (lead_hbm, lead_ref)]
    pairs += [(a.at[:, near], b) for a, b in zip(sources, (k_ref, v_ref, key_part_ref, value_part_ref))]
    pairs += [(a.at[:, far], b) for a, b in zip(sources, (k_far, v_far, key_part_far, value_part_far))]
    made = copies(pairs, sems)
    start(made)
    wait(made[:6])
    for i in range(group):
        cols = slice(i * HEAD, (i + 1) * HEAD)
        key_grad_ref[:, cols], value_grad_ref[:, cols] = final_head(
            core, core * group + i, i, within_ref, k_ref, v_ref, key_part_ref, value_part_ref,
            chip_ref, lead_ref,
        )
    wait(made[6:])


def final_other_kernel(
    core_ref, chip_ref, lead_ref, within_ref, k_ref, v_ref, key_part_ref, value_part_ref, key_near, value_near,
    key_grad_hbm, value_grad_hbm, key_grad_ref, value_grad_ref, near_sems, sems,
):
    core = core_ref[0]
    group = chip_ref.shape[0]
    near = half_of(core, group)
    made = copies(
        [(key_near, key_grad_hbm.at[:, near]), (value_near, value_grad_hbm.at[:, near])], near_sems
    )
    start(made)
    for i in range(group):
        cols = slice(i * HEAD, (i + 1) * HEAD)
        head = (1 - core) * group + i
        key_grad_ref[:, cols], value_grad_ref[:, cols] = final_head(
            core, head, i, within_ref, k_ref, v_ref, key_part_ref, value_part_ref, chip_ref, lead_ref
        )
        stores = [
            pltpu.make_async_copy(a.at[:, cols], b.at[:, lanes(head)], sems.at[j, i])
            for j, (a, b) in enumerate(((key_grad_ref, key_grad_hbm), (value_grad_ref, value_grad_hbm)))
        ]
        start(stores)
        made = made + stores
    wait(made)


def shape(dims, dtype=F32):
    return jax.ShapeDtypeStruct(dims, dtype)


def swap(x):
    return lax.ppermute(x, "c", [(0, 1), (1, 0)])


def spread(x):
    return lax.all_to_all(x, CHIPS, split_axis=0, concat_axis=0, tiled=True)


def call(kernel, name, near, far, near_out, far_out, buffers, sems, core=None, aliases=(), mib=16):
    scalars = () if core is None else (core,)
    vmem = pl.BlockSpec(memory_space=pltpu.VMEM)
    hbm = pl.BlockSpec(memory_space=pl.ANY)
    return pl.pallas_call(
        kernel,
        grid_spec=pltpu.PrefetchScalarGridSpec(
            num_scalar_prefetch=len(scalars),
            grid=(1,),
            in_specs=[vmem] * len(near) + [hbm] * len(far),
            out_specs=[hbm] * len(far_out) + [vmem] * len(near_out),
            scratch_shapes=[pltpu.VMEM(x.shape, x.dtype) for x in buffers]
            + [pltpu.SemaphoreType.DMA(dims) for dims in sems],
        ),
        out_shape=[pltpu.HBM(x.shape, x.dtype) for x in far_out]
        + [pltpu.VMEM(x.shape, x.dtype) for x in near_out],
        input_output_aliases=dict(aliases),
        compiler_params=pltpu.CompilerParams(
            dimension_semantics=("arbitrary",), vmem_limit_bytes=mib * 2**20
        ),
        name=name,
    )(*scalars, *near, *(pltpu.with_memory_space_constraint(x, pltpu.HBM) for x in far))


def shards(queries, keys, values, gate, log_decay, out_grad):
    tokens, flat = queries.shape
    heads = log_decay.shape[1]
    group = heads // 2
    chips = lax.axis_size("x") * lax.axis_size("y")
    rows = group * HEAD // chips
    core = lax.axis_index("c").astype(jnp.int32).reshape(1)
    packed = shape((group, HEAD + PAD, HEAD))
    sliced = shape((chips, rows, HEAD))
    carried = shape((chips, rows + PAD, HEAD))
    wide = shape((tokens, flat))
    narrow = shape((tokens, flat), BF16)
    double = shape((tokens, 2 * flat), BF16)
    half = shape((tokens, flat // 2))
    half_narrow = shape((tokens, flat // 2), BF16)
    column = shape((tokens, HEAD))
    states = shape((heads, HEAD, HEAD))
    table_rows = shape((8, HEAD))
    sums_rows = shape((8, 8, HEAD))
    rates = shape((heads, tokens))
    table_of = shape((heads, tokens, tokens), BF16)

    def combined(lead, mine, other):
        return call(
            combine_kernel, "combine", (mine, other), (), (), (carried, packed, packed), (carried,), ((3,),),
            lead,
        )

    def scanned(x, reverse):
        (out,) = call(
            lambda *refs: scan_kernel(reverse, *refs), "scan", (x,), (), (), (sliced,), (sliced,), ((1,),)
        )
        return out

    within, theirs, k_near, v_near = call(
        local_other_kernel, "local_other", (), (log_decay.T, keys, values),
        (rates, packed, half_narrow, half_narrow), (), (rates, half_narrow, half_narrow), ((5,),), core,
    )
    lead_mine = swap(theirs)
    (mine,) = call(
        local_mine_kernel, "local_mine", (within, k_near, v_near), (), (packed,), (), (), (), core
    )
    chip_state, mine, lead_mine = combined(1 - core, mine, lead_mine)
    chip_state = spread(chip_state)
    probs, intra = call(
        inside_kernel, "inside", (), (within, queries, keys, values), (), (table_of, wide),
        (rates, narrow, narrow, narrow, table_of, wide), ((1,), (3, heads), (3, heads)),
    )
    chip_state, probs, intra, mine, within = lax.optimization_barrier(
        (chip_state, probs, intra, mine, within)
    )
    chip_state, within = lax.optimization_barrier((scanned(chip_state, False), within))
    chip_mine = spread(chip_state)
    dnorm, grown = call(
        prepare_kernel, "prepare", (), (within, queries, gate, out_grad), (), (wide, double),
        (rates, narrow, narrow, narrow, wide, double), ((1,), (3, heads), (2, heads)),
    )
    chip_mine, mine, dnorm, grown = lax.optimization_barrier((chip_mine, mine, dnorm, grown))
    chip_mine = chip_mine.reshape(group, HEAD, HEAD)
    chip_other, lead_other = swap(chip_mine), swap(mine)
    attn, dnorm, grown, state, square, inner, intra_far, within_near = call(
        attn_mine_kernel, "attn_mine", (chip_mine,), (within, lead_mine, grown, intra, dnorm),
        (wide, wide, double, states, column, column, half, rates), (), (packed, half), ((8,),), core,
    )
    attn, state, sums = call(
        attn_other_kernel, "attn_other",
        (chip_other, lead_other, intra_far, square, inner, dnorm, grown, attn, state), (),
        (wide, states, sums_rows), (), (), (), core, {8: 0, 9: 1},
    )
    sums = lax.all_to_all(sums, "tp", split_axis=0, concat_axis=0, tiled=True)
    grad_far, theirs, scale, center, table = call(
        grad_other_kernel, "grad_other", (sums, within_near, grown, attn, dnorm), (),
        (half_narrow, packed, column, column, table_rows), (), (), (), core,
    )
    lead_mine = swap(theirs)
    grad, table, mine = call(
        grad_mine_kernel, "grad_mine",
        (scale, center, table, within_near, grown, attn, dnorm, grad_far), (),
        (packed,), (narrow, table_rows), (half_narrow,), ((group,), (2,)), core,
    )
    chip_state, mine, lead_mine = combined(core, mine, lead_mine)
    chip_state = spread(chip_state)
    query_grad, key_part = call(
        back_kernel, "back", (), (within, queries, keys, values, grad, state), (), (narrow, wide),
        (rates, narrow, narrow, narrow, narrow, states, narrow, wide), ((1,), (5, heads), (2, heads)),
    )
    chip_state, key_part, mine, grad, table = lax.optimization_barrier(
        (chip_state, key_part, mine, grad, table)
    )
    chip_state, grad, table = lax.optimization_barrier((scanned(chip_state, True), grad, table))
    chip_mine = spread(chip_state)
    value_part, output, gate_grad = call(
        value_gate_kernel, "value_gate", (), (table, attn, gate, out_grad, grad, probs), (), (wide, narrow, narrow),
        (table_rows, wide, narrow, narrow, narrow, table_of, wide, narrow, narrow, column),
        ((1,), (6, heads), (3, heads)), mib=24,
    )
    chip_mine, value_part, output, gate_grad, mine = lax.optimization_barrier(
        (chip_mine, value_part, output, gate_grad, mine)
    )
    chip_mine = chip_mine.reshape(group, HEAD, HEAD)
    chip_other, lead_other = swap(chip_mine), swap(mine)
    key_near, value_near, *far, within_near = call(
        final_mine_kernel, "final_mine", (chip_mine,), (within, lead_mine, keys, values, key_part, value_part),
        (half_narrow, half_narrow, half_narrow, half_narrow, half, half, rates), (),
        (packed, half_narrow, half_narrow, half, half), ((10,),), core,
    )
    key_grad, value_grad = call(
        final_other_kernel, "final_other", (chip_other, lead_other, within_near, *far, key_near, value_near), (),
        (), (narrow, narrow), (half_narrow, half_narrow), ((2,), (2, group)), core,
    )
    return output, query_grad, key_grad, value_grad, gate_grad


def solution(mesh):
    split = Mesh(mesh.devices.reshape(4, 4, 2, mesh.shape["tp"]), ("x", "y", "c", "tp"))
    return jax.shard_map(
        shards,
        mesh=split,
        in_specs=(P(SEQ, "tp"),) * 6,
        out_specs=(P(SEQ, "tp"),) * 5,
        check_vma=False,
    )
```

```python
import jax
import jax.numpy as jnp
from jax import lax
from jax.experimental import pallas as pl
from jax.experimental.pallas import tpu as pltpu
from jax.sharding import Mesh
from jax.sharding import PartitionSpec as P

HEAD_COUNT = 64
HEAD = 128
SEQ = ("x", "y", "c")
CHIPS = ("x", "y")
HIGH = lax.Precision.HIGHEST
F32 = jnp.float32
BF16 = jnp.bfloat16
PAD = 8

NN = (((1,), (0,)), ((), ()))
NT = (((1,), (1,)), ((), ()))
TN = (((0,), (0,)), ((), ()))


def dot(a, b, dims, precision=None):
    return lax.dot_general(a, b, dims, precision=precision, preferred_element_type=F32)


def halves(x):
    high = x.astype(BF16)
    return high, (x - high.astype(F32)).astype(BF16)


def as_column(row):
    return jnp.transpose(jnp.broadcast_to(row, (HEAD, row.shape[1])))


def sigmoid(x):
    return 1.0 / (1.0 + jnp.exp(-x))


def lanes(head, count=1):
    return pl.ds(pl.multiple_of(head * (count * HEAD), HEAD), count * HEAD)


def put_state(ref, i, state, factor):
    ref[i, 0:HEAD, :] = state
    ref[i, HEAD : HEAD + PAD, :] = jnp.broadcast_to(factor, (PAD, HEAD))


def outer_state(wide, narrow):
    both = dot(narrow, wide, TN)
    return both[:, :HEAD] + both[:, HEAD:]


def sum_over(rate_ref, within_ref, rate_copy):
    heads, tokens = rate_ref.shape
    early = lax.broadcasted_iota(jnp.int32, (tokens, tokens), 0)
    late = lax.broadcasted_iota(jnp.int32, (tokens, tokens), 1)
    upto = (early <= late).astype(F32).astype(BF16)
    rate_copy.wait()
    rate = rate_ref[...]
    high, rest = halves(rate)
    low = (rate - high.astype(F32) - rest.astype(F32)).astype(BF16)
    parts = jnp.concatenate([x.astype(F32) for x in (high, rest, low)], axis=0).astype(BF16)
    sums = dot(parts, upto, NN)
    within_ref[...] = sums[0:heads] + sums[heads : 2 * heads] + sums[2 * heads :]


def half_of(half, group, count=1):
    width = group * count * HEAD
    return pl.ds(pl.multiple_of(half * width, HEAD), width)


def copies(pairs, sems):
    return [pltpu.make_async_copy(a, b, sems.at[i]) for i, (a, b) in enumerate(pairs)]


def start(group):
    for copy in group:
        copy.start()


def wait(group):
    for copy in group:
        copy.wait()


def each_head(heads, body):
    def step(head, carry):
        body(head)
        return carry

    lax.fori_loop(0, heads, step, 0)


def each_pair(heads, before, work, after):
    def step(pair, carry):
        both = (2 * pair, 2 * pair + 1)
        for stage in (before, work, after):
            for head in both:
                stage(head)
        return carry

    lax.fori_loop(0, heads // 2, step, 0)


def head_copies(arrays, sems, head):
    made = []
    for i, (a, b, count) in enumerate(arrays):
        at = (head,) if count == 0 else (slice(None), lanes(head, count))
        made.append(pltpu.make_async_copy(a.at[at], b.at[at], sems.at[i, head]))
    return made


def local_state(head, cols, within_ref, k_ref, v_ref, out_ref, i):
    tokens = k_ref.shape[0]
    within = within_ref[pl.ds(head, 1), :]
    last = within[:, tokens - 1 :]
    tail = as_column(jnp.exp(last - within))
    scaled = jnp.concatenate(halves(k_ref[:, cols].astype(F32) * tail), axis=1)
    put_state(out_ref, i, outer_state(scaled, v_ref[:, cols]), jnp.exp(last))


def local_other_kernel(
    core_ref, rate_hbm, k_hbm, v_hbm, within_ref, out_ref, k_near, v_near, rate_ref, k_ref, v_ref, sems
):
    group = out_ref.shape[0]
    core = core_ref[0]
    far, near = half_of(1 - core, group), half_of(core, group)
    made = copies(
        [
            (rate_hbm, rate_ref),
            (v_hbm.at[:, far], v_ref),
            (k_hbm.at[:, far], k_ref),
            (v_hbm.at[:, near], v_near),
            (k_hbm.at[:, near], k_near),
        ],
        sems,
    )
    start(made)
    sum_over(rate_ref, within_ref, made[0])
    wait(made[1:3])
    for i in range(group):
        cols = slice(i * HEAD, (i + 1) * HEAD)
        local_state((1 - core) * group + i, cols, within_ref, k_ref, v_ref, out_ref, i)
    wait(made[3:])


def local_mine_kernel(core_ref, within_ref, k_ref, v_ref, out_ref):
    group = out_ref.shape[0]
    for i in range(group):
        cols = slice(i * HEAD, (i + 1) * HEAD)
        local_state(core_ref[0] * group + i, cols, within_ref, k_ref, v_ref, out_ref, i)


def combine_kernel(
    lead_ref, mine_ref, other_ref, out_hbm, mine_hbm, other_hbm, out_ref, sems
):
    group = mine_ref.shape[0]
    made = copies([(mine_ref, mine_hbm), (other_ref, other_hbm)], sems)
    lead = lead_ref[0] == 1
    rows = HEAD // 4
    for i in range(group):
        own = mine_ref[i, HEAD : HEAD + PAD, :]
        far = other_ref[i, HEAD : HEAD + PAD, :]
        mine = mine_ref[i, 0:HEAD, :]
        other = other_ref[i, 0:HEAD, :]
        both = jnp.where(lead, far[0:1] * mine + other, own[0:1] * other + mine)
        for j in range(4):
            out_ref[4 * i + j, 0:rows, :] = both[j * rows : (j + 1) * rows]
            out_ref[4 * i + j, rows : rows + PAD, :] = own * far
        part = pl.ds(4 * i, 4)
        store = pltpu.make_async_copy(out_ref.at[part], out_hbm.at[part], sems.at[2 + i])
        store.start()
        made.append(store)
    start(made[:2])
    wait(made)


def scan_kernel(reverse, in_ref, out_hbm, out_ref, sems):
    chips, rows = out_ref.shape[0], out_ref.shape[1]
    state = jnp.zeros(out_ref.shape[1:], F32)
    made = []
    for n in reversed(range(chips)) if reverse else range(chips):
        out_ref[n] = state
        state = in_ref[n, rows : rows + 1, :] * state + in_ref[n, 0:rows, :]
    made = copies([(out_ref, out_hbm)], sems)
    start(made)
    wait(made)


def decayed(scores, first, within, column):
    width = scores.shape[1]
    rows = lax.broadcasted_iota(jnp.int32, (HEAD, HEAD), 0)
    cols = lax.broadcasted_iota(jnp.int32, (HEAD, HEAD), 1)
    bands = []
    for start_at in range(first, width, HEAD):
        band = scores[start_at - first : start_at - first + HEAD]
        own = column[start_at : start_at + HEAD]
        pieces = []
        if start_at:
            edge = within[:, start_at - 1 : start_at]
            grow = jnp.concatenate([jnp.exp(own - edge)] * (start_at // HEAD), axis=1)
            pieces.append(band[:, :start_at] * jnp.exp(edge - within[:, :start_at]) * grow)
        gap = own - within[:, start_at : start_at + HEAD]
        inside = jnp.where(rows >= cols, jnp.exp(jnp.minimum(gap, 0.0)), 0.0)
        pieces.append(band[:, start_at : start_at + HEAD] * inside)
        if start_at + HEAD < width:
            pieces.append(jnp.zeros((HEAD, width - start_at - HEAD), F32))
        bands.append(jnp.concatenate(pieces, axis=1).astype(BF16))
    return jnp.concatenate(bands, axis=0)


def inside_kernel(
    within_hbm, q_hbm, k_hbm, v_hbm, probs_hbm, intra_hbm,
    within_ref, q_ref, k_ref, v_ref, probs_ref, intra_ref, sem, in_sems, out_sems,
):
    heads = within_ref.shape[0]
    tokens = q_ref.shape[0]
    size = tokens // 2
    small = copies([(within_hbm, within_ref)], sem)
    start(small)
    loads = [(q_hbm, q_ref, 1), (k_hbm, k_ref, 1), (v_hbm, v_ref, 1)]
    each_head(heads, lambda h: start(head_copies(loads, in_sems, h)))
    wait(small)

    def results(h):
        upper, lower = pl.ds(0, size), pl.ds(size, size)
        pairs = [
            (probs_ref.at[h, upper, upper], probs_hbm.at[h, upper, upper]),
            (probs_ref.at[h, lower], probs_hbm.at[h, lower]),
            (intra_ref.at[:, lanes(h)], intra_hbm.at[:, lanes(h)]),
        ]
        return [pltpu.make_async_copy(a, b, out_sems.at[i, h]) for i, (a, b) in enumerate(pairs)]

    def one(h):
        within = within_ref[pl.ds(h, 1), :]
        column = as_column(within)
        q, k, v = q_ref[:, lanes(h)], k_ref[:, lanes(h)], v_ref[:, lanes(h)]
        for first in (0, size):
            width = first + size
            probs = decayed(dot(q[first:width], k[0:width], NT), first, within, column)
            probs_ref[h, first:width, 0:width] = probs
            intra_ref[first:width, lanes(h)] = dot(probs, v[0:width], NN)

    each_pair(heads, lambda h: wait(head_copies(loads, in_sems, h)), one, lambda h: start(results(h)))
    each_head(heads, lambda h: wait(results(h)))


def prepare_kernel(
    within_hbm, q_hbm, gate_hbm, up_hbm, dnorm_hbm, grown_hbm,
    within_ref, q_ref, gate_ref, up_ref, dnorm_ref, grown_ref, sem, in_sems, out_sems,
):
    heads = within_ref.shape[0]
    small = copies([(within_hbm, within_ref)], sem)
    start(small)
    loads = [(q_hbm, q_ref, 1), (gate_hbm, gate_ref, 1), (up_hbm, up_ref, 1)]
    stores = [(dnorm_ref, dnorm_hbm, 1), (grown_ref, grown_hbm, 2)]
    each_head(heads, lambda h: start(head_copies(loads, in_sems, h)))
    wait(small)

    def one(h):
        grow = as_column(jnp.exp(within_ref[pl.ds(h, 1), :]))
        dnorm_ref[:, lanes(h)] = up_ref[:, lanes(h)].astype(F32) * sigmoid(
            gate_ref[:, lanes(h)].astype(F32)
        )
        grown = q_ref[:, lanes(h)].astype(F32) * grow
        grown_ref[:, lanes(h, 2)] = jnp.concatenate(halves(grown), axis=1)

    each_pair(
        heads, lambda h: wait(head_copies(loads, in_sems, h)), one,
        lambda h: start(head_copies(stores, out_sems, h)),
    )
    each_head(heads, lambda h: wait(head_copies(stores, out_sems, h)))


def pick_state(follows, chip_ref, lead_ref, i):
    chip = chip_ref[i]
    return jnp.where(
        follows, lead_ref[i, HEAD : HEAD + 1, :] * chip + lead_ref[i, 0:HEAD, :], chip
    )


def attn_head(core, head, i, at, grown_ref, intra_ref, dnorm_ref, chip_ref, lead_ref, attn_ref, state_ref):
    state = pick_state(core == 1, chip_ref, lead_ref, i)
    state_ref[head] = state
    high, low = halves(state)
    grown = grown_ref[:, lanes(head, 2)]
    attn = intra_ref[:, at] + dot(
        jnp.concatenate([grown, grown[:, :HEAD]], axis=1),
        jnp.concatenate([high, high, low], axis=1),
        NT,
    )
    attn_ref[:, lanes(head)] = attn
    return attn * attn, dnorm_ref[:, lanes(head)] * attn


def attn_mine_kernel(
    core_ref, chip_ref, within_hbm, lead_hbm, grown_hbm, intra_hbm, dnorm_hbm,
    attn_ref, dnorm_ref, grown_ref, state_ref, square_ref, inner_ref, intra_far, within_ref,
    lead_ref, intra_ref, sems,
):
    core = core_ref[0]
    group = chip_ref.shape[0]
    pairs = [(lead_hbm, lead_ref)]
    for half, target in ((core, intra_ref), (1 - core, intra_far)):
        wide, two = half_of(half, group), half_of(half, group, 2)
        pairs += [
            (grown_hbm.at[:, two], grown_ref.at[:, two]),
            (intra_hbm.at[:, wide], target),
            (dnorm_hbm.at[:, wide], dnorm_ref.at[:, wide]),
        ]
    made = copies(pairs + [(within_hbm, within_ref)], sems)
    start(made)
    wait(made[:4])
    square = inner = jnp.zeros(square_ref.shape, F32)
    for i in range(group):
        more = attn_head(
            core, core * group + i, i, slice(i * HEAD, (i + 1) * HEAD), grown_ref, intra_ref,
            dnorm_ref, chip_ref, lead_ref, attn_ref, state_ref,
        )
        square, inner = square + more[0], inner + more[1]
    square_ref[...] = square
    inner_ref[...] = inner
    wait(made[4:])


def attn_other_kernel(
    core_ref, chip_ref, lead_ref, intra_ref, square_ref, inner_ref, dnorm_ref, grown_ref, attn_in, state_in,
    attn_ref, state_ref, sums_ref,
):
    core = core_ref[0]
    group = chip_ref.shape[0]
    square, inner = square_ref[...], inner_ref[...]
    for i in range(group):
        more = attn_head(
            core, (1 - core) * group + i, i, slice(i * HEAD, (i + 1) * HEAD), grown_ref, intra_ref,
            dnorm_ref, chip_ref, lead_ref, attn_ref, state_ref,
        )
        square, inner = square + more[0], inner + more[1]
    ones = jnp.ones((8, HEAD), F32)
    square = dot(ones, square, NT, HIGH)
    inner = dot(ones, inner, NT, HIGH)
    rows = lax.broadcasted_iota(jnp.int32, (8, HEAD), 0)
    packed = jnp.zeros((8, HEAD), F32)
    for i in range(4):
        cols = slice(i * HEAD, (i + 1) * HEAD)
        packed = jnp.where(rows == i, square[:, cols], packed)
        packed = jnp.where(rows == i + 4, inner[:, cols], packed)
    sums_ref[...] = jnp.broadcast_to(packed[None], sums_ref.shape)


def grad_head(head, attn_ref, dnorm_ref, scale_ref, center_ref):
    scale = scale_ref[...]
    normed = attn_ref[:, lanes(head)] * scale
    return (scale * (dnorm_ref[:, lanes(head)] - normed * center_ref[...])).astype(BF16)


def grad_state(head, i, grad, within_ref, grown_ref, out_ref):
    last = within_ref[pl.ds(head, 1), :][:, grad.shape[0] - 1 :]
    put_state(out_ref, i, outer_state(grown_ref[:, lanes(head, 2)], grad), jnp.exp(last))


def grad_other_kernel(
    core_ref, sums_ref, within_ref, grown_ref, attn_ref, dnorm_ref,
    grad_ref, out_ref, scale_ref, center_ref, table_ref,
):
    total = jnp.sum(sums_ref[...], axis=0) / (HEAD_COUNT * HEAD)
    scale = lax.rsqrt(total[0:4] + 1e-06)
    center = scale * total[4:8]
    table_ref[0:4] = scale
    table_ref[4:8] = center
    for i in range(4):
        rows = slice(i * HEAD, (i + 1) * HEAD)
        scale_ref[rows] = as_column(scale[i : i + 1])
        center_ref[rows] = as_column(center[i : i + 1])
    group = out_ref.shape[0]
    for i in range(group):
        head = (1 - core_ref[0]) * group + i
        grad = grad_head(head, attn_ref, dnorm_ref, scale_ref, center_ref)
        grad_ref[:, i * HEAD : (i + 1) * HEAD] = grad
        grad_state(head, i, grad, within_ref, grown_ref, out_ref)


def grad_mine_kernel(
    core_ref, scale_ref, center_ref, table_ref, within_ref, grown_ref, attn_ref, dnorm_ref, grad_far,
    grad_hbm, table_hbm, out_ref, grad_ref, sems, far_sems,
):
    core = core_ref[0]
    group = out_ref.shape[0]
    made = copies(
        [(grad_far, grad_hbm.at[:, half_of(1 - core, group)]), (table_ref, table_hbm)], far_sems
    )
    start(made)
    for i in range(group):
        head = core * group + i
        cols = slice(i * HEAD, (i + 1) * HEAD)
        grad_ref[:, cols] = grad_head(head, attn_ref, dnorm_ref, scale_ref, center_ref)
        store = pltpu.make_async_copy(
            grad_ref.at[:, cols], grad_hbm.at[:, lanes(head)], sems.at[i]
        )
        store.start()
        made.append(store)
    for i in range(group):
        grad = grad_ref[:, i * HEAD : (i + 1) * HEAD]
        grad_state(core * group + i, i, grad, within_ref, grown_ref, out_ref)
    wait(made)


def back_kernel(
    within_hbm, q_hbm, k_hbm, v_hbm, grad_hbm, state_hbm, query_grad_hbm, key_hbm,
    within_ref, q_ref, k_ref, v_ref, grad_ref, state_ref, query_grad_ref, key_ref, sem, in_sems, out_sems,
):
    heads = within_ref.shape[0]
    tokens = q_ref.shape[0]
    size = tokens // 2
    small = copies([(within_hbm, within_ref)], sem)
    start(small)
    loads = [
        (grad_hbm, grad_ref, 1), (v_hbm, v_ref, 1), (k_hbm, k_ref, 1), (q_hbm, q_ref, 1),
        (state_hbm, state_ref, 0),
    ]
    stores = [(query_grad_ref, query_grad_hbm, 1), (key_ref, key_hbm, 1)]
    each_head(heads, lambda h: start(head_copies(loads, in_sems, h)))
    wait(small)

    def one(h):
        within = within_ref[pl.ds(h, 1), :]
        column = as_column(within)
        grow = jnp.exp(column)
        at = lanes(h)
        q, k, v = q_ref[:, at], k_ref[:, at], v_ref[:, at]
        state = jnp.concatenate(halves(state_ref[h]), axis=0)
        for first in (0, size):
            width = first + size
            grad = grad_ref[first:width, at]
            pgrad = decayed(dot(grad, v[0:width], NT), first, within, column)
            inter = dot(jnp.concatenate([grad, grad], axis=1), state, NN)
            query_grad_ref[first:width, at] = (
                dot(pgrad, k[0:width], NN) + grow[first:width] * inter
            ).astype(BF16)
            key_part = dot(pgrad, q[first:width], TN)
            if first == 0:
                early = key_part
            else:
                key_ref[0:first, at] = (early + key_part[0:first]).astype(BF16)
                key_ref[first:width, at] = key_part[first:width].astype(BF16)

    each_pair(
        heads, lambda h: wait(head_copies(loads, in_sems, h)), one,
        lambda h: start(head_copies(stores, out_sems, h)),
    )
    each_head(heads, lambda h: wait(head_copies(stores, out_sems, h)))


def value_gate_kernel(
    table_hbm, attn_hbm, gate_hbm, up_hbm, grad_hbm, probs_hbm, value_hbm, output_hbm, gate_grad_hbm,
    table_ref, attn_ref, gate_ref, up_ref, grad_ref, probs_ref, value_ref, output_ref, gate_grad_ref,
    scale_ref, sem, in_sems, out_sems,
):
    heads = probs_ref.shape[0]
    tokens = grad_ref.shape[0]
    size = tokens // 2
    small = copies([(table_hbm, table_ref)], sem)
    start(small)

    def loads(h):
        upper, lower = pl.ds(0, size), pl.ds(size, size)
        pairs = [
            (probs_hbm.at[h, upper, upper], probs_ref.at[h, upper, upper]),
            (probs_hbm.at[h, lower], probs_ref.at[h, lower]),
        ]
        pairs += [
            (a.at[:, lanes(h)], b.at[:, lanes(h)])
            for a, b in (
                (grad_hbm, grad_ref), (attn_hbm, attn_ref), (gate_hbm, gate_ref), (up_hbm, up_ref)
            )
        ]
        return [pltpu.make_async_copy(a, b, in_sems.at[i, h]) for i, (a, b) in enumerate(pairs)]

    stores = [(value_ref, value_hbm, 1), (output_ref, output_hbm, 1), (gate_grad_ref, gate_grad_hbm, 1)]
    each_head(heads, lambda h: start(loads(h)))
    wait(small)
    for i in range(4):
        scale_ref[i * HEAD : (i + 1) * HEAD] = as_column(table_ref[i : i + 1])

    def one(h):
        at = lanes(h)
        late = dot(probs_ref[h, size:tokens, :], grad_ref[size:tokens, at], TN)
        early = dot(probs_ref[h, 0:size, 0:size], grad_ref[0:size, at], TN)
        normed = attn_ref[:, at] * scale_ref[...]
        sig = sigmoid(gate_ref[:, at].astype(F32))
        output_ref[:, at] = (normed * sig).astype(BF16)
        gate_grad_ref[:, at] = (up_ref[:, at].astype(F32) * normed * sig * (1.0 - sig)).astype(BF16)
        value_ref[0:size, at] = (late[0:size] + early).astype(BF16)
        value_ref[size:tokens, at] = late[size:tokens].astype(BF16)

    each_pair(
        heads, lambda h: wait(loads(h)), one, lambda h: start(head_copies(stores, out_sems, h))
    )
    each_head(heads, lambda h: wait(head_copies(stores, out_sems, h)))


def final_head(core, head, i, within_ref, k_ref, v_ref, key_part_ref, value_part_ref, chip_ref, lead_ref):
    tokens = k_ref.shape[0]
    at = slice(i * HEAD, (i + 1) * HEAD)
    state = halves(pick_state(core == 0, chip_ref, lead_ref, i))
    within = within_ref[pl.ds(head, 1), :]
    tail = as_column(jnp.exp(within[:, tokens - 1 :] - within))
    k, v = k_ref[:, at], v_ref[:, at]
    key_inter = dot(jnp.concatenate([v, v], axis=1), jnp.concatenate(state, axis=0), NN)
    value_inter = dot(jnp.concatenate([k, k], axis=1), jnp.concatenate(state, axis=1), NT)
    return (
        (key_part_ref[:, at].astype(F32) + tail * key_inter).astype(BF16),
        (value_part_ref[:, at].astype(F32) + tail * value_inter).astype(BF16),
    )


def final_mine_kernel(
    core_ref, chip_ref, within_hbm, lead_hbm, k_hbm, v_hbm, key_part_hbm, value_part_hbm,
    key_grad_ref, value_grad_ref, k_far, v_far, key_part_far, value_part_far, within_ref,
    lead_ref, k_ref, v_ref, key_part_ref, value_part_ref, sems,
):
    core = core_ref[0]
    group = chip_ref.shape[0]
    sources = (k_hbm, v_hbm, key_part_hbm, value_part_hbm)
    near, far = half_of(core, group), half_of(1 - core, group)
    pairs = [(within_hbm, within_ref), (lead_hbm, lead_ref)]
    pairs += [(a.at[:, near], b) for a, b in zip(sources, (k_ref, v_ref, key_part_ref, value_part_ref))]
    pairs += [(a.at[:, far], b) for a, b in zip(sources, (k_far, v_far, key_part_far, value_part_far))]
    made = copies(pairs, sems)
    start(made)
    wait(made[:6])
    for i in range(group):
        cols = slice(i * HEAD, (i + 1) * HEAD)
        key_grad_ref[:, cols], value_grad_ref[:, cols] = final_head(
            core, core * group + i, i, within_ref, k_ref, v_ref, key_part_ref, value_part_ref,
            chip_ref, lead_ref,
        )
    wait(made[6:])


def final_other_kernel(
    core_ref, chip_ref, lead_ref, within_ref, k_ref, v_ref, key_part_ref, value_part_ref, key_near, value_near,
    key_grad_hbm, value_grad_hbm, key_grad_ref, value_grad_ref, near_sems, sems,
):
    core = core_ref[0]
    group = chip_ref.shape[0]
    near = half_of(core, group)
    made = copies(
        [(key_near, key_grad_hbm.at[:, near]), (value_near, value_grad_hbm.at[:, near])], near_sems
    )
    start(made)
    for i in range(group):
        cols = slice(i * HEAD, (i + 1) * HEAD)
        head = (1 - core) * group + i
        key_grad_ref[:, cols], value_grad_ref[:, cols] = final_head(
            core, head, i, within_ref, k_ref, v_ref, key_part_ref, value_part_ref, chip_ref, lead_ref
        )
        stores = [
            pltpu.make_async_copy(a.at[:, cols], b.at[:, lanes(head)], sems.at[j, i])
            for j, (a, b) in enumerate(((key_grad_ref, key_grad_hbm), (value_grad_ref, value_grad_hbm)))
        ]
        start(stores)
        made = made + stores
    wait(made)


def shape(dims, dtype=F32):
    return jax.ShapeDtypeStruct(dims, dtype)


def swap(x):
    return lax.ppermute(x, "c", [(0, 1), (1, 0)])


def spread(x):
    return lax.all_to_all(x, CHIPS, split_axis=0, concat_axis=0, tiled=True)


def call(kernel, name, near, far, near_out, far_out, buffers, sems, core=None, aliases=(), mib=16):
    scalars = () if core is None else (core,)
    vmem = pl.BlockSpec(memory_space=pltpu.VMEM)
    hbm = pl.BlockSpec(memory_space=pl.ANY)
    return pl.pallas_call(
        kernel,
        grid_spec=pltpu.PrefetchScalarGridSpec(
            num_scalar_prefetch=len(scalars),
            grid=(1,),
            in_specs=[vmem] * len(near) + [hbm] * len(far),
            out_specs=[hbm] * len(far_out) + [vmem] * len(near_out),
            scratch_shapes=[pltpu.VMEM(x.shape, x.dtype) for x in buffers]
            + [pltpu.SemaphoreType.DMA(dims) for dims in sems],
        ),
        out_shape=[pltpu.HBM(x.shape, x.dtype) for x in far_out]
        + [pltpu.VMEM(x.shape, x.dtype) for x in near_out],
        input_output_aliases=dict(aliases),
        compiler_params=pltpu.CompilerParams(
            dimension_semantics=("arbitrary",), vmem_limit_bytes=mib * 2**20
        ),
        name=name,
    )(*scalars, *near, *(pltpu.with_memory_space_constraint(x, pltpu.HBM) for x in far))


def shards(queries, keys, values, gate, log_decay, out_grad):
    tokens, flat = queries.shape
    heads = log_decay.shape[1]
    group = heads // 2
    chips = lax.axis_size("x") * lax.axis_size("y")
    rows = group * HEAD // chips
    core = lax.axis_index("c").astype(jnp.int32).reshape(1)
    packed = shape((group, HEAD + PAD, HEAD))
    sliced = shape((chips, rows, HEAD))
    carried = shape((chips, rows + PAD, HEAD))
    wide = shape((tokens, flat))
    narrow = shape((tokens, flat), BF16)
    double = shape((tokens, 2 * flat), BF16)
    half = shape((tokens, flat // 2))
    half_narrow = shape((tokens, flat // 2), BF16)
    column = shape((tokens, HEAD))
    states = shape((heads, HEAD, HEAD))
    table_rows = shape((8, HEAD))
    sums_rows = shape((8, 8, HEAD))
    rates = shape((heads, tokens))
    table_of = shape((heads, tokens, tokens), BF16)

    def combined(lead, mine, other):
        return call(
            combine_kernel, "combine", (mine, other), (), (), (carried, packed, packed), (carried,), ((2 + group,),),
            lead,
        )

    def scanned(x, reverse):
        (out,) = call(
            lambda *refs: scan_kernel(reverse, *refs), "scan", (x,), (), (), (sliced,), (sliced,), ((1,),)
        )
        return out

    within, theirs, k_near, v_near = call(
        local_other_kernel, "local_other", (), (log_decay.T, keys, values),
        (rates, packed, half_narrow, half_narrow), (), (rates, half_narrow, half_narrow), ((5,),), core,
    )
    lead_mine = swap(theirs)
    (mine,) = call(
        local_mine_kernel, "local_mine", (within, k_near, v_near), (), (packed,), (), (), (), core
    )
    chip_state, mine, lead_mine = combined(1 - core, mine, lead_mine)
    chip_state = spread(chip_state)
    probs, intra = call(
        inside_kernel, "inside", (), (within, queries, keys, values), (), (table_of, wide),
        (rates, narrow, narrow, narrow, table_of, wide), ((1,), (3, heads), (3, heads)),
    )
    chip_state, probs, intra, mine, within = lax.optimization_barrier(
        (chip_state, probs, intra, mine, within)
    )
    chip_state, within = lax.optimization_barrier((scanned(chip_state, False), within))
    chip_mine = spread(chip_state)
    dnorm, grown = call(
        prepare_kernel, "prepare", (), (within, queries, gate, out_grad), (), (wide, double),
        (rates, narrow, narrow, narrow, wide, double), ((1,), (3, heads), (2, heads)),
    )
    chip_mine, mine, dnorm, grown = lax.optimization_barrier((chip_mine, mine, dnorm, grown))
    chip_mine = chip_mine.reshape(group, HEAD, HEAD)
    chip_other, lead_other = swap(chip_mine), swap(mine)
    attn, dnorm, grown, state, square, inner, intra_far, within_near = call(
        attn_mine_kernel, "attn_mine", (chip_mine,), (within, lead_mine, grown, intra, dnorm),
        (wide, wide, double, states, column, column, half, rates), (), (packed, half), ((8,),), core,
    )
    attn, state, sums = call(
        attn_other_kernel, "attn_other",
        (chip_other, lead_other, intra_far, square, inner, dnorm, grown, attn, state), (),
        (wide, states, sums_rows), (), (), (), core, {8: 0, 9: 1},
    )
    sums = lax.all_to_all(sums, "tp", split_axis=0, concat_axis=0, tiled=True)
    grad_far, theirs, scale, center, table = call(
        grad_other_kernel, "grad_other", (sums, within_near, grown, attn, dnorm), (),
        (half_narrow, packed, column, column, table_rows), (), (), (), core,
    )
    lead_mine = swap(theirs)
    grad, table, mine = call(
        grad_mine_kernel, "grad_mine",
        (scale, center, table, within_near, grown, attn, dnorm, grad_far), (),
        (packed,), (narrow, table_rows), (half_narrow,), ((group,), (2,)), core,
    )
    chip_state, mine, lead_mine = combined(core, mine, lead_mine)
    chip_state = spread(chip_state)
    query_grad, key_part = call(
        back_kernel, "back", (), (within, queries, keys, values, grad, state), (), (narrow, narrow),
        (rates, narrow, narrow, narrow, narrow, states, narrow, narrow), ((1,), (5, heads), (2, heads)),
    )
    chip_state, key_part, mine, grad, table = lax.optimization_barrier(
        (chip_state, key_part, mine, grad, table)
    )
    chip_state, grad, table = lax.optimization_barrier((scanned(chip_state, True), grad, table))
    chip_mine = spread(chip_state)
    value_part, output, gate_grad = call(
        value_gate_kernel, "value_gate", (), (table, attn, gate, out_grad, grad, probs), (), (narrow, narrow, narrow),
        (table_rows, wide, narrow, narrow, narrow, table_of, narrow, narrow, narrow, column),
        ((1,), (6, heads), (3, heads)), mib=24,
    )
    chip_mine, value_part, output, gate_grad, mine = lax.optimization_barrier(
        (chip_mine, value_part, output, gate_grad, mine)
    )
    chip_mine = chip_mine.reshape(group, HEAD, HEAD)
    chip_other, lead_other = swap(chip_mine), swap(mine)
    key_near, value_near, *far, within_near = call(
        final_mine_kernel, "final_mine", (chip_mine,), (within, lead_mine, keys, values, key_part, value_part),
        (half_narrow,) * 6 + (rates,), (), (packed,) + (half_narrow,) * 4, ((10,),), core,
    )
    key_grad, value_grad = call(
        final_other_kernel, "final_other", (chip_other, lead_other, within_near, *far, key_near, value_near), (),
        (), (narrow, narrow), (half_narrow, half_narrow), ((2,), (2, group)), core,
    )
    return output, query_grad, key_grad, value_grad, gate_grad


def solution(mesh):
    split = Mesh(mesh.devices.reshape(4, 4, 2, mesh.shape["tp"]), ("x", "y", "c", "tp"))
    return jax.shard_map(
        shards,
        mesh=split,
        in_specs=(P(SEQ, "tp"),) * 6,
        out_specs=(P(SEQ, "tp"),) * 5,
        check_vma=False,
    )
```

```python
import jax
import jax.numpy as jnp
from jax import lax
from jax.experimental import pallas as pl
from jax.experimental.pallas import tpu as pltpu
from jax.sharding import Mesh
from jax.sharding import PartitionSpec as P

HEAD_COUNT = 64
HEAD = 128
SEQ = ("x", "y", "c")
CHIPS = ("x", "y")
HIGH = lax.Precision.HIGHEST
F32 = jnp.float32
BF16 = jnp.bfloat16
PAD = 8

NN = (((1,), (0,)), ((), ()))
NT = (((1,), (1,)), ((), ()))
TN = (((0,), (0,)), ((), ()))


def dot(a, b, dims, precision=None):
    return lax.dot_general(a, b, dims, precision=precision, preferred_element_type=F32)


def halves(x):
    high = x.astype(BF16)
    return high, (x - high.astype(F32)).astype(BF16)


def as_column(row):
    return jnp.transpose(jnp.broadcast_to(row, (HEAD, row.shape[1])))


def sigmoid(x):
    return 1.0 / (1.0 + jnp.exp(-x))


def lanes(head, count=1):
    return pl.ds(pl.multiple_of(head * (count * HEAD), HEAD), count * HEAD)


def put_state(ref, i, state, factor):
    ref[i, 0:HEAD, :] = state
    ref[i, HEAD : HEAD + PAD, :] = jnp.broadcast_to(factor, (PAD, HEAD))


def outer_state(wide, narrow):
    both = dot(narrow, wide, TN)
    return both[:, :HEAD] + both[:, HEAD:]


def sum_over(rate_ref, within_ref, rate_copy):
    heads, tokens = rate_ref.shape
    early = lax.broadcasted_iota(jnp.int32, (tokens, tokens), 0)
    late = lax.broadcasted_iota(jnp.int32, (tokens, tokens), 1)
    upto = (early <= late).astype(F32).astype(BF16)
    rate_copy.wait()
    rate = rate_ref[...]
    high, rest = halves(rate)
    low = (rate - high.astype(F32) - rest.astype(F32)).astype(BF16)
    parts = jnp.concatenate([x.astype(F32) for x in (high, rest, low)], axis=0).astype(BF16)
    sums = dot(parts, upto, NN)
    within_ref[...] = sums[0:heads] + sums[heads : 2 * heads] + sums[2 * heads :]


def half_of(half, group, count=1):
    width = group * count * HEAD
    return pl.ds(pl.multiple_of(half * width, HEAD), width)


def copies(pairs, sems):
    return [pltpu.make_async_copy(a, b, sems.at[i]) for i, (a, b) in enumerate(pairs)]


def start(group):
    for copy in group:
        copy.start()


def wait(group):
    for copy in group:
        copy.wait()


def each_head(heads, body):
    def step(head, carry):
        body(head)
        return carry

    lax.fori_loop(0, heads, step, 0)


def each_pair(heads, before, work, after):
    def step(pair, carry):
        both = (2 * pair, 2 * pair + 1)
        for stage in (before, work, after):
            for head in both:
                stage(head)
        return carry

    lax.fori_loop(0, heads // 2, step, 0)


def head_copies(arrays, sems, head):
    made = []
    for i, (a, b, count) in enumerate(arrays):
        at = (head,) if count == 0 else (slice(None), lanes(head, count))
        made.append(pltpu.make_async_copy(a.at[at], b.at[at], sems.at[i, head]))
    return made


def local_state(head, cols, within_ref, k_ref, v_ref, out_ref, i):
    tokens = k_ref.shape[0]
    within = within_ref[pl.ds(head, 1), :]
    last = within[:, tokens - 1 :]
    tail = as_column(jnp.exp(last - within))
    scaled = jnp.concatenate(halves(k_ref[:, cols].astype(F32) * tail), axis=1)
    put_state(out_ref, i, outer_state(scaled, v_ref[:, cols]), jnp.exp(last))


def local_other_kernel(
    core_ref, rate_hbm, k_hbm, v_hbm, within_ref, out_ref, k_near, v_near, rate_ref, k_ref, v_ref, sems
):
    group = out_ref.shape[0]
    core = core_ref[0]
    far, near = half_of(1 - core, group), half_of(core, group)
    made = copies(
        [
            (rate_hbm, rate_ref),
            (v_hbm.at[:, far], v_ref),
            (k_hbm.at[:, far], k_ref),
            (v_hbm.at[:, near], v_near),
            (k_hbm.at[:, near], k_near),
        ],
        sems,
    )
    start(made)
    sum_over(rate_ref, within_ref, made[0])
    wait(made[1:3])
    for i in range(group):
        cols = slice(i * HEAD, (i + 1) * HEAD)
        local_state((1 - core) * group + i, cols, within_ref, k_ref, v_ref, out_ref, i)
    wait(made[3:])


def local_mine_kernel(core_ref, within_ref, k_ref, v_ref, out_ref):
    group = out_ref.shape[0]
    for i in range(group):
        cols = slice(i * HEAD, (i + 1) * HEAD)
        local_state(core_ref[0] * group + i, cols, within_ref, k_ref, v_ref, out_ref, i)


def combine_kernel(
    lead_ref, mine_ref, other_ref, out_hbm, mine_hbm, other_hbm, out_ref, sems
):
    group = mine_ref.shape[0]
    made = copies([(mine_ref, mine_hbm), (other_ref, other_hbm)], sems)
    lead = lead_ref[0] == 1
    rows = HEAD // 4
    for i in range(group):
        own = mine_ref[i, HEAD : HEAD + PAD, :]
        far = other_ref[i, HEAD : HEAD + PAD, :]
        mine = mine_ref[i, 0:HEAD, :]
        other = other_ref[i, 0:HEAD, :]
        both = jnp.where(lead, far[0:1] * mine + other, own[0:1] * other + mine)
        for j in range(4):
            out_ref[4 * i + j, 0:rows, :] = both[j * rows : (j + 1) * rows]
            out_ref[4 * i + j, rows : rows + PAD, :] = own * far
        part = pl.ds(4 * i, 4)
        store = pltpu.make_async_copy(out_ref.at[part], out_hbm.at[part], sems.at[2 + i])
        store.start()
        made.append(store)
    start(made[:2])
    wait(made)


def scan_kernel(reverse, in_ref, out_hbm, out_ref, sems):
    chips, rows = out_ref.shape[0], out_ref.shape[1]
    state = jnp.zeros(out_ref.shape[1:], F32)
    made = []
    for n in reversed(range(chips)) if reverse else range(chips):
        out_ref[n] = state
        state = in_ref[n, rows : rows + 1, :] * state + in_ref[n, 0:rows, :]
    made = copies([(out_ref, out_hbm)], sems)
    start(made)
    wait(made)


def decayed(scores, left, within, column):
    size = scores.shape[1]
    rows = lax.broadcasted_iota(jnp.int32, (HEAD, HEAD), 0)
    cols = lax.broadcasted_iota(jnp.int32, (HEAD, HEAD), 1)
    bands = []
    for at in range(0, scores.shape[0], HEAD):
        band = scores[at : at + HEAD]
        own = column[left + at : left + at + HEAD]
        pieces = []
        before = min(at, size)
        if before:
            edge = within[:, left + at - 1 : left + at]
            grow = jnp.concatenate([jnp.exp(own - edge)] * (before // HEAD), axis=1)
            pieces.append(band[:, :before] * jnp.exp(edge - within[:, left : left + before]) * grow)
        if at < size:
            gap = own - within[:, left + at : left + at + HEAD]
            inside = jnp.where(rows >= cols, jnp.exp(jnp.minimum(gap, 0.0)), 0.0)
            pieces.append(band[:, at : at + HEAD] * inside)
        if at + HEAD < size:
            pieces.append(jnp.zeros((HEAD, size - at - HEAD), F32))
        bands.append(jnp.concatenate(pieces, axis=1).astype(BF16))
    return jnp.concatenate(bands, axis=0)


def inside_kernel(
    within_hbm, q_hbm, k_hbm, v_hbm, probs_hbm, intra_hbm,
    within_ref, q_ref, k_ref, v_ref, probs_ref, intra_ref, sem, in_sems, out_sems,
):
    heads = within_ref.shape[0]
    tokens = q_ref.shape[0]
    size = tokens // 2
    small = copies([(within_hbm, within_ref)], sem)
    start(small)
    loads = [(q_hbm, q_ref, 1), (k_hbm, k_ref, 1), (v_hbm, v_ref, 1)]
    each_head(heads, lambda h: start(head_copies(loads, in_sems, h)))
    wait(small)

    def results(h):
        upper, lower = pl.ds(0, size), pl.ds(size, size)
        pairs = [
            (probs_ref.at[h, upper, upper], probs_hbm.at[h, upper, upper]),
            (probs_ref.at[h, lower], probs_hbm.at[h, lower]),
            (intra_ref.at[:, lanes(h)], intra_hbm.at[:, lanes(h)]),
        ]
        return [pltpu.make_async_copy(a, b, out_sems.at[i, h]) for i, (a, b) in enumerate(pairs)]

    def one(h):
        within = within_ref[pl.ds(h, 1), :]
        column = as_column(within)
        q, k, v = q_ref[:, lanes(h)], k_ref[:, lanes(h)], v_ref[:, lanes(h)]
        early = decayed(dot(q, k[0:size], NT), 0, within, column)
        late = decayed(dot(q[size:], k[size:], NT), size, within, column)
        probs_ref[h, :, 0:size] = early
        probs_ref[h, size:tokens, size:tokens] = late
        intra = dot(early, v[0:size], NN)
        intra_ref[0:size, lanes(h)] = intra[0:size]
        intra_ref[size:tokens, lanes(h)] = intra[size:] + dot(late, v[size:], NN)

    each_pair(heads, lambda h: wait(head_copies(loads, in_sems, h)), one, lambda h: start(results(h)))
    each_head(heads, lambda h: wait(results(h)))


def prepare_kernel(
    within_hbm, q_hbm, gate_hbm, up_hbm, dnorm_hbm, grown_hbm,
    within_ref, q_ref, gate_ref, up_ref, dnorm_ref, grown_ref, sem, in_sems, out_sems,
):
    heads = within_ref.shape[0]
    small = copies([(within_hbm, within_ref)], sem)
    start(small)
    loads = [(q_hbm, q_ref, 1), (gate_hbm, gate_ref, 1), (up_hbm, up_ref, 1)]
    stores = [(dnorm_ref, dnorm_hbm, 1), (grown_ref, grown_hbm, 2)]
    each_head(heads, lambda h: start(head_copies(loads, in_sems, h)))
    wait(small)

    def one(h):
        grow = as_column(jnp.exp(within_ref[pl.ds(h, 1), :]))
        dnorm_ref[:, lanes(h)] = up_ref[:, lanes(h)].astype(F32) * sigmoid(
            gate_ref[:, lanes(h)].astype(F32)
        )
        grown = q_ref[:, lanes(h)].astype(F32) * grow
        grown_ref[:, lanes(h, 2)] = jnp.concatenate(halves(grown), axis=1)

    each_pair(
        heads, lambda h: wait(head_copies(loads, in_sems, h)), one,
        lambda h: start(head_copies(stores, out_sems, h)),
    )
    each_head(heads, lambda h: wait(head_copies(stores, out_sems, h)))


def pick_state(follows, chip_ref, lead_ref, i):
    chip = chip_ref[i]
    return jnp.where(
        follows, lead_ref[i, HEAD : HEAD + 1, :] * chip + lead_ref[i, 0:HEAD, :], chip
    )


def attn_head(core, head, i, at, grown_ref, intra_ref, dnorm_ref, chip_ref, lead_ref, attn_ref, state_ref):
    state = pick_state(core == 1, chip_ref, lead_ref, i)
    state_ref[head] = state
    high, low = halves(state)
    grown = grown_ref[:, lanes(head, 2)]
    attn = intra_ref[:, at] + dot(
        jnp.concatenate([grown, grown[:, :HEAD]], axis=1),
        jnp.concatenate([high, high, low], axis=1),
        NT,
    )
    attn_ref[:, lanes(head)] = attn
    return attn * attn, dnorm_ref[:, lanes(head)] * attn


def attn_mine_kernel(
    core_ref, chip_ref, within_hbm, lead_hbm, grown_hbm, intra_hbm, dnorm_hbm,
    attn_ref, dnorm_ref, grown_ref, state_ref, square_ref, inner_ref, intra_far, within_ref,
    lead_ref, intra_ref, sems,
):
    core = core_ref[0]
    group = chip_ref.shape[0]
    pairs = [(lead_hbm, lead_ref)]
    for half, target in ((core, intra_ref), (1 - core, intra_far)):
        wide, two = half_of(half, group), half_of(half, group, 2)
        pairs += [
            (grown_hbm.at[:, two], grown_ref.at[:, two]),
            (intra_hbm.at[:, wide], target),
            (dnorm_hbm.at[:, wide], dnorm_ref.at[:, wide]),
        ]
    made = copies(pairs + [(within_hbm, within_ref)], sems)
    start(made)
    wait(made[:4])
    square = inner = jnp.zeros(square_ref.shape, F32)
    for i in range(group):
        more = attn_head(
            core, core * group + i, i, slice(i * HEAD, (i + 1) * HEAD), grown_ref, intra_ref,
            dnorm_ref, chip_ref, lead_ref, attn_ref, state_ref,
        )
        square, inner = square + more[0], inner + more[1]
    square_ref[...] = square
    inner_ref[...] = inner
    wait(made[4:])


def attn_other_kernel(
    core_ref, chip_ref, lead_ref, intra_ref, square_ref, inner_ref, dnorm_ref, grown_ref, attn_in, state_in,
    attn_ref, state_ref, sums_ref,
):
    core = core_ref[0]
    group = chip_ref.shape[0]
    square, inner = square_ref[...], inner_ref[...]
    for i in range(group):
        more = attn_head(
            core, (1 - core) * group + i, i, slice(i * HEAD, (i + 1) * HEAD), grown_ref, intra_ref,
            dnorm_ref, chip_ref, lead_ref, attn_ref, state_ref,
        )
        square, inner = square + more[0], inner + more[1]
    ones = jnp.ones((8, HEAD), F32)
    square = dot(ones, square, NT, HIGH)
    inner = dot(ones, inner, NT, HIGH)
    rows = lax.broadcasted_iota(jnp.int32, (8, HEAD), 0)
    packed = jnp.zeros((8, HEAD), F32)
    for i in range(4):
        cols = slice(i * HEAD, (i + 1) * HEAD)
        packed = jnp.where(rows == i, square[:, cols], packed)
        packed = jnp.where(rows == i + 4, inner[:, cols], packed)
    sums_ref[...] = jnp.broadcast_to(packed[None], sums_ref.shape)


def grad_head(head, attn_ref, dnorm_ref, scale_ref, center_ref):
    scale = scale_ref[...]
    normed = attn_ref[:, lanes(head)] * scale
    return (scale * (dnorm_ref[:, lanes(head)] - normed * center_ref[...])).astype(BF16)


def grad_state(head, i, grad, within_ref, grown_ref, out_ref):
    last = within_ref[pl.ds(head, 1), :][:, grad.shape[0] - 1 :]
    put_state(out_ref, i, outer_state(grown_ref[:, lanes(head, 2)], grad), jnp.exp(last))


def grad_other_kernel(
    core_ref, sums_ref, within_ref, grown_ref, attn_ref, dnorm_ref,
    grad_ref, out_ref, scale_ref, center_ref, table_ref,
):
    total = jnp.sum(sums_ref[...], axis=0) / (HEAD_COUNT * HEAD)
    scale = lax.rsqrt(total[0:4] + 1e-06)
    center = scale * total[4:8]
    table_ref[0:4] = scale
    table_ref[4:8] = center
    for i in range(4):
        rows = slice(i * HEAD, (i + 1) * HEAD)
        scale_ref[rows] = as_column(scale[i : i + 1])
        center_ref[rows] = as_column(center[i : i + 1])
    group = out_ref.shape[0]
    for i in range(group):
        head = (1 - core_ref[0]) * group + i
        grad = grad_head(head, attn_ref, dnorm_ref, scale_ref, center_ref)
        grad_ref[:, i * HEAD : (i + 1) * HEAD] = grad
        grad_state(head, i, grad, within_ref, grown_ref, out_ref)


def grad_mine_kernel(
    core_ref, scale_ref, center_ref, table_ref, within_ref, grown_ref, attn_ref, dnorm_ref, grad_far,
    grad_hbm, table_hbm, out_ref, grad_ref, sems, far_sems,
):
    core = core_ref[0]
    group = out_ref.shape[0]
    made = copies(
        [(grad_far, grad_hbm.at[:, half_of(1 - core, group)]), (table_ref, table_hbm)], far_sems
    )
    start(made)
    for i in range(group):
        head = core * group + i
        cols = slice(i * HEAD, (i + 1) * HEAD)
        grad_ref[:, cols] = grad_head(head, attn_ref, dnorm_ref, scale_ref, center_ref)
        store = pltpu.make_async_copy(
            grad_ref.at[:, cols], grad_hbm.at[:, lanes(head)], sems.at[i]
        )
        store.start()
        made.append(store)
    for i in range(group):
        grad = grad_ref[:, i * HEAD : (i + 1) * HEAD]
        grad_state(core * group + i, i, grad, within_ref, grown_ref, out_ref)
    wait(made)


def back_kernel(
    within_hbm, q_hbm, k_hbm, v_hbm, grad_hbm, state_hbm, query_grad_hbm, key_hbm,
    within_ref, q_ref, k_ref, v_ref, grad_ref, state_ref, query_grad_ref, key_ref, sem, in_sems, out_sems,
):
    heads = within_ref.shape[0]
    tokens = q_ref.shape[0]
    size = tokens // 2
    small = copies([(within_hbm, within_ref)], sem)
    start(small)
    loads = [
        (grad_hbm, grad_ref, 1), (v_hbm, v_ref, 1), (k_hbm, k_ref, 1), (q_hbm, q_ref, 1),
        (state_hbm, state_ref, 0),
    ]
    stores = [(query_grad_ref, query_grad_hbm, 1), (key_ref, key_hbm, 1)]
    each_head(heads, lambda h: start(head_copies(loads, in_sems, h)))
    wait(small)

    def one(h):
        within = within_ref[pl.ds(h, 1), :]
        column = as_column(within)
        grow = jnp.exp(column)
        at = lanes(h)
        q, k, v = q_ref[:, at], k_ref[:, at], v_ref[:, at]
        state = jnp.concatenate(halves(state_ref[h]), axis=0)
        grad = grad_ref[:, at]
        early = decayed(dot(grad, v[0:size], NT), 0, within, column)
        late = decayed(dot(grad[size:], v[size:], NT), size, within, column)
        query = dot(early, k[0:size], NN)
        query = jnp.concatenate([query[0:size], query[size:] + dot(late, k[size:], NN)], axis=0)
        inter = dot(jnp.concatenate([grad, grad], axis=1), state, NN)
        query_grad_ref[:, at] = (query + grow * inter).astype(BF16)
        key_ref[0:size, at] = dot(early, q, TN).astype(BF16)
        key_ref[size:tokens, at] = dot(late, q[size:], TN).astype(BF16)

    each_pair(
        heads, lambda h: wait(head_copies(loads, in_sems, h)), one,
        lambda h: start(head_copies(stores, out_sems, h)),
    )
    each_head(heads, lambda h: wait(head_copies(stores, out_sems, h)))


def value_gate_kernel(
    table_hbm, attn_hbm, gate_hbm, up_hbm, grad_hbm, probs_hbm, value_hbm, output_hbm, gate_grad_hbm,
    table_ref, attn_ref, gate_ref, up_ref, grad_ref, probs_ref, value_ref, output_ref, gate_grad_ref,
    scale_ref, sem, in_sems, out_sems,
):
    heads = probs_ref.shape[0]
    tokens = grad_ref.shape[0]
    size = tokens // 2
    small = copies([(table_hbm, table_ref)], sem)
    start(small)

    def loads(h):
        upper, lower = pl.ds(0, size), pl.ds(size, size)
        pairs = [
            (probs_hbm.at[h, upper, upper], probs_ref.at[h, upper, upper]),
            (probs_hbm.at[h, lower], probs_ref.at[h, lower]),
        ]
        pairs += [
            (a.at[:, lanes(h)], b.at[:, lanes(h)])
            for a, b in (
                (grad_hbm, grad_ref), (attn_hbm, attn_ref), (gate_hbm, gate_ref), (up_hbm, up_ref)
            )
        ]
        return [pltpu.make_async_copy(a, b, in_sems.at[i, h]) for i, (a, b) in enumerate(pairs)]

    stores = [(value_ref, value_hbm, 1), (output_ref, output_hbm, 1), (gate_grad_ref, gate_grad_hbm, 1)]
    each_head(heads, lambda h: start(loads(h)))
    wait(small)
    for i in range(4):
        scale_ref[i * HEAD : (i + 1) * HEAD] = as_column(table_ref[i : i + 1])

    def one(h):
        at = lanes(h)
        early = dot(probs_ref[h, :, 0:size], grad_ref[:, at], TN)
        late = dot(probs_ref[h, size:tokens, size:tokens], grad_ref[size:tokens, at], TN)
        normed = attn_ref[:, at] * scale_ref[...]
        sig = sigmoid(gate_ref[:, at].astype(F32))
        output_ref[:, at] = (normed * sig).astype(BF16)
        gate_grad_ref[:, at] = (up_ref[:, at].astype(F32) * normed * sig * (1.0 - sig)).astype(BF16)
        value_ref[0:size, at] = early.astype(BF16)
        value_ref[size:tokens, at] = late.astype(BF16)

    each_pair(
        heads, lambda h: wait(loads(h)), one, lambda h: start(head_copies(stores, out_sems, h))
    )
    each_head(heads, lambda h: wait(head_copies(stores, out_sems, h)))


def final_head(core, head, i, within_ref, k_ref, v_ref, key_part_ref, value_part_ref, chip_ref, lead_ref):
    tokens = k_ref.shape[0]
    at = slice(i * HEAD, (i + 1) * HEAD)
    state = halves(pick_state(core == 0, chip_ref, lead_ref, i))
    within = within_ref[pl.ds(head, 1), :]
    tail = as_column(jnp.exp(within[:, tokens - 1 :] - within))
    k, v = k_ref[:, at], v_ref[:, at]
    key_inter = dot(jnp.concatenate([v, v], axis=1), jnp.concatenate(state, axis=0), NN)
    value_inter = dot(jnp.concatenate([k, k], axis=1), jnp.concatenate(state, axis=1), NT)
    return (
        (key_part_ref[:, at].astype(F32) + tail * key_inter).astype(BF16),
        (value_part_ref[:, at].astype(F32) + tail * value_inter).astype(BF16),
    )


def final_mine_kernel(
    core_ref, chip_ref, within_hbm, lead_hbm, k_hbm, v_hbm, key_part_hbm, value_part_hbm,
    key_grad_ref, value_grad_ref, k_far, v_far, key_part_far, value_part_far, within_ref,
    lead_ref, k_ref, v_ref, key_part_ref, value_part_ref, sems,
):
    core = core_ref[0]
    group = chip_ref.shape[0]
    sources = (k_hbm, v_hbm, key_part_hbm, value_part_hbm)
    near, far = half_of(core, group), half_of(1 - core, group)
    pairs = [(within_hbm, within_ref), (lead_hbm, lead_ref)]
    pairs += [(a.at[:, near], b) for a, b in zip(sources, (k_ref, v_ref, key_part_ref, value_part_ref))]
    pairs += [(a.at[:, far], b) for a, b in zip(sources, (k_far, v_far, key_part_far, value_part_far))]
    made = copies(pairs, sems)
    start(made)
    wait(made[:6])
    for i in range(group):
        cols = slice(i * HEAD, (i + 1) * HEAD)
        key_grad_ref[:, cols], value_grad_ref[:, cols] = final_head(
            core, core * group + i, i, within_ref, k_ref, v_ref, key_part_ref, value_part_ref,
            chip_ref, lead_ref,
        )
    wait(made[6:])


def final_other_kernel(
    core_ref, chip_ref, lead_ref, within_ref, k_ref, v_ref, key_part_ref, value_part_ref, key_near, value_near,
    key_grad_hbm, value_grad_hbm, key_grad_ref, value_grad_ref, near_sems, sems,
):
    core = core_ref[0]
    group = chip_ref.shape[0]
    near = half_of(core, group)
    made = copies(
        [(key_near, key_grad_hbm.at[:, near]), (value_near, value_grad_hbm.at[:, near])], near_sems
    )
    start(made)
    for i in range(group):
        cols = slice(i * HEAD, (i + 1) * HEAD)
        head = (1 - core) * group + i
        key_grad_ref[:, cols], value_grad_ref[:, cols] = final_head(
            core, head, i, within_ref, k_ref, v_ref, key_part_ref, value_part_ref, chip_ref, lead_ref
        )
        stores = [
            pltpu.make_async_copy(a.at[:, cols], b.at[:, lanes(head)], sems.at[j, i])
            for j, (a, b) in enumerate(((key_grad_ref, key_grad_hbm), (value_grad_ref, value_grad_hbm)))
        ]
        start(stores)
        made = made + stores
    wait(made)


def shape(dims, dtype=F32):
    return jax.ShapeDtypeStruct(dims, dtype)


def swap(x):
    return lax.ppermute(x, "c", [(0, 1), (1, 0)])


def spread(x):
    return lax.all_to_all(x, CHIPS, split_axis=0, concat_axis=0, tiled=True)


def call(kernel, name, near, far, near_out, far_out, buffers, sems, core=None, aliases=(), mib=16):
    scalars = () if core is None else (core,)
    vmem = pl.BlockSpec(memory_space=pltpu.VMEM)
    hbm = pl.BlockSpec(memory_space=pl.ANY)
    return pl.pallas_call(
        kernel,
        grid_spec=pltpu.PrefetchScalarGridSpec(
            num_scalar_prefetch=len(scalars),
            grid=(1,),
            in_specs=[vmem] * len(near) + [hbm] * len(far),
            out_specs=[hbm] * len(far_out) + [vmem] * len(near_out),
            scratch_shapes=[pltpu.VMEM(x.shape, x.dtype) for x in buffers]
            + [pltpu.SemaphoreType.DMA(dims) for dims in sems],
        ),
        out_shape=[pltpu.HBM(x.shape, x.dtype) for x in far_out]
        + [pltpu.VMEM(x.shape, x.dtype) for x in near_out],
        input_output_aliases=dict(aliases),
        compiler_params=pltpu.CompilerParams(
            dimension_semantics=("arbitrary",), vmem_limit_bytes=mib * 2**20
        ),
        name=name,
    )(*scalars, *near, *(pltpu.with_memory_space_constraint(x, pltpu.HBM) for x in far))


def shards(queries, keys, values, gate, log_decay, out_grad):
    tokens, flat = queries.shape
    heads = log_decay.shape[1]
    group = heads // 2
    chips = lax.axis_size("x") * lax.axis_size("y")
    rows = group * HEAD // chips
    core = lax.axis_index("c").astype(jnp.int32).reshape(1)
    packed = shape((group, HEAD + PAD, HEAD))
    sliced = shape((chips, rows, HEAD))
    carried = shape((chips, rows + PAD, HEAD))
    wide = shape((tokens, flat))
    narrow = shape((tokens, flat), BF16)
    double = shape((tokens, 2 * flat), BF16)
    half = shape((tokens, flat // 2))
    half_narrow = shape((tokens, flat // 2), BF16)
    column = shape((tokens, HEAD))
    states = shape((heads, HEAD, HEAD))
    table_rows = shape((8, HEAD))
    sums_rows = shape((8, 8, HEAD))
    rates = shape((heads, tokens))
    table_of = shape((heads, tokens, tokens), BF16)

    def combined(lead, mine, other):
        return call(
            combine_kernel, "combine", (mine, other), (), (), (carried, packed, packed), (carried,), ((2 + group,),),
            lead,
        )

    def scanned(x, reverse):
        (out,) = call(
            lambda *refs: scan_kernel(reverse, *refs), "scan", (x,), (), (), (sliced,), (sliced,), ((1,),)
        )
        return out

    within, theirs, k_near, v_near = call(
        local_other_kernel, "local_other", (), (log_decay.T, keys, values),
        (rates, packed, half_narrow, half_narrow), (), (rates, half_narrow, half_narrow), ((5,),), core,
    )
    lead_mine = swap(theirs)
    (mine,) = call(
        local_mine_kernel, "local_mine", (within, k_near, v_near), (), (packed,), (), (), (), core
    )
    chip_state, mine, lead_mine = combined(1 - core, mine, lead_mine)
    chip_state = spread(chip_state)
    probs, intra = call(
        inside_kernel, "inside", (), (within, queries, keys, values), (), (table_of, wide),
        (rates, narrow, narrow, narrow, table_of, wide), ((1,), (3, heads), (3, heads)),
    )
    chip_state, probs, intra, mine, within = lax.optimization_barrier(
        (chip_state, probs, intra, mine, within)
    )
    chip_state, within = lax.optimization_barrier((scanned(chip_state, False), within))
    chip_mine = spread(chip_state)
    dnorm, grown = call(
        prepare_kernel, "prepare", (), (within, queries, gate, out_grad), (), (wide, double),
        (rates, narrow, narrow, narrow, wide, double), ((1,), (3, heads), (2, heads)),
    )
    chip_mine, mine, dnorm, grown = lax.optimization_barrier((chip_mine, mine, dnorm, grown))
    chip_mine = chip_mine.reshape(group, HEAD, HEAD)
    chip_other, lead_other = swap(chip_mine), swap(mine)
    attn, dnorm, grown, state, square, inner, intra_far, within_near = call(
        attn_mine_kernel, "attn_mine", (chip_mine,), (within, lead_mine, grown, intra, dnorm),
        (wide, wide, double, states, column, column, half, rates), (), (packed, half), ((8,),), core,
    )
    attn, state, sums = call(
        attn_other_kernel, "attn_other",
        (chip_other, lead_other, intra_far, square, inner, dnorm, grown, attn, state), (),
        (wide, states, sums_rows), (), (), (), core, {8: 0, 9: 1},
    )
    sums = lax.all_to_all(sums, "tp", split_axis=0, concat_axis=0, tiled=True)
    grad_far, theirs, scale, center, table = call(
        grad_other_kernel, "grad_other", (sums, within_near, grown, attn, dnorm), (),
        (half_narrow, packed, column, column, table_rows), (), (), (), core,
    )
    lead_mine = swap(theirs)
    grad, table, mine = call(
        grad_mine_kernel, "grad_mine",
        (scale, center, table, within_near, grown, attn, dnorm, grad_far), (),
        (packed,), (narrow, table_rows), (half_narrow,), ((group,), (2,)), core,
    )
    chip_state, mine, lead_mine = combined(core, mine, lead_mine)
    chip_state = spread(chip_state)
    query_grad, key_part = call(
        back_kernel, "back", (), (within, queries, keys, values, grad, state), (), (narrow, narrow),
        (rates, narrow, narrow, narrow, narrow, states, narrow, narrow), ((1,), (5, heads), (2, heads)),
    )
    chip_state, key_part, mine, grad, table = lax.optimization_barrier(
        (chip_state, key_part, mine, grad, table)
    )
    chip_state, grad, table = lax.optimization_barrier((scanned(chip_state, True), grad, table))
    chip_mine = spread(chip_state)
    value_part, output, gate_grad = call(
        value_gate_kernel, "value_gate", (), (table, attn, gate, out_grad, grad, probs), (), (narrow, narrow, narrow),
        (table_rows, wide, narrow, narrow, narrow, table_of, narrow, narrow, narrow, column),
        ((1,), (6, heads), (3, heads)), mib=24,
    )
    chip_mine, value_part, output, gate_grad, mine = lax.optimization_barrier(
        (chip_mine, value_part, output, gate_grad, mine)
    )
    chip_mine = chip_mine.reshape(group, HEAD, HEAD)
    chip_other, lead_other = swap(chip_mine), swap(mine)
    key_near, value_near, *far, within_near = call(
        final_mine_kernel, "final_mine", (chip_mine,), (within, lead_mine, keys, values, key_part, value_part),
        (half_narrow,) * 6 + (rates,), (), (packed,) + (half_narrow,) * 4, ((10,),), core,
    )
    key_grad, value_grad = call(
        final_other_kernel, "final_other", (chip_other, lead_other, within_near, *far, key_near, value_near), (),
        (), (narrow, narrow), (half_narrow, half_narrow), ((2,), (2, group)), core,
    )
    return output, query_grad, key_grad, value_grad, gate_grad


def solution(mesh):
    split = Mesh(mesh.devices.reshape(4, 4, 2, mesh.shape["tp"]), ("x", "y", "c", "tp"))
    return jax.shard_map(
        shards,
        mesh=split,
        in_specs=(P(SEQ, "tp"),) * 6,
        out_specs=(P(SEQ, "tp"),) * 5,
        check_vma=False,
    )
```

```python
import jax
import jax.numpy as jnp
from jax import lax
from jax.experimental import pallas as pl
from jax.experimental.pallas import tpu as pltpu
from jax.sharding import Mesh
from jax.sharding import PartitionSpec as P

HEAD_COUNT = 64
HEAD = 128
SEQ = ("x", "y", "c")
CHIPS = ("x", "y")
HIGH = lax.Precision.HIGHEST
F32 = jnp.float32
BF16 = jnp.bfloat16
PAD = 8

NN = (((1,), (0,)), ((), ()))
NT = (((1,), (1,)), ((), ()))
TN = (((0,), (0,)), ((), ()))


def dot(a, b, dims, precision=None):
    return lax.dot_general(a, b, dims, precision=precision, preferred_element_type=F32)


def halves(x):
    high = x.astype(BF16)
    return high, (x - high.astype(F32)).astype(BF16)


def as_column(row):
    return jnp.transpose(jnp.broadcast_to(row, (HEAD, row.shape[1])))


def sigmoid(x):
    return 1.0 / (1.0 + jnp.exp(-x))


def lanes(head, count=1):
    return pl.ds(pl.multiple_of(head * (count * HEAD), HEAD), count * HEAD)


def put_state(ref, i, state, factor):
    ref[i, 0:HEAD, :] = state
    ref[i, HEAD : HEAD + PAD, :] = jnp.broadcast_to(factor, (PAD, HEAD))


def outer_state(wide, narrow):
    both = dot(narrow, wide, TN)
    return both[:, :HEAD] + both[:, HEAD:]


def sum_over(rate_ref, within_ref, rate_copy):
    heads, tokens = rate_ref.shape
    early = lax.broadcasted_iota(jnp.int32, (tokens, tokens), 0)
    late = lax.broadcasted_iota(jnp.int32, (tokens, tokens), 1)
    upto = (early <= late).astype(F32).astype(BF16)
    rate_copy.wait()
    rate = rate_ref[...]
    high, rest = halves(rate)
    low = (rate - high.astype(F32) - rest.astype(F32)).astype(BF16)
    parts = jnp.concatenate([x.astype(F32) for x in (high, rest, low)], axis=0).astype(BF16)
    sums = dot(parts, upto, NN)
    within_ref[...] = sums[0:heads] + sums[heads : 2 * heads] + sums[2 * heads :]


def half_of(half, group, count=1):
    width = group * count * HEAD
    return pl.ds(pl.multiple_of(half * width, HEAD), width)


def copies(pairs, sems):
    return [pltpu.make_async_copy(a, b, sems.at[i]) for i, (a, b) in enumerate(pairs)]


def start(group):
    for copy in group:
        copy.start()


def wait(group):
    for copy in group:
        copy.wait()


def each_head(heads, body):
    def step(head, carry):
        body(head)
        return carry

    lax.fori_loop(0, heads, step, 0)


def each_pair(heads, before, work, after):
    def step(pair, carry):
        both = (2 * pair, 2 * pair + 1)
        for stage in (before, work, after):
            for head in both:
                stage(head)
        return carry

    lax.fori_loop(0, heads // 2, step, 0)


def head_copies(arrays, sems, head):
    made = []
    for i, (a, b, count) in enumerate(arrays):
        at = (head,) if count == 0 else (slice(None), lanes(head, count))
        made.append(pltpu.make_async_copy(a.at[at], b.at[at], sems.at[i, head]))
    return made


def local_state(head, cols, within_ref, k_ref, v_ref, out_ref, i):
    tokens = k_ref.shape[0]
    within = within_ref[pl.ds(head, 1), :]
    last = within[:, tokens - 1 :]
    tail = as_column(jnp.exp(last - within))
    scaled = jnp.concatenate(halves(k_ref[:, cols].astype(F32) * tail), axis=1)
    put_state(out_ref, i, outer_state(scaled, v_ref[:, cols]), jnp.exp(last))


def local_other_kernel(
    core_ref, rate_hbm, k_hbm, v_hbm, within_ref, out_ref, k_near, v_near, rate_ref, k_ref, v_ref, sems
):
    group = out_ref.shape[0]
    core = core_ref[0]
    far, near = half_of(1 - core, group), half_of(core, group)
    made = copies(
        [
            (rate_hbm, rate_ref),
            (v_hbm.at[:, far], v_ref),
            (k_hbm.at[:, far], k_ref),
            (v_hbm.at[:, near], v_near),
            (k_hbm.at[:, near], k_near),
        ],
        sems,
    )
    start(made)
    sum_over(rate_ref, within_ref, made[0])
    wait(made[1:3])
    for i in range(group):
        cols = slice(i * HEAD, (i + 1) * HEAD)
        local_state((1 - core) * group + i, cols, within_ref, k_ref, v_ref, out_ref, i)
    wait(made[3:])


def local_mine_kernel(core_ref, within_ref, k_ref, v_ref, out_ref):
    group = out_ref.shape[0]
    for i in range(group):
        cols = slice(i * HEAD, (i + 1) * HEAD)
        local_state(core_ref[0] * group + i, cols, within_ref, k_ref, v_ref, out_ref, i)


def combine_kernel(
    lead_ref, mine_ref, other_ref, out_hbm, mine_hbm, other_hbm, out_ref, sems
):
    group = mine_ref.shape[0]
    made = copies([(mine_ref, mine_hbm), (other_ref, other_hbm)], sems)
    lead = lead_ref[0] == 1
    rows = HEAD // 4
    for i in range(group):
        own = mine_ref[i, HEAD : HEAD + PAD, :]
        far = other_ref[i, HEAD : HEAD + PAD, :]
        mine = mine_ref[i, 0:HEAD, :]
        other = other_ref[i, 0:HEAD, :]
        both = jnp.where(lead, far[0:1] * mine + other, own[0:1] * other + mine)
        for j in range(4):
            out_ref[4 * i + j, 0:rows, :] = both[j * rows : (j + 1) * rows]
            out_ref[4 * i + j, rows : rows + PAD, :] = own * far
        part = pl.ds(4 * i, 4)
        store = pltpu.make_async_copy(out_ref.at[part], out_hbm.at[part], sems.at[2 + i])
        store.start()
        made.append(store)
    start(made[:2])
    wait(made)


def scan_kernel(reverse, in_ref, out_hbm, out_ref, sems):
    chips, rows = out_ref.shape[0], out_ref.shape[1]
    state = jnp.zeros(out_ref.shape[1:], F32)
    made = []
    for n in reversed(range(chips)) if reverse else range(chips):
        out_ref[n] = state
        state = in_ref[n, rows : rows + 1, :] * state + in_ref[n, 0:rows, :]
    made = copies([(out_ref, out_hbm)], sems)
    start(made)
    wait(made)


def decayed(scores, left, within, column):
    size = scores.shape[1]
    rows = lax.broadcasted_iota(jnp.int32, (HEAD, HEAD), 0)
    cols = lax.broadcasted_iota(jnp.int32, (HEAD, HEAD), 1)
    bands = []
    for at in range(0, scores.shape[0], HEAD):
        band = scores[at : at + HEAD]
        own = column[left + at : left + at + HEAD]
        pieces = []
        before = min(at, size)
        if before:
            edge = within[:, left + at - 1 : left + at]
            grow = jnp.concatenate([jnp.exp(own - edge)] * (before // HEAD), axis=1)
            pieces.append(band[:, :before] * jnp.exp(edge - within[:, left : left + before]) * grow)
        if at < size:
            gap = own - within[:, left + at : left + at + HEAD]
            inside = jnp.where(rows >= cols, jnp.exp(jnp.minimum(gap, 0.0)), 0.0)
            pieces.append(band[:, at : at + HEAD] * inside)
        if at + HEAD < size:
            pieces.append(jnp.zeros((HEAD, size - at - HEAD), F32))
        bands.append(jnp.concatenate(pieces, axis=1).astype(BF16))
    return jnp.concatenate(bands, axis=0)


def inside_kernel(
    within_hbm, q_hbm, k_hbm, v_hbm, probs_hbm, intra_hbm,
    within_ref, q_ref, k_ref, v_ref, probs_ref, intra_ref, sem, in_sems, out_sems,
):
    heads = within_ref.shape[0]
    tokens = q_ref.shape[0]
    size = tokens // 2
    small = copies([(within_hbm, within_ref)], sem)
    start(small)
    loads = [(q_hbm, q_ref, 1), (k_hbm, k_ref, 1), (v_hbm, v_ref, 1)]
    each_head(heads, lambda h: start(head_copies(loads, in_sems, h)))
    wait(small)

    def results(h):
        upper, lower = pl.ds(0, size), pl.ds(size, size)
        pairs = [
            (probs_ref.at[h, upper, upper], probs_hbm.at[h, upper, upper]),
            (probs_ref.at[h, lower], probs_hbm.at[h, lower]),
            (intra_ref.at[:, lanes(h)], intra_hbm.at[:, lanes(h)]),
        ]
        return [pltpu.make_async_copy(a, b, out_sems.at[i, h]) for i, (a, b) in enumerate(pairs)]

    def one(h):
        within = within_ref[pl.ds(h, 1), :]
        column = as_column(within)
        q, k, v = q_ref[:, lanes(h)], k_ref[:, lanes(h)], v_ref[:, lanes(h)]
        early = decayed(dot(q, k[0:size], NT), 0, within, column)
        late = decayed(dot(q[size:], k[size:], NT), size, within, column)
        probs_ref[h, :, 0:size] = early
        probs_ref[h, size:tokens, size:tokens] = late
        intra = dot(early, v[0:size], NN)
        intra_ref[0:size, lanes(h)] = intra[0:size]
        intra_ref[size:tokens, lanes(h)] = intra[size:] + dot(late, v[size:], NN)

    each_pair(heads, lambda h: wait(head_copies(loads, in_sems, h)), one, lambda h: start(results(h)))
    each_head(heads, lambda h: wait(results(h)))


def prepare_kernel(
    within_hbm, q_hbm, gate_hbm, up_hbm, dnorm_hbm, grown_hbm,
    within_ref, q_ref, gate_ref, up_ref, dnorm_ref, grown_ref, sem, in_sems, out_sems,
):
    heads = within_ref.shape[0]
    small = copies([(within_hbm, within_ref)], sem)
    start(small)
    loads = [(q_hbm, q_ref, 1), (gate_hbm, gate_ref, 1), (up_hbm, up_ref, 1)]
    stores = [(dnorm_ref, dnorm_hbm, 1), (grown_ref, grown_hbm, 2)]
    each_head(heads, lambda h: start(head_copies(loads, in_sems, h)))
    wait(small)

    def one(h):
        grow = as_column(jnp.exp(within_ref[pl.ds(h, 1), :]))
        dnorm_ref[:, lanes(h)] = up_ref[:, lanes(h)].astype(F32) * sigmoid(
            gate_ref[:, lanes(h)].astype(F32)
        )
        grown = q_ref[:, lanes(h)].astype(F32) * grow
        grown_ref[:, lanes(h, 2)] = jnp.concatenate(halves(grown), axis=1)

    each_pair(
        heads, lambda h: wait(head_copies(loads, in_sems, h)), one,
        lambda h: start(head_copies(stores, out_sems, h)),
    )
    each_head(heads, lambda h: wait(head_copies(stores, out_sems, h)))


def pick_state(follows, chip_ref, lead_ref, i):
    chip = chip_ref[i]
    return jnp.where(
        follows, lead_ref[i, HEAD : HEAD + 1, :] * chip + lead_ref[i, 0:HEAD, :], chip
    )


def attn_head(core, head, i, at, grown_ref, intra_ref, dnorm_ref, chip_ref, lead_ref, attn_ref, state_ref):
    state = pick_state(core == 1, chip_ref, lead_ref, i)
    state_ref[head] = state
    high, low = halves(state)
    grown = grown_ref[:, lanes(head, 2)]
    attn = intra_ref[:, at] + dot(
        jnp.concatenate([grown, grown[:, :HEAD]], axis=1),
        jnp.concatenate([high, high, low], axis=1),
        NT,
    )
    attn_ref[:, lanes(head)] = attn
    return attn * attn, dnorm_ref[:, lanes(head)] * attn


def attn_mine_kernel(
    core_ref, chip_ref, within_hbm, lead_hbm, grown_hbm, intra_hbm, dnorm_hbm,
    attn_ref, dnorm_ref, grown_ref, state_ref, square_ref, inner_ref, intra_far, within_ref,
    lead_ref, intra_ref, sems,
):
    core = core_ref[0]
    group = chip_ref.shape[0]
    pairs = [(lead_hbm, lead_ref)]
    for half, target in ((core, intra_ref), (1 - core, intra_far)):
        wide, two = half_of(half, group), half_of(half, group, 2)
        pairs += [
            (grown_hbm.at[:, two], grown_ref.at[:, two]),
            (intra_hbm.at[:, wide], target),
            (dnorm_hbm.at[:, wide], dnorm_ref.at[:, wide]),
        ]
    made = copies(pairs + [(within_hbm, within_ref)], sems)
    start(made)
    wait(made[:4])
    square = inner = jnp.zeros(square_ref.shape, F32)
    for i in range(group):
        more = attn_head(
            core, core * group + i, i, slice(i * HEAD, (i + 1) * HEAD), grown_ref, intra_ref,
            dnorm_ref, chip_ref, lead_ref, attn_ref, state_ref,
        )
        square, inner = square + more[0], inner + more[1]
    square_ref[...] = square
    inner_ref[...] = inner
    wait(made[4:])


def attn_other_kernel(
    core_ref, chip_ref, lead_ref, intra_ref, square_ref, inner_ref, dnorm_ref, grown_ref, attn_in, state_in,
    attn_ref, state_ref, sums_ref,
):
    core = core_ref[0]
    group = chip_ref.shape[0]
    square, inner = square_ref[...], inner_ref[...]
    for i in range(group):
        more = attn_head(
            core, (1 - core) * group + i, i, slice(i * HEAD, (i + 1) * HEAD), grown_ref, intra_ref,
            dnorm_ref, chip_ref, lead_ref, attn_ref, state_ref,
        )
        square, inner = square + more[0], inner + more[1]
    ones = jnp.ones((8, HEAD), F32)
    square = dot(ones, square, NT, HIGH)
    inner = dot(ones, inner, NT, HIGH)
    rows = lax.broadcasted_iota(jnp.int32, (8, HEAD), 0)
    packed = jnp.zeros((8, HEAD), F32)
    for i in range(4):
        cols = slice(i * HEAD, (i + 1) * HEAD)
        packed = jnp.where(rows == i, square[:, cols], packed)
        packed = jnp.where(rows == i + 4, inner[:, cols], packed)
    sums_ref[...] = jnp.broadcast_to(packed[None], sums_ref.shape)


def grad_head(head, attn_ref, dnorm_ref, scale_ref, center_ref):
    scale = scale_ref[...]
    normed = attn_ref[:, lanes(head)] * scale
    return (scale * (dnorm_ref[:, lanes(head)] - normed * center_ref[...])).astype(BF16)


def grad_state(head, i, grad, within_ref, grown_ref, out_ref):
    last = within_ref[pl.ds(head, 1), :][:, grad.shape[0] - 1 :]
    put_state(out_ref, i, outer_state(grown_ref[:, lanes(head, 2)], grad), jnp.exp(last))


def grad_other_kernel(
    core_ref, sums_ref, within_ref, grown_ref, attn_ref, dnorm_ref,
    grad_ref, out_ref, scale_ref, center_ref, table_ref,
):
    total = jnp.sum(sums_ref[...], axis=0) / (HEAD_COUNT * HEAD)
    scale = lax.rsqrt(total[0:4] + 1e-06)
    center = scale * total[4:8]
    table_ref[0:4] = scale
    table_ref[4:8] = center
    for i in range(4):
        rows = slice(i * HEAD, (i + 1) * HEAD)
        scale_ref[rows] = as_column(scale[i : i + 1])
        center_ref[rows] = as_column(center[i : i + 1])
    group = out_ref.shape[0]
    for i in range(group):
        head = (1 - core_ref[0]) * group + i
        grad = grad_head(head, attn_ref, dnorm_ref, scale_ref, center_ref)
        grad_ref[:, i * HEAD : (i + 1) * HEAD] = grad
        grad_state(head, i, grad, within_ref, grown_ref, out_ref)


def grad_mine_kernel(
    core_ref, scale_ref, center_ref, table_ref, within_ref, grown_ref, attn_ref, dnorm_ref, grad_far,
    grad_hbm, table_hbm, out_ref, grad_ref, sems, far_sems,
):
    core = core_ref[0]
    group = out_ref.shape[0]
    made = copies(
        [(grad_far, grad_hbm.at[:, half_of(1 - core, group)]), (table_ref, table_hbm)], far_sems
    )
    start(made)
    for i in range(group):
        head = core * group + i
        cols = slice(i * HEAD, (i + 1) * HEAD)
        grad_ref[:, cols] = grad_head(head, attn_ref, dnorm_ref, scale_ref, center_ref)
        store = pltpu.make_async_copy(
            grad_ref.at[:, cols], grad_hbm.at[:, lanes(head)], sems.at[i]
        )
        store.start()
        made.append(store)
    for i in range(group):
        grad = grad_ref[:, i * HEAD : (i + 1) * HEAD]
        grad_state(core * group + i, i, grad, within_ref, grown_ref, out_ref)
    wait(made)


def back_kernel(
    within_hbm, q_hbm, k_hbm, v_hbm, grad_hbm, state_hbm, query_grad_hbm, key_ref,
    within_ref, q_ref, k_ref, v_ref, grad_ref, state_ref, query_grad_ref, sem, in_sems, out_sems,
):
    heads = within_ref.shape[0]
    tokens = q_ref.shape[0]
    size = tokens // 2
    small = copies([(within_hbm, within_ref)], sem)
    start(small)
    loads = [
        (grad_hbm, grad_ref, 1), (v_hbm, v_ref, 1), (k_hbm, k_ref, 1), (q_hbm, q_ref, 1),
        (state_hbm, state_ref, 0),
    ]
    stores = [(query_grad_ref, query_grad_hbm, 1)]
    each_head(heads, lambda h: start(head_copies(loads, in_sems, h)))
    wait(small)

    def one(h):
        within = within_ref[pl.ds(h, 1), :]
        column = as_column(within)
        grow = jnp.exp(column)
        at = lanes(h)
        q, k, v = q_ref[:, at], k_ref[:, at], v_ref[:, at]
        state = jnp.concatenate(halves(state_ref[h]), axis=0)
        grad = grad_ref[:, at]
        early = decayed(dot(grad, v[0:size], NT), 0, within, column)
        late = decayed(dot(grad[size:], v[size:], NT), size, within, column)
        query = dot(early, k[0:size], NN)
        query = jnp.concatenate([query[0:size], query[size:] + dot(late, k[size:], NN)], axis=0)
        inter = dot(jnp.concatenate([grad, grad], axis=1), state, NN)
        query_grad_ref[:, at] = (query + grow * inter).astype(BF16)
        key_ref[0:size, at] = dot(early, q, TN).astype(BF16)
        key_ref[size:tokens, at] = dot(late, q[size:], TN).astype(BF16)

    each_pair(
        heads, lambda h: wait(head_copies(loads, in_sems, h)), one,
        lambda h: start(head_copies(stores, out_sems, h)),
    )
    each_head(heads, lambda h: wait(head_copies(stores, out_sems, h)))


def value_gate_kernel(
    table_hbm, attn_hbm, gate_hbm, up_hbm, grad_hbm, probs_hbm, output_hbm, gate_grad_hbm, value_ref,
    table_ref, attn_ref, gate_ref, up_ref, grad_ref, probs_ref, output_ref, gate_grad_ref,
    scale_ref, sem, in_sems, out_sems,
):
    heads = probs_ref.shape[0]
    tokens = grad_ref.shape[0]
    size = tokens // 2
    small = copies([(table_hbm, table_ref)], sem)
    start(small)

    def loads(h):
        upper, lower = pl.ds(0, size), pl.ds(size, size)
        pairs = [
            (probs_hbm.at[h, upper, upper], probs_ref.at[h, upper, upper]),
            (probs_hbm.at[h, lower], probs_ref.at[h, lower]),
        ]
        pairs += [
            (a.at[:, lanes(h)], b.at[:, lanes(h)])
            for a, b in (
                (grad_hbm, grad_ref), (attn_hbm, attn_ref), (gate_hbm, gate_ref), (up_hbm, up_ref)
            )
        ]
        return [pltpu.make_async_copy(a, b, in_sems.at[i, h]) for i, (a, b) in enumerate(pairs)]

    stores = [(output_ref, output_hbm, 1), (gate_grad_ref, gate_grad_hbm, 1)]
    each_head(heads, lambda h: start(loads(h)))
    wait(small)
    for i in range(4):
        scale_ref[i * HEAD : (i + 1) * HEAD] = as_column(table_ref[i : i + 1])

    def one(h):
        at = lanes(h)
        early = dot(probs_ref[h, :, 0:size], grad_ref[:, at], TN)
        late = dot(probs_ref[h, size:tokens, size:tokens], grad_ref[size:tokens, at], TN)
        normed = attn_ref[:, at] * scale_ref[...]
        sig = sigmoid(gate_ref[:, at].astype(F32))
        output_ref[:, at] = (normed * sig).astype(BF16)
        gate_grad_ref[:, at] = (up_ref[:, at].astype(F32) * normed * sig * (1.0 - sig)).astype(BF16)
        value_ref[0:size, at] = early.astype(BF16)
        value_ref[size:tokens, at] = late.astype(BF16)

    each_pair(
        heads, lambda h: wait(loads(h)), one, lambda h: start(head_copies(stores, out_sems, h))
    )
    each_head(heads, lambda h: wait(head_copies(stores, out_sems, h)))


def final_head(core, head, i, within_ref, k_ref, v_ref, key_part_ref, value_part_ref, chip_ref, lead_ref):
    tokens = k_ref.shape[0]
    at = slice(i * HEAD, (i + 1) * HEAD)
    own = lanes(head)
    state = halves(pick_state(core == 0, chip_ref, lead_ref, i))
    within = within_ref[pl.ds(head, 1), :]
    tail = as_column(jnp.exp(within[:, tokens - 1 :] - within))
    k, v = k_ref[:, at], v_ref[:, at]
    key_inter = dot(jnp.concatenate([v, v], axis=1), jnp.concatenate(state, axis=0), NN)
    value_inter = dot(jnp.concatenate([k, k], axis=1), jnp.concatenate(state, axis=1), NT)
    return (
        (key_part_ref[:, own].astype(F32) + tail * key_inter).astype(BF16),
        (value_part_ref[:, own].astype(F32) + tail * value_inter).astype(BF16),
    )


def final_mine_kernel(
    core_ref, chip_ref, key_part_ref, value_part_ref, within_hbm, lead_hbm, k_hbm, v_hbm,
    key_grad_ref, value_grad_ref, k_far, v_far, within_ref, lead_ref, k_ref, v_ref, sems,
):
    core = core_ref[0]
    group = chip_ref.shape[0]
    near, far = half_of(core, group), half_of(1 - core, group)
    pairs = [(within_hbm, within_ref), (lead_hbm, lead_ref)]
    pairs += [(v_hbm.at[:, near], v_ref), (k_hbm.at[:, near], k_ref)]
    pairs += [(v_hbm.at[:, far], v_far), (k_hbm.at[:, far], k_far)]
    made = copies(pairs, sems)
    start(made)
    wait(made[:4])
    for i in range(group):
        cols = slice(i * HEAD, (i + 1) * HEAD)
        key_grad_ref[:, cols], value_grad_ref[:, cols] = final_head(
            core, core * group + i, i, within_ref, k_ref, v_ref, key_part_ref, value_part_ref,
            chip_ref, lead_ref,
        )
    wait(made[4:])


def final_other_kernel(
    core_ref, chip_ref, lead_ref, within_ref, k_ref, v_ref, key_part_ref, value_part_ref, key_near, value_near,
    key_grad_hbm, value_grad_hbm, key_grad_ref, value_grad_ref, near_sems, sems,
):
    core = core_ref[0]
    group = chip_ref.shape[0]
    near = half_of(core, group)
    made = copies(
        [(key_near, key_grad_hbm.at[:, near]), (value_near, value_grad_hbm.at[:, near])], near_sems
    )
    start(made)
    for i in range(group):
        cols = slice(i * HEAD, (i + 1) * HEAD)
        head = (1 - core) * group + i
        key_grad_ref[:, cols], value_grad_ref[:, cols] = final_head(
            core, head, i, within_ref, k_ref, v_ref, key_part_ref, value_part_ref, chip_ref, lead_ref
        )
        stores = [
            pltpu.make_async_copy(a.at[:, cols], b.at[:, lanes(head)], sems.at[j, i])
            for j, (a, b) in enumerate(((key_grad_ref, key_grad_hbm), (value_grad_ref, value_grad_hbm)))
        ]
        start(stores)
        made = made + stores
    wait(made)


def shape(dims, dtype=F32):
    return jax.ShapeDtypeStruct(dims, dtype)


def swap(x):
    return lax.ppermute(x, "c", [(0, 1), (1, 0)])


def spread(x):
    return lax.all_to_all(x, CHIPS, split_axis=0, concat_axis=0, tiled=True)


def call(kernel, name, near, far, near_out, far_out, buffers, sems, core=None, aliases=(), mib=16):
    scalars = () if core is None else (core,)
    vmem = pl.BlockSpec(memory_space=pltpu.VMEM)
    hbm = pl.BlockSpec(memory_space=pl.ANY)
    return pl.pallas_call(
        kernel,
        grid_spec=pltpu.PrefetchScalarGridSpec(
            num_scalar_prefetch=len(scalars),
            grid=(1,),
            in_specs=[vmem] * len(near) + [hbm] * len(far),
            out_specs=[hbm] * len(far_out) + [vmem] * len(near_out),
            scratch_shapes=[pltpu.VMEM(x.shape, x.dtype) for x in buffers]
            + [pltpu.SemaphoreType.DMA(dims) for dims in sems],
        ),
        out_shape=[pltpu.HBM(x.shape, x.dtype) for x in far_out]
        + [pltpu.VMEM(x.shape, x.dtype) for x in near_out],
        input_output_aliases=dict(aliases),
        compiler_params=pltpu.CompilerParams(
            dimension_semantics=("arbitrary",), vmem_limit_bytes=mib * 2**20
        ),
        name=name,
    )(*scalars, *near, *(pltpu.with_memory_space_constraint(x, pltpu.HBM) for x in far))


def shards(queries, keys, values, gate, log_decay, out_grad):
    tokens, flat = queries.shape
    heads = log_decay.shape[1]
    group = heads // 2
    chips = lax.axis_size("x") * lax.axis_size("y")
    rows = group * HEAD // chips
    core = lax.axis_index("c").astype(jnp.int32).reshape(1)
    packed = shape((group, HEAD + PAD, HEAD))
    sliced = shape((chips, rows, HEAD))
    carried = shape((chips, rows + PAD, HEAD))
    wide = shape((tokens, flat))
    narrow = shape((tokens, flat), BF16)
    double = shape((tokens, 2 * flat), BF16)
    half = shape((tokens, flat // 2))
    half_narrow = shape((tokens, flat // 2), BF16)
    column = shape((tokens, HEAD))
    states = shape((heads, HEAD, HEAD))
    table_rows = shape((8, HEAD))
    sums_rows = shape((8, 8, HEAD))
    rates = shape((heads, tokens))
    table_of = shape((heads, tokens, tokens), BF16)

    def combined(lead, mine, other):
        return call(
            combine_kernel, "combine", (mine, other), (), (), (carried, packed, packed), (carried,), ((2 + group,),),
            lead,
        )

    def scanned(x, reverse):
        (out,) = call(
            lambda *refs: scan_kernel(reverse, *refs), "scan", (x,), (), (), (sliced,), (sliced,), ((1,),)
        )
        return out

    within, theirs, k_near, v_near = call(
        local_other_kernel, "local_other", (), (log_decay.T, keys, values),
        (rates, packed, half_narrow, half_narrow), (), (rates, half_narrow, half_narrow), ((5,),), core,
    )
    lead_mine = swap(theirs)
    (mine,) = call(
        local_mine_kernel, "local_mine", (within, k_near, v_near), (), (packed,), (), (), (), core
    )
    chip_state, mine, lead_mine = combined(1 - core, mine, lead_mine)
    chip_state = spread(chip_state)
    probs, intra = call(
        inside_kernel, "inside", (), (within, queries, keys, values), (), (table_of, wide),
        (rates, narrow, narrow, narrow, table_of, wide), ((1,), (3, heads), (3, heads)),
    )
    chip_state, probs, intra, mine, within = lax.optimization_barrier(
        (chip_state, probs, intra, mine, within)
    )
    chip_state, within = lax.optimization_barrier((scanned(chip_state, False), within))
    chip_mine = spread(chip_state)
    dnorm, grown = call(
        prepare_kernel, "prepare", (), (within, queries, gate, out_grad), (), (wide, double),
        (rates, narrow, narrow, narrow, wide, double), ((1,), (3, heads), (2, heads)),
    )
    chip_mine, mine, dnorm, grown = lax.optimization_barrier((chip_mine, mine, dnorm, grown))
    chip_mine = chip_mine.reshape(group, HEAD, HEAD)
    chip_other, lead_other = swap(chip_mine), swap(mine)
    attn, dnorm, grown, state, square, inner, intra_far, within_near = call(
        attn_mine_kernel, "attn_mine", (chip_mine,), (within, lead_mine, grown, intra, dnorm),
        (wide, wide, double, states, column, column, half, rates), (), (packed, half), ((8,),), core,
    )
    attn, state, sums = call(
        attn_other_kernel, "attn_other",
        (chip_other, lead_other, intra_far, square, inner, dnorm, grown, attn, state), (),
        (wide, states, sums_rows), (), (), (), core, {8: 0, 9: 1},
    )
    sums = lax.all_to_all(sums, "tp", split_axis=0, concat_axis=0, tiled=True)
    grad_far, theirs, scale, center, table = call(
        grad_other_kernel, "grad_other", (sums, within_near, grown, attn, dnorm), (),
        (half_narrow, packed, column, column, table_rows), (), (), (), core,
    )
    lead_mine = swap(theirs)
    grad, table, mine = call(
        grad_mine_kernel, "grad_mine",
        (scale, center, table, within_near, grown, attn, dnorm, grad_far), (),
        (packed,), (narrow, table_rows), (half_narrow,), ((group,), (2,)), core,
    )
    chip_state, mine, lead_mine = combined(core, mine, lead_mine)
    chip_state = spread(chip_state)
    query_grad, key_part = call(
        back_kernel, "back", (), (within, queries, keys, values, grad, state), (narrow,), (narrow,),
        (rates, narrow, narrow, narrow, narrow, states, narrow), ((1,), (5, heads), (1, heads)),
    )
    chip_state, key_part, mine, grad, table = lax.optimization_barrier(
        (chip_state, key_part, mine, grad, table)
    )
    chip_state, grad, table = lax.optimization_barrier((scanned(chip_state, True), grad, table))
    chip_mine = spread(chip_state)
    output, gate_grad, value_part = call(
        value_gate_kernel, "value_gate", (), (table, attn, gate, out_grad, grad, probs), (narrow,), (narrow, narrow),
        (table_rows, wide, narrow, narrow, narrow, table_of, narrow, narrow, column),
        ((1,), (6, heads), (2, heads)), mib=24,
    )
    chip_mine, value_part, output, gate_grad, mine = lax.optimization_barrier(
        (chip_mine, value_part, output, gate_grad, mine)
    )
    chip_mine = chip_mine.reshape(group, HEAD, HEAD)
    chip_other, lead_other = swap(chip_mine), swap(mine)
    key_near, value_near, k_far, v_far, within_near = call(
        final_mine_kernel, "final_mine", (chip_mine, key_part, value_part), (within, lead_mine, keys, values),
        (half_narrow,) * 4 + (rates,), (), (packed, half_narrow, half_narrow), ((6,),), core,
    )
    key_grad, value_grad = call(
        final_other_kernel, "final_other",
        (chip_other, lead_other, within_near, k_far, v_far, key_part, value_part, key_near, value_near), (),
        (), (narrow, narrow), (half_narrow, half_narrow), ((2,), (2, group)), core,
    )
    return output, query_grad, key_grad, value_grad, gate_grad


def solution(mesh):
    split = Mesh(mesh.devices.reshape(4, 4, 2, mesh.shape["tp"]), ("x", "y", "c", "tp"))
    return jax.shard_map(
        shards,
        mesh=split,
        in_specs=(P(SEQ, "tp"),) * 6,
        out_specs=(P(SEQ, "tp"),) * 5,
        check_vma=False,
    )
```

```python
import jax
import jax.numpy as jnp
from jax import lax
from jax.experimental import pallas as pl
from jax.experimental.pallas import tpu as pltpu
from jax.sharding import Mesh
from jax.sharding import PartitionSpec as P

HEAD_COUNT = 64
HEAD = 128
SEQ = ("x", "y", "c")
CHIPS = ("x", "y")
HIGH = lax.Precision.HIGHEST
F32 = jnp.float32
BF16 = jnp.bfloat16
PAD = 8

NN = (((1,), (0,)), ((), ()))
NT = (((1,), (1,)), ((), ()))
TN = (((0,), (0,)), ((), ()))


def dot(a, b, dims, precision=None):
    return lax.dot_general(a, b, dims, precision=precision, preferred_element_type=F32)


def halves(x):
    high = x.astype(BF16)
    return high, (x - high.astype(F32)).astype(BF16)


def as_column(row):
    return jnp.transpose(jnp.broadcast_to(row, (HEAD, row.shape[1])))


def sigmoid(x):
    return 1.0 / (1.0 + jnp.exp(-x))


def lanes(head, count=1):
    return pl.ds(pl.multiple_of(head * (count * HEAD), HEAD), count * HEAD)


def put_state(ref, i, state, factor):
    ref[i, 0:HEAD, :] = state
    ref[i, HEAD : HEAD + PAD, :] = jnp.broadcast_to(factor, (PAD, HEAD))


def outer_state(wide, narrow):
    both = dot(narrow, wide, TN)
    return both[:, :HEAD] + both[:, HEAD:]


def sum_over(rate_ref, within_ref, rate_copy):
    heads, tokens = rate_ref.shape
    early = lax.broadcasted_iota(jnp.int32, (tokens, tokens), 0)
    late = lax.broadcasted_iota(jnp.int32, (tokens, tokens), 1)
    upto = (early <= late).astype(F32).astype(BF16)
    rate_copy.wait()
    rate = rate_ref[...]
    high, rest = halves(rate)
    low = (rate - high.astype(F32) - rest.astype(F32)).astype(BF16)
    parts = jnp.concatenate([x.astype(F32) for x in (high, rest, low)], axis=0).astype(BF16)
    sums = dot(parts, upto, NN)
    within_ref[...] = sums[0:heads] + sums[heads : 2 * heads] + sums[2 * heads :]


def half_of(half, group, count=1):
    width = group * count * HEAD
    return pl.ds(pl.multiple_of(half * width, HEAD), width)


def copies(pairs, sems):
    return [pltpu.make_async_copy(a, b, sems.at[i]) for i, (a, b) in enumerate(pairs)]


def start(group):
    for copy in group:
        copy.start()


def wait(group):
    for copy in group:
        copy.wait()


def each_head(heads, body):
    def step(head, carry):
        body(head)
        return carry

    lax.fori_loop(0, heads, step, 0)


def each_pair(heads, before, work, after):
    def step(pair, carry):
        both = (2 * pair, 2 * pair + 1)
        for stage in (before, work, after):
            for head in both:
                stage(head)
        return carry

    lax.fori_loop(0, heads // 2, step, 0)


def head_copies(arrays, sems, head):
    made = []
    for i, (a, b, count) in enumerate(arrays):
        at = (head,) if count == 0 else (slice(None), lanes(head, count))
        made.append(pltpu.make_async_copy(a.at[at], b.at[at], sems.at[i, head]))
    return made


def local_state(head, cols, within_ref, k_ref, v_ref, out_ref, i):
    tokens = k_ref.shape[0]
    within = within_ref[pl.ds(head, 1), :]
    last = within[:, tokens - 1 :]
    tail = as_column(jnp.exp(last - within))
    scaled = jnp.concatenate(halves(k_ref[:, cols].astype(F32) * tail), axis=1)
    put_state(out_ref, i, outer_state(scaled, v_ref[:, cols]), jnp.exp(last))


def local_other_kernel(
    core_ref, rate_hbm, k_hbm, v_hbm, within_ref, out_ref, k_near, v_near, rate_ref, k_ref, v_ref, sems
):
    group = out_ref.shape[0]
    core = core_ref[0]
    far, near = half_of(1 - core, group), half_of(core, group)
    made = copies(
        [
            (rate_hbm, rate_ref),
            (v_hbm.at[:, far], v_ref),
            (k_hbm.at[:, far], k_ref),
            (v_hbm.at[:, near], v_near),
            (k_hbm.at[:, near], k_near),
        ],
        sems,
    )
    start(made)
    sum_over(rate_ref, within_ref, made[0])
    wait(made[1:3])
    for i in range(group):
        cols = slice(i * HEAD, (i + 1) * HEAD)
        local_state((1 - core) * group + i, cols, within_ref, k_ref, v_ref, out_ref, i)
    wait(made[3:])


def local_mine_kernel(core_ref, within_ref, k_ref, v_ref, out_ref):
    group = out_ref.shape[0]
    for i in range(group):
        cols = slice(i * HEAD, (i + 1) * HEAD)
        local_state(core_ref[0] * group + i, cols, within_ref, k_ref, v_ref, out_ref, i)


def combine_kernel(
    lead_ref, mine_ref, other_ref, out_hbm, mine_hbm, other_hbm, out_ref, sems
):
    group = mine_ref.shape[0]
    made = copies([(mine_ref, mine_hbm), (other_ref, other_hbm)], sems)
    lead = lead_ref[0] == 1
    rows = HEAD // 4
    for i in range(group):
        own = mine_ref[i, HEAD : HEAD + PAD, :]
        far = other_ref[i, HEAD : HEAD + PAD, :]
        mine = mine_ref[i, 0:HEAD, :]
        other = other_ref[i, 0:HEAD, :]
        both = jnp.where(lead, far[0:1] * mine + other, own[0:1] * other + mine)
        for j in range(4):
            out_ref[4 * i + j, 0:rows, :] = both[j * rows : (j + 1) * rows]
            if out_ref.shape[1] > rows:
                out_ref[4 * i + j, rows : rows + PAD, :] = own * far
        part = pl.ds(4 * i, 4)
        store = pltpu.make_async_copy(out_ref.at[part], out_hbm.at[part], sems.at[2 + i])
        store.start()
        made.append(store)
    start(made[:2])
    wait(made)


def scan_kernel(in_ref, out_hbm, decay_ref, out_ref, sems):
    chips, rows = out_ref.shape[0], out_ref.shape[1]
    state = jnp.zeros(out_ref.shape[1:], F32)
    for n in range(chips):
        out_ref[n] = state
        state = in_ref[n, rows : rows + 1, :] * state + in_ref[n, 0:rows, :]
        decay_ref[n] = in_ref[n, rows : rows + PAD, :]
    made = copies([(out_ref, out_hbm)], sems)
    start(made)
    wait(made)


def scan_back_kernel(in_ref, decay_ref, out_hbm, out_ref, sems):
    chips = out_ref.shape[0]
    state = jnp.zeros(out_ref.shape[1:], F32)
    for n in reversed(range(chips)):
        out_ref[n] = state
        state = decay_ref[n, 0:1, :] * state + in_ref[n]
    made = copies([(out_ref, out_hbm)], sems)
    start(made)
    wait(made)


def decayed(scores, left, within, column):
    size = scores.shape[1]
    rows = lax.broadcasted_iota(jnp.int32, (HEAD, HEAD), 0)
    cols = lax.broadcasted_iota(jnp.int32, (HEAD, HEAD), 1)
    bands = []
    for at in range(0, scores.shape[0], HEAD):
        band = scores[at : at + HEAD]
        own = column[left + at : left + at + HEAD]
        pieces = []
        before = min(at, size)
        if before:
            edge = within[:, left + at - 1 : left + at]
            grow = jnp.concatenate([jnp.exp(own - edge)] * (before // HEAD), axis=1)
            pieces.append(band[:, :before] * jnp.exp(edge - within[:, left : left + before]) * grow)
        if at < size:
            gap = own - within[:, left + at : left + at + HEAD]
            inside = jnp.where(rows >= cols, jnp.exp(jnp.minimum(gap, 0.0)), 0.0)
            pieces.append(band[:, at : at + HEAD] * inside)
        if at + HEAD < size:
            pieces.append(jnp.zeros((HEAD, size - at - HEAD), F32))
        bands.append(jnp.concatenate(pieces, axis=1).astype(BF16))
    return jnp.concatenate(bands, axis=0)


def inside_kernel(
    within_hbm, q_hbm, k_hbm, v_hbm, probs_hbm, intra_hbm,
    within_ref, q_ref, k_ref, v_ref, probs_ref, intra_ref, sem, in_sems, out_sems,
):
    heads = within_ref.shape[0]
    tokens = q_ref.shape[0]
    size = tokens // 2
    small = copies([(within_hbm, within_ref)], sem)
    start(small)
    loads = [(q_hbm, q_ref, 1), (k_hbm, k_ref, 1), (v_hbm, v_ref, 1)]
    each_head(heads, lambda h: start(head_copies(loads, in_sems, h)))
    wait(small)

    def results(h):
        upper, lower = pl.ds(0, size), pl.ds(size, size)
        pairs = [
            (probs_ref.at[h, upper, upper], probs_hbm.at[h, upper, upper]),
            (probs_ref.at[h, lower], probs_hbm.at[h, lower]),
            (intra_ref.at[:, lanes(h)], intra_hbm.at[:, lanes(h)]),
        ]
        return [pltpu.make_async_copy(a, b, out_sems.at[i, h]) for i, (a, b) in enumerate(pairs)]

    def one(h):
        within = within_ref[pl.ds(h, 1), :]
        column = as_column(within)
        q, k, v = q_ref[:, lanes(h)], k_ref[:, lanes(h)], v_ref[:, lanes(h)]
        early = decayed(dot(q, k[0:size], NT), 0, within, column)
        late = decayed(dot(q[size:], k[size:], NT), size, within, column)
        probs_ref[h, :, 0:size] = early
        probs_ref[h, size:tokens, size:tokens] = late
        intra = dot(early, v[0:size], NN)
        intra_ref[0:size, lanes(h)] = intra[0:size]
        intra_ref[size:tokens, lanes(h)] = intra[size:] + dot(late, v[size:], NN)

    each_pair(heads, lambda h: wait(head_copies(loads, in_sems, h)), one, lambda h: start(results(h)))
    each_head(heads, lambda h: wait(results(h)))


def prepare_kernel(gate_hbm, up_hbm, dnorm_hbm, gate_ref, up_ref, dnorm_ref, in_sems, out_sems):
    heads = in_sems.shape[1]
    loads = [(gate_hbm, gate_ref, 1), (up_hbm, up_ref, 1)]
    stores = [(dnorm_ref, dnorm_hbm, 1)]
    each_head(heads, lambda h: start(head_copies(loads, in_sems, h)))

    def one(h):
        dnorm_ref[:, lanes(h)] = up_ref[:, lanes(h)].astype(F32) * sigmoid(
            gate_ref[:, lanes(h)].astype(F32)
        )

    each_pair(
        heads, lambda h: wait(head_copies(loads, in_sems, h)), one,
        lambda h: start(head_copies(stores, out_sems, h)),
    )
    each_head(heads, lambda h: wait(head_copies(stores, out_sems, h)))


def pick_state(follows, chip_ref, lead_ref, i):
    chip = chip_ref[i]
    return jnp.where(
        follows, lead_ref[i, HEAD : HEAD + 1, :] * chip + lead_ref[i, 0:HEAD, :], chip
    )


def attn_head(core, head, i, at, grown_ref, intra_ref, dnorm_ref, chip_ref, lead_ref, attn_ref, state_ref):
    state = pick_state(core == 1, chip_ref, lead_ref, i)
    state_ref[head] = state
    high, low = halves(state)
    grown = grown_ref[:, lanes(head, 2)]
    attn = intra_ref[:, at] + dot(
        jnp.concatenate([grown, grown[:, :HEAD]], axis=1),
        jnp.concatenate([high, high, low], axis=1),
        NT,
    )
    attn_ref[:, lanes(head)] = attn
    return attn * attn, dnorm_ref[:, lanes(head)] * attn


def make_grown(head, q, within_ref, grown_ref):
    grown = q.astype(F32) * as_column(jnp.exp(within_ref[pl.ds(head, 1), :]))
    grown_ref[:, lanes(head, 2)] = jnp.concatenate(halves(grown), axis=1)


def attn_mine_kernel(
    core_ref, chip_ref, within_hbm, lead_hbm, q_hbm, intra_hbm, dnorm_hbm,
    attn_ref, dnorm_ref, grown_ref, state_ref, square_ref, inner_ref, intra_far, within_ref,
    lead_ref, intra_ref, q_ref, q_far, sems,
):
    core = core_ref[0]
    group = chip_ref.shape[0]
    pairs = [(within_hbm, within_ref), (lead_hbm, lead_ref)]
    for half, q, intra in ((core, q_ref, intra_ref), (1 - core, q_far, intra_far)):
        wide = half_of(half, group)
        pairs += [
            (q_hbm.at[:, wide], q),
            (intra_hbm.at[:, wide], intra),
            (dnorm_hbm.at[:, wide], dnorm_ref.at[:, wide]),
        ]
    made = copies(pairs, sems)
    start(made)
    wait(made[:5])
    square = inner = jnp.zeros(square_ref.shape, F32)
    for i in range(group):
        cols = slice(i * HEAD, (i + 1) * HEAD)
        head = core * group + i
        make_grown(head, q_ref[:, cols], within_ref, grown_ref)
        more = attn_head(
            core, head, i, cols, grown_ref, intra_ref, dnorm_ref, chip_ref, lead_ref, attn_ref, state_ref
        )
        square, inner = square + more[0], inner + more[1]
    square_ref[...] = square
    inner_ref[...] = inner
    made[5].wait()
    for i in range(group):
        cols = slice(i * HEAD, (i + 1) * HEAD)
        make_grown((1 - core) * group + i, q_far[:, cols], within_ref, grown_ref)
    wait(made[6:])


def attn_other_kernel(
    core_ref, chip_ref, lead_ref, intra_ref, square_ref, inner_ref, dnorm_ref, grown_ref, attn_in, state_in,
    attn_ref, state_ref, sums_ref,
):
    core = core_ref[0]
    group = chip_ref.shape[0]
    square, inner = square_ref[...], inner_ref[...]
    for i in range(group):
        more = attn_head(
            core, (1 - core) * group + i, i, slice(i * HEAD, (i + 1) * HEAD), grown_ref, intra_ref,
            dnorm_ref, chip_ref, lead_ref, attn_ref, state_ref,
        )
        square, inner = square + more[0], inner + more[1]
    ones = jnp.ones((8, HEAD), F32)
    square = dot(ones, square, NT, HIGH)
    inner = dot(ones, inner, NT, HIGH)
    rows = lax.broadcasted_iota(jnp.int32, (8, HEAD), 0)
    packed = jnp.zeros((8, HEAD), F32)
    for i in range(4):
        cols = slice(i * HEAD, (i + 1) * HEAD)
        packed = jnp.where(rows == i, square[:, cols], packed)
        packed = jnp.where(rows == i + 4, inner[:, cols], packed)
    sums_ref[...] = jnp.broadcast_to(packed[None], sums_ref.shape)


def grad_head(head, attn_ref, dnorm_ref, scale_ref, center_ref):
    scale = scale_ref[...]
    normed = attn_ref[:, lanes(head)] * scale
    return (scale * (dnorm_ref[:, lanes(head)] - normed * center_ref[...])).astype(BF16)


def grad_state(head, i, grad, within_ref, grown_ref, out_ref):
    last = within_ref[pl.ds(head, 1), :][:, grad.shape[0] - 1 :]
    put_state(out_ref, i, outer_state(grown_ref[:, lanes(head, 2)], grad), jnp.exp(last))


def grad_other_kernel(
    core_ref, sums_ref, within_ref, grown_ref, attn_ref, dnorm_ref,
    grad_ref, out_ref, scale_ref, center_ref, table_ref,
):
    total = jnp.sum(sums_ref[...], axis=0) / (HEAD_COUNT * HEAD)
    scale = lax.rsqrt(total[0:4] + 1e-06)
    center = scale * total[4:8]
    table_ref[0:4] = scale
    table_ref[4:8] = center
    for i in range(4):
        rows = slice(i * HEAD, (i + 1) * HEAD)
        scale_ref[rows] = as_column(scale[i : i + 1])
        center_ref[rows] = as_column(center[i : i + 1])
    group = out_ref.shape[0]
    for i in range(group):
        head = (1 - core_ref[0]) * group + i
        grad = grad_head(head, attn_ref, dnorm_ref, scale_ref, center_ref)
        grad_ref[:, i * HEAD : (i + 1) * HEAD] = grad
        grad_state(head, i, grad, within_ref, grown_ref, out_ref)


def grad_mine_kernel(
    core_ref, scale_ref, center_ref, table_ref, within_ref, grown_ref, attn_ref, dnorm_ref, grad_far,
    grad_hbm, table_hbm, out_ref, grad_ref, sems, far_sems,
):
    core = core_ref[0]
    group = out_ref.shape[0]
    made = copies(
        [(grad_far, grad_hbm.at[:, half_of(1 - core, group)]), (table_ref, table_hbm)], far_sems
    )
    start(made)
    for i in range(group):
        head = core * group + i
        cols = slice(i * HEAD, (i + 1) * HEAD)
        grad_ref[:, cols] = grad_head(head, attn_ref, dnorm_ref, scale_ref, center_ref)
        store = pltpu.make_async_copy(
            grad_ref.at[:, cols], grad_hbm.at[:, lanes(head)], sems.at[i]
        )
        store.start()
        made.append(store)
    for i in range(group):
        grad = grad_ref[:, i * HEAD : (i + 1) * HEAD]
        grad_state(core * group + i, i, grad, within_ref, grown_ref, out_ref)
    wait(made)


def back_kernel(
    within_hbm, q_hbm, k_hbm, v_hbm, grad_hbm, state_hbm, query_grad_hbm, key_ref,
    within_ref, q_ref, k_ref, v_ref, grad_ref, state_ref, query_grad_ref, sem, in_sems, out_sems,
):
    heads = within_ref.shape[0]
    tokens = q_ref.shape[0]
    size = tokens // 2
    small = copies([(within_hbm, within_ref)], sem)
    start(small)
    loads = [
        (grad_hbm, grad_ref, 1), (v_hbm, v_ref, 1), (k_hbm, k_ref, 1), (q_hbm, q_ref, 1),
        (state_hbm, state_ref, 0),
    ]
    stores = [(query_grad_ref, query_grad_hbm, 1)]
    each_head(heads, lambda h: start(head_copies(loads, in_sems, h)))
    wait(small)

    def one(h):
        within = within_ref[pl.ds(h, 1), :]
        column = as_column(within)
        grow = jnp.exp(column)
        at = lanes(h)
        q, k, v = q_ref[:, at], k_ref[:, at], v_ref[:, at]
        state = jnp.concatenate(halves(state_ref[h]), axis=0)
        grad = grad_ref[:, at]
        early = decayed(dot(grad, v[0:size], NT), 0, within, column)
        late = decayed(dot(grad[size:], v[size:], NT), size, within, column)
        query = dot(early, k[0:size], NN)
        query = jnp.concatenate([query[0:size], query[size:] + dot(late, k[size:], NN)], axis=0)
        inter = dot(jnp.concatenate([grad, grad], axis=1), state, NN)
        query_grad_ref[:, at] = (query + grow * inter).astype(BF16)
        key_ref[0:size, at] = dot(early, q, TN).astype(BF16)
        key_ref[size:tokens, at] = dot(late, q[size:], TN).astype(BF16)

    each_pair(
        heads, lambda h: wait(head_copies(loads, in_sems, h)), one,
        lambda h: start(head_copies(stores, out_sems, h)),
    )
    each_head(heads, lambda h: wait(head_copies(stores, out_sems, h)))


def value_gate_kernel(
    table_hbm, attn_hbm, gate_hbm, up_hbm, grad_hbm, probs_hbm, output_hbm, gate_grad_hbm, value_ref,
    table_ref, attn_ref, gate_ref, up_ref, grad_ref, probs_ref, output_ref, gate_grad_ref,
    scale_ref, sem, in_sems, out_sems,
):
    heads = probs_ref.shape[0]
    tokens = grad_ref.shape[0]
    size = tokens // 2
    small = copies([(table_hbm, table_ref)], sem)
    start(small)

    def loads(h):
        upper, lower = pl.ds(0, size), pl.ds(size, size)
        pairs = [
            (probs_hbm.at[h, upper, upper], probs_ref.at[h, upper, upper]),
            (probs_hbm.at[h, lower], probs_ref.at[h, lower]),
        ]
        pairs += [
            (a.at[:, lanes(h)], b.at[:, lanes(h)])
            for a, b in (
                (grad_hbm, grad_ref), (attn_hbm, attn_ref), (gate_hbm, gate_ref), (up_hbm, up_ref)
            )
        ]
        return [pltpu.make_async_copy(a, b, in_sems.at[i, h]) for i, (a, b) in enumerate(pairs)]

    stores = [(output_ref, output_hbm, 1), (gate_grad_ref, gate_grad_hbm, 1)]
    each_head(heads, lambda h: start(loads(h)))
    wait(small)
    for i in range(4):
        scale_ref[i * HEAD : (i + 1) * HEAD] = as_column(table_ref[i : i + 1])

    def one(h):
        at = lanes(h)
        early = dot(probs_ref[h, :, 0:size], grad_ref[:, at], TN)
        late = dot(probs_ref[h, size:tokens, size:tokens], grad_ref[size:tokens, at], TN)
        normed = attn_ref[:, at] * scale_ref[...]
        sig = sigmoid(gate_ref[:, at].astype(F32))
        output_ref[:, at] = (normed * sig).astype(BF16)
        gate_grad_ref[:, at] = (up_ref[:, at].astype(F32) * normed * sig * (1.0 - sig)).astype(BF16)
        value_ref[0:size, at] = early.astype(BF16)
        value_ref[size:tokens, at] = late.astype(BF16)

    each_pair(
        heads, lambda h: wait(loads(h)), one, lambda h: start(head_copies(stores, out_sems, h))
    )
    each_head(heads, lambda h: wait(head_copies(stores, out_sems, h)))


def final_head(core, head, i, within_ref, k_ref, v_ref, key_part_ref, value_part_ref, chip_ref, lead_ref):
    tokens = k_ref.shape[0]
    at = slice(i * HEAD, (i + 1) * HEAD)
    own = lanes(head)
    state = halves(pick_state(core == 0, chip_ref, lead_ref, i))
    within = within_ref[pl.ds(head, 1), :]
    tail = as_column(jnp.exp(within[:, tokens - 1 :] - within))
    k, v = k_ref[:, at], v_ref[:, at]
    key_inter = dot(jnp.concatenate([v, v], axis=1), jnp.concatenate(state, axis=0), NN)
    value_inter = dot(jnp.concatenate([k, k], axis=1), jnp.concatenate(state, axis=1), NT)
    return (
        (key_part_ref[:, own].astype(F32) + tail * key_inter).astype(BF16),
        (value_part_ref[:, own].astype(F32) + tail * value_inter).astype(BF16),
    )


def final_mine_kernel(
    core_ref, chip_ref, key_part_ref, value_part_ref, within_hbm, lead_hbm, k_hbm, v_hbm,
    key_grad_ref, value_grad_ref, k_far, v_far, within_ref, lead_ref, k_ref, v_ref, sems,
):
    core = core_ref[0]
    group = chip_ref.shape[0]
    near, far = half_of(core, group), half_of(1 - core, group)
    pairs = [(within_hbm, within_ref), (lead_hbm, lead_ref)]
    pairs += [(v_hbm.at[:, near], v_ref), (k_hbm.at[:, near], k_ref)]
    pairs += [(v_hbm.at[:, far], v_far), (k_hbm.at[:, far], k_far)]
    made = copies(pairs, sems)
    start(made)
    wait(made[:4])
    for i in range(group):
        cols = slice(i * HEAD, (i + 1) * HEAD)
        key_grad_ref[:, cols], value_grad_ref[:, cols] = final_head(
            core, core * group + i, i, within_ref, k_ref, v_ref, key_part_ref, value_part_ref,
            chip_ref, lead_ref,
        )
    wait(made[4:])


def final_other_kernel(
    core_ref, chip_ref, lead_ref, within_ref, k_ref, v_ref, key_part_ref, value_part_ref, key_near, value_near,
    key_grad_hbm, value_grad_hbm, key_grad_ref, value_grad_ref, near_sems, sems,
):
    core = core_ref[0]
    group = chip_ref.shape[0]
    near = half_of(core, group)
    made = copies(
        [(key_near, key_grad_hbm.at[:, near]), (value_near, value_grad_hbm.at[:, near])], near_sems
    )
    start(made)
    for i in range(group):
        cols = slice(i * HEAD, (i + 1) * HEAD)
        head = (1 - core) * group + i
        key_grad_ref[:, cols], value_grad_ref[:, cols] = final_head(
            core, head, i, within_ref, k_ref, v_ref, key_part_ref, value_part_ref, chip_ref, lead_ref
        )
        stores = [
            pltpu.make_async_copy(a.at[:, cols], b.at[:, lanes(head)], sems.at[j, i])
            for j, (a, b) in enumerate(((key_grad_ref, key_grad_hbm), (value_grad_ref, value_grad_hbm)))
        ]
        start(stores)
        made = made + stores
    wait(made)


def shape(dims, dtype=F32):
    return jax.ShapeDtypeStruct(dims, dtype)


def swap(x):
    return lax.ppermute(x, "c", [(0, 1), (1, 0)])


def spread(x):
    return lax.all_to_all(x, CHIPS, split_axis=0, concat_axis=0, tiled=True)


def call(kernel, name, near, far, near_out, far_out, buffers, sems, core=None, aliases=(), mib=16):
    scalars = () if core is None else (core,)
    vmem = pl.BlockSpec(memory_space=pltpu.VMEM)
    hbm = pl.BlockSpec(memory_space=pl.ANY)
    return pl.pallas_call(
        kernel,
        grid_spec=pltpu.PrefetchScalarGridSpec(
            num_scalar_prefetch=len(scalars),
            grid=(1,),
            in_specs=[vmem] * len(near) + [hbm] * len(far),
            out_specs=[hbm] * len(far_out) + [vmem] * len(near_out),
            scratch_shapes=[pltpu.VMEM(x.shape, x.dtype) for x in buffers]
            + [pltpu.SemaphoreType.DMA(dims) for dims in sems],
        ),
        out_shape=[pltpu.HBM(x.shape, x.dtype) for x in far_out]
        + [pltpu.VMEM(x.shape, x.dtype) for x in near_out],
        input_output_aliases=dict(aliases),
        compiler_params=pltpu.CompilerParams(
            dimension_semantics=("arbitrary",), vmem_limit_bytes=mib * 2**20
        ),
        name=name,
    )(*scalars, *near, *(pltpu.with_memory_space_constraint(x, pltpu.HBM) for x in far))


def shards(queries, keys, values, gate, log_decay, out_grad):
    tokens, flat = queries.shape
    heads = log_decay.shape[1]
    group = heads // 2
    chips = lax.axis_size("x") * lax.axis_size("y")
    rows = group * HEAD // chips
    core = lax.axis_index("c").astype(jnp.int32).reshape(1)
    packed = shape((group, HEAD + PAD, HEAD))
    sliced = shape((chips, rows, HEAD))
    carried = shape((chips, rows + PAD, HEAD))
    wide = shape((tokens, flat))
    narrow = shape((tokens, flat), BF16)
    double = shape((tokens, 2 * flat), BF16)
    half = shape((tokens, flat // 2))
    half_narrow = shape((tokens, flat // 2), BF16)
    column = shape((tokens, HEAD))
    states = shape((heads, HEAD, HEAD))
    table_rows = shape((8, HEAD))
    sums_rows = shape((8, 8, HEAD))
    rates = shape((heads, tokens))
    table_of = shape((heads, tokens, tokens), BF16)

    def combined(lead, mine, other, sent):
        return call(
            combine_kernel, "combine", (mine, other), (), (), (sent, packed, packed), (sent,), ((2 + group,),),
            lead,
        )

    def scanned(x, decays=None):
        if decays is None:
            return call(
                scan_kernel, "scan", (x,), (), (shape((chips, PAD, HEAD)),), (sliced,), (sliced,), ((1,),)
            )
        (out,) = call(scan_back_kernel, "scan_back", (x, decays), (), (), (sliced,), (sliced,), ((1,),))
        return out

    within, theirs, k_near, v_near = call(
        local_other_kernel, "local_other", (), (log_decay.T, keys, values),
        (rates, packed, half_narrow, half_narrow), (), (rates, half_narrow, half_narrow), ((5,),), core,
    )
    lead_mine = swap(theirs)
    (mine,) = call(
        local_mine_kernel, "local_mine", (within, k_near, v_near), (), (packed,), (), (), (), core
    )
    chip_state, mine, lead_mine = combined(1 - core, mine, lead_mine, carried)
    chip_state = spread(chip_state)
    lead_other = swap(mine)
    probs, intra = call(
        inside_kernel, "inside", (), (within, queries, keys, values), (), (table_of, wide),
        (rates, narrow, narrow, narrow, table_of, wide), ((1,), (3, heads), (3, heads)),
    )
    chip_state, probs, intra = lax.optimization_barrier((chip_state, probs, intra))
    chip_state, decays = scanned(chip_state)
    chip_state, out_grad = lax.optimization_barrier((chip_state, out_grad))
    chip_mine = spread(chip_state)
    (dnorm,) = call(
        prepare_kernel, "prepare", (), (gate, out_grad), (), (wide,), (narrow, narrow, wide),
        ((2, heads), (1, heads)),
    )
    chip_mine, dnorm = lax.optimization_barrier((chip_mine, dnorm))
    chip_mine = chip_mine.reshape(group, HEAD, HEAD)
    chip_other = swap(chip_mine)
    attn, dnorm, grown, state, square, inner, intra_far, within_near = call(
        attn_mine_kernel, "attn_mine", (chip_mine,), (within, lead_mine, queries, intra, dnorm),
        (wide, wide, double, states, column, column, half, rates), (), (packed, half, half_narrow, half_narrow),
        ((8,),), core,
    )
    attn, state, sums = call(
        attn_other_kernel, "attn_other",
        (chip_other, lead_other, intra_far, square, inner, dnorm, grown, attn, state), (),
        (wide, states, sums_rows), (), (), (), core, {8: 0, 9: 1},
    )
    sums = lax.all_to_all(sums, "tp", split_axis=0, concat_axis=0, tiled=True)
    grad_far, theirs, scale, center, table = call(
        grad_other_kernel, "grad_other", (sums, within_near, grown, attn, dnorm), (),
        (half_narrow, packed, column, column, table_rows), (), (), (), core,
    )
    lead_mine = swap(theirs)
    grad, table, mine = call(
        grad_mine_kernel, "grad_mine",
        (scale, center, table, within_near, grown, attn, dnorm, grad_far), (),
        (packed,), (narrow, table_rows), (half_narrow,), ((group,), (2,)), core,
    )
    chip_state, mine, lead_mine = combined(core, mine, lead_mine, sliced)
    chip_state = spread(chip_state)
    lead_other = swap(mine)
    query_grad, key_part = call(
        back_kernel, "back", (), (within, queries, keys, values, grad, state), (narrow,), (narrow,),
        (rates, narrow, narrow, narrow, narrow, states, narrow), ((1,), (5, heads), (1, heads)),
    )
    chip_state, key_part, grad, table = lax.optimization_barrier((chip_state, key_part, grad, table))
    chip_state, grad, table = lax.optimization_barrier((scanned(chip_state, decays), grad, table))
    chip_mine = spread(chip_state)
    output, gate_grad, value_part = call(
        value_gate_kernel, "value_gate", (), (table, attn, gate, out_grad, grad, probs), (narrow,), (narrow, narrow),
        (table_rows, wide, narrow, narrow, narrow, table_of, narrow, narrow, column),
        ((1,), (6, heads), (2, heads)), mib=24,
    )
    chip_mine, value_part, output, gate_grad = lax.optimization_barrier(
        (chip_mine, value_part, output, gate_grad)
    )
    chip_mine = chip_mine.reshape(group, HEAD, HEAD)
    chip_other = swap(chip_mine)
    key_near, value_near, k_far, v_far, within_near = call(
        final_mine_kernel, "final_mine", (chip_mine, key_part, value_part), (within, lead_mine, keys, values),
        (half_narrow,) * 4 + (rates,), (), (packed, half_narrow, half_narrow), ((6,),), core,
    )
    key_grad, value_grad = call(
        final_other_kernel, "final_other",
        (chip_other, lead_other, within_near, k_far, v_far, key_part, value_part, key_near, value_near), (),
        (), (narrow, narrow), (half_narrow, half_narrow), ((2,), (2, group)), core,
    )
    return output, query_grad, key_grad, value_grad, gate_grad


def solution(mesh):
    split = Mesh(mesh.devices.reshape(4, 4, 2, mesh.shape["tp"]), ("x", "y", "c", "tp"))
    return jax.shard_map(
        shards,
        mesh=split,
        in_specs=(P(SEQ, "tp"),) * 6,
        out_specs=(P(SEQ, "tp"),) * 5,
        check_vma=False,
    )
```

```python
import jax
import jax.numpy as jnp
from jax import lax
from jax.experimental import pallas as pl
from jax.experimental.pallas import tpu as pltpu
from jax.sharding import Mesh
from jax.sharding import PartitionSpec as P

HEAD_COUNT = 64
HEAD = 128
SEQ = ("x", "y", "c")
CHIPS = ("x", "y")
HIGH = lax.Precision.HIGHEST
F32 = jnp.float32
BF16 = jnp.bfloat16
PAD = 8

NN = (((1,), (0,)), ((), ()))
NT = (((1,), (1,)), ((), ()))
TN = (((0,), (0,)), ((), ()))


def dot(a, b, dims, precision=None):
    return lax.dot_general(a, b, dims, precision=precision, preferred_element_type=F32)


def halves(x):
    high = x.astype(BF16)
    return high, (x - high.astype(F32)).astype(BF16)


def as_column(row):
    return jnp.transpose(jnp.broadcast_to(row, (HEAD, row.shape[1])))


def sigmoid(x):
    return 1.0 / (1.0 + jnp.exp(-x))


def lanes(head, count=1):
    return pl.ds(pl.multiple_of(head * (count * HEAD), HEAD), count * HEAD)


def put_state(ref, i, state, factor):
    ref[i, 0:HEAD, :] = state
    ref[i, HEAD : HEAD + PAD, :] = jnp.broadcast_to(factor, (PAD, HEAD))


def outer_state(wide, narrow):
    both = dot(narrow, wide, TN)
    return both[:, :HEAD] + both[:, HEAD:]


def sum_over(rate_ref, within_ref, rate_copy):
    heads, tokens = rate_ref.shape
    early = lax.broadcasted_iota(jnp.int32, (tokens, tokens), 0)
    late = lax.broadcasted_iota(jnp.int32, (tokens, tokens), 1)
    upto = (early <= late).astype(F32).astype(BF16)
    rate_copy.wait()
    rate = rate_ref[...]
    high, rest = halves(rate)
    low = (rate - high.astype(F32) - rest.astype(F32)).astype(BF16)
    parts = jnp.concatenate([x.astype(F32) for x in (high, rest, low)], axis=0).astype(BF16)
    sums = dot(parts, upto, NN)
    within_ref[...] = sums[0:heads] + sums[heads : 2 * heads] + sums[2 * heads :]


def half_of(half, group, count=1):
    width = group * count * HEAD
    return pl.ds(pl.multiple_of(half * width, HEAD), width)


def copies(pairs, sems):
    return [pltpu.make_async_copy(a, b, sems.at[i]) for i, (a, b) in enumerate(pairs)]


def start(group):
    for copy in group:
        copy.start()


def wait(group):
    for copy in group:
        copy.wait()


def each_head(heads, body):
    def step(head, carry):
        body(head)
        return carry

    lax.fori_loop(0, heads, step, 0)


def each_pair(heads, before, work, after, count=2):
    def step(first, carry):
        for stage in (before, work, after):
            for i in range(count):
                stage(count * first + i)
        return carry

    lax.fori_loop(0, heads // count, step, 0)


def head_copies(arrays, sems, head):
    made = []
    for i, (a, b, count) in enumerate(arrays):
        at = (head,) if count == 0 else (slice(None), lanes(head, count))
        made.append(pltpu.make_async_copy(a.at[at], b.at[at], sems.at[i, head]))
    return made


def local_state(head, cols, within_ref, k_ref, v_ref, out_ref, i):
    tokens = k_ref.shape[0]
    within = within_ref[pl.ds(head, 1), :]
    last = within[:, tokens - 1 :]
    tail = as_column(jnp.exp(last - within))
    scaled = jnp.concatenate(halves(k_ref[:, cols].astype(F32) * tail), axis=1)
    put_state(out_ref, i, outer_state(scaled, v_ref[:, cols]), jnp.exp(last))


def local_other_kernel(
    core_ref, rate_hbm, k_hbm, v_hbm, within_ref, out_ref, k_near, v_near, rate_ref, k_ref, v_ref, sems
):
    group = out_ref.shape[0]
    core = core_ref[0]
    far, near = half_of(1 - core, group), half_of(core, group)
    made = copies(
        [
            (rate_hbm, rate_ref),
            (v_hbm.at[:, far], v_ref),
            (k_hbm.at[:, far], k_ref),
            (v_hbm.at[:, near], v_near),
            (k_hbm.at[:, near], k_near),
        ],
        sems,
    )
    start(made)
    sum_over(rate_ref, within_ref, made[0])
    wait(made[1:3])
    for i in range(group):
        cols = slice(i * HEAD, (i + 1) * HEAD)
        local_state((1 - core) * group + i, cols, within_ref, k_ref, v_ref, out_ref, i)
    wait(made[3:])


def local_mine_kernel(core_ref, within_ref, k_ref, v_ref, out_ref):
    group = out_ref.shape[0]
    for i in range(group):
        cols = slice(i * HEAD, (i + 1) * HEAD)
        local_state(core_ref[0] * group + i, cols, within_ref, k_ref, v_ref, out_ref, i)


def combine_kernel(
    lead_ref, mine_ref, other_ref, out_hbm, mine_hbm, other_hbm, out_ref, sems
):
    group = mine_ref.shape[0]
    made = copies([(mine_ref, mine_hbm), (other_ref, other_hbm)], sems)
    lead = lead_ref[0] == 1
    rows = HEAD // 4
    for i in range(group):
        own = mine_ref[i, HEAD : HEAD + PAD, :]
        far = other_ref[i, HEAD : HEAD + PAD, :]
        mine = mine_ref[i, 0:HEAD, :]
        other = other_ref[i, 0:HEAD, :]
        both = jnp.where(lead, far[0:1] * mine + other, own[0:1] * other + mine)
        for j in range(4):
            out_ref[4 * i + j, 0:rows, :] = both[j * rows : (j + 1) * rows]
            if out_ref.shape[1] > rows:
                out_ref[4 * i + j, rows : rows + PAD, :] = own * far
        part = pl.ds(4 * i, 4)
        store = pltpu.make_async_copy(out_ref.at[part], out_hbm.at[part], sems.at[2 + i])
        store.start()
        made.append(store)
    start(made[:2])
    wait(made)


def scan_kernel(in_ref, out_hbm, decay_ref, out_ref, sems):
    chips, rows = out_ref.shape[0], out_ref.shape[1]
    state = jnp.zeros(out_ref.shape[1:], F32)
    for n in range(chips):
        out_ref[n] = state
        state = in_ref[n, rows : rows + 1, :] * state + in_ref[n, 0:rows, :]
        decay_ref[n] = in_ref[n, rows : rows + PAD, :]
    made = copies([(out_ref, out_hbm)], sems)
    start(made)
    wait(made)


def scan_back_kernel(in_ref, decay_ref, out_hbm, out_ref, sems):
    chips = out_ref.shape[0]
    state = jnp.zeros(out_ref.shape[1:], F32)
    for n in reversed(range(chips)):
        out_ref[n] = state
        state = decay_ref[n, 0:1, :] * state + in_ref[n]
    made = copies([(out_ref, out_hbm)], sems)
    start(made)
    wait(made)


def decayed(scores, left, within, column):
    size = scores.shape[1]
    rows = lax.broadcasted_iota(jnp.int32, (HEAD, HEAD), 0)
    cols = lax.broadcasted_iota(jnp.int32, (HEAD, HEAD), 1)
    bands = []
    for at in range(0, scores.shape[0], HEAD):
        band = scores[at : at + HEAD]
        own = column[left + at : left + at + HEAD]
        pieces = []
        before = min(at, size)
        if before:
            edge = within[:, left + at - 1 : left + at]
            grow = jnp.concatenate([jnp.exp(own - edge)] * (before // HEAD), axis=1)
            pieces.append(band[:, :before] * jnp.exp(edge - within[:, left : left + before]) * grow)
        if at < size:
            gap = own - within[:, left + at : left + at + HEAD]
            inside = jnp.where(rows >= cols, jnp.exp(jnp.minimum(gap, 0.0)), 0.0)
            pieces.append(band[:, at : at + HEAD] * inside)
        if at + HEAD < size:
            pieces.append(jnp.zeros((HEAD, size - at - HEAD), F32))
        bands.append(jnp.concatenate(pieces, axis=1).astype(BF16))
    return jnp.concatenate(bands, axis=0)


def inside_kernel(
    within_hbm, q_hbm, k_hbm, v_hbm, probs_hbm, intra_hbm,
    within_ref, q_ref, k_ref, v_ref, probs_ref, intra_ref, sem, in_sems, out_sems,
):
    heads = within_ref.shape[0]
    tokens = q_ref.shape[0]
    size = tokens // 2
    small = copies([(within_hbm, within_ref)], sem)
    start(small)
    loads = [(q_hbm, q_ref, 1), (k_hbm, k_ref, 1), (v_hbm, v_ref, 1)]
    each_head(heads, lambda h: start(head_copies(loads, in_sems, h)))
    wait(small)

    def results(h):
        upper, lower = pl.ds(0, size), pl.ds(size, size)
        pairs = [
            (probs_ref.at[h, upper], probs_hbm.at[h, upper]),
            (probs_ref.at[h, lower, lower], probs_hbm.at[h, lower, lower]),
            (intra_ref.at[:, lanes(h)], intra_hbm.at[:, lanes(h)]),
        ]
        return [pltpu.make_async_copy(a, b, out_sems.at[i, h]) for i, (a, b) in enumerate(pairs)]

    def one(h):
        within = within_ref[pl.ds(h, 1), :]
        column = as_column(within)
        q, k, v = q_ref[:, lanes(h)], k_ref[:, lanes(h)], v_ref[:, lanes(h)]
        early = decayed(dot(q, k[0:size], NT), 0, within, column)
        late = decayed(dot(q[size:], k[size:], NT), size, within, column)
        probs_ref[h, 0:size, :] = jnp.transpose(early)
        probs_ref[h, size:tokens, size:tokens] = jnp.transpose(late)
        intra = dot(early, v[0:size], NN)
        intra_ref[0:size, lanes(h)] = intra[0:size]
        intra_ref[size:tokens, lanes(h)] = intra[size:] + dot(late, v[size:], NN)

    each_pair(heads, lambda h: wait(head_copies(loads, in_sems, h)), one, lambda h: start(results(h)))
    each_head(heads, lambda h: wait(results(h)))


def prepare_kernel(gate_hbm, up_hbm, dnorm_hbm, gate_ref, up_ref, dnorm_ref, in_sems, out_sems):
    heads = in_sems.shape[1]
    loads = [(gate_hbm, gate_ref, 1), (up_hbm, up_ref, 1)]
    stores = [(dnorm_ref, dnorm_hbm, 1)]
    each_head(heads, lambda h: start(head_copies(loads, in_sems, h)))

    def one(h):
        dnorm_ref[:, lanes(h)] = up_ref[:, lanes(h)].astype(F32) * sigmoid(
            gate_ref[:, lanes(h)].astype(F32)
        )

    each_pair(
        heads, lambda h: wait(head_copies(loads, in_sems, h)), one,
        lambda h: start(head_copies(stores, out_sems, h)),
    )
    each_head(heads, lambda h: wait(head_copies(stores, out_sems, h)))


def pick_state(follows, chip_ref, lead_ref, i):
    chip = chip_ref[i]
    return jnp.where(
        follows, lead_ref[i, HEAD : HEAD + 1, :] * chip + lead_ref[i, 0:HEAD, :], chip
    )


def attn_head(core, head, i, at, grown_ref, intra_ref, dnorm_ref, chip_ref, lead_ref, attn_ref, state_ref):
    state = pick_state(core == 1, chip_ref, lead_ref, i)
    state_ref[head] = state
    high, low = halves(state)
    grown = grown_ref[:, lanes(head, 2)]
    attn = intra_ref[:, at] + dot(
        jnp.concatenate([grown, grown[:, :HEAD]], axis=1),
        jnp.concatenate([high, high, low], axis=1),
        NT,
    )
    attn_ref[:, lanes(head)] = attn
    return attn * attn, dnorm_ref[:, lanes(head)] * attn


def make_grown(head, q, within_ref, grown_ref):
    grown = q.astype(F32) * as_column(jnp.exp(within_ref[pl.ds(head, 1), :]))
    grown_ref[:, lanes(head, 2)] = jnp.concatenate(halves(grown), axis=1)


def attn_mine_kernel(
    core_ref, chip_ref, within_hbm, lead_hbm, q_hbm, intra_hbm, dnorm_hbm,
    attn_ref, dnorm_ref, grown_ref, state_ref, square_ref, inner_ref, intra_far, within_ref,
    lead_ref, intra_ref, q_ref, q_far, sems,
):
    core = core_ref[0]
    group = chip_ref.shape[0]
    near, far = half_of(core, group), half_of(1 - core, group)
    made = copies(
        [
            (within_hbm, within_ref),
            (q_hbm.at[:, near], q_ref),
            (lead_hbm, lead_ref),
            (intra_hbm.at[:, near], intra_ref),
            (dnorm_hbm.at[:, near], dnorm_ref.at[:, near]),
            (q_hbm.at[:, far], q_far),
            (intra_hbm.at[:, far], intra_far),
            (dnorm_hbm.at[:, far], dnorm_ref.at[:, far]),
        ],
        sems,
    )
    start(made)
    wait(made[:2])
    for i in range(group):
        cols = slice(i * HEAD, (i + 1) * HEAD)
        make_grown(core * group + i, q_ref[:, cols], within_ref, grown_ref)
    wait(made[2:5])
    square = inner = jnp.zeros(square_ref.shape, F32)
    for i in range(group):
        cols = slice(i * HEAD, (i + 1) * HEAD)
        more = attn_head(
            core, core * group + i, i, cols, grown_ref, intra_ref, dnorm_ref, chip_ref, lead_ref, attn_ref,
            state_ref,
        )
        square, inner = square + more[0], inner + more[1]
    square_ref[...] = square
    inner_ref[...] = inner
    made[5].wait()
    for i in range(group):
        cols = slice(i * HEAD, (i + 1) * HEAD)
        make_grown((1 - core) * group + i, q_far[:, cols], within_ref, grown_ref)
    wait(made[6:])


def attn_other_kernel(
    core_ref, chip_ref, lead_ref, intra_ref, square_ref, inner_ref, dnorm_ref, grown_ref, attn_in, state_in,
    attn_ref, state_ref, sums_ref,
):
    core = core_ref[0]
    group = chip_ref.shape[0]
    square, inner = square_ref[...], inner_ref[...]
    for i in range(group):
        more = attn_head(
            core, (1 - core) * group + i, i, slice(i * HEAD, (i + 1) * HEAD), grown_ref, intra_ref,
            dnorm_ref, chip_ref, lead_ref, attn_ref, state_ref,
        )
        square, inner = square + more[0], inner + more[1]
    ones = jnp.ones((8, HEAD), F32)
    square = dot(ones, square, NT, HIGH)
    inner = dot(ones, inner, NT, HIGH)
    rows = lax.broadcasted_iota(jnp.int32, (8, HEAD), 0)
    packed = jnp.zeros((8, HEAD), F32)
    for i in range(4):
        cols = slice(i * HEAD, (i + 1) * HEAD)
        packed = jnp.where(rows == i, square[:, cols], packed)
        packed = jnp.where(rows == i + 4, inner[:, cols], packed)
    sums_ref[...] = jnp.broadcast_to(packed[None], sums_ref.shape)


def grad_head(head, attn_ref, dnorm_ref, scale_ref, center_ref):
    scale = scale_ref[...]
    normed = attn_ref[:, lanes(head)] * scale
    return (scale * (dnorm_ref[:, lanes(head)] - normed * center_ref[...])).astype(BF16)


def grad_state(head, i, grad, within_ref, grown_ref, out_ref):
    last = within_ref[pl.ds(head, 1), :][:, grad.shape[0] - 1 :]
    put_state(out_ref, i, outer_state(grown_ref[:, lanes(head, 2)], grad), jnp.exp(last))


def grad_other_kernel(
    core_ref, sums_ref, within_ref, grown_ref, attn_ref, dnorm_ref,
    grad_ref, out_ref, scale_ref, center_ref, table_ref,
):
    total = jnp.sum(sums_ref[...], axis=0) / (HEAD_COUNT * HEAD)
    scale = lax.rsqrt(total[0:4] + 1e-06)
    center = scale * total[4:8]
    table_ref[0:4] = scale
    table_ref[4:8] = center
    for i in range(4):
        rows = slice(i * HEAD, (i + 1) * HEAD)
        scale_ref[rows] = as_column(scale[i : i + 1])
        center_ref[rows] = as_column(center[i : i + 1])
    group = out_ref.shape[0]
    for i in range(group):
        head = (1 - core_ref[0]) * group + i
        grad = grad_head(head, attn_ref, dnorm_ref, scale_ref, center_ref)
        grad_ref[:, lanes(head)] = grad
        grad_state(head, i, grad, within_ref, grown_ref, out_ref)


def grad_mine_kernel(
    core_ref, scale_ref, center_ref, table_ref, within_ref, grown_ref, attn_ref, dnorm_ref, grad_in,
    table_hbm, grad_ref, out_ref, sems,
):
    made = copies([(table_ref, table_hbm)], sems)
    start(made)
    group = out_ref.shape[0]
    for i in range(group):
        head = core_ref[0] * group + i
        grad = grad_head(head, attn_ref, dnorm_ref, scale_ref, center_ref)
        grad_ref[:, lanes(head)] = grad
        grad_state(head, i, grad, within_ref, grown_ref, out_ref)
    wait(made)


def back_kernel(
    grad_ref, within_hbm, q_hbm, k_hbm, v_hbm, state_hbm, query_grad_hbm, key_ref,
    within_ref, q_ref, k_ref, v_ref, state_ref, query_grad_ref, sem, in_sems, out_sems,
):
    heads = within_ref.shape[0]
    tokens = q_ref.shape[0]
    size = tokens // 2
    small = copies([(within_hbm, within_ref)], sem)
    start(small)
    loads = [
        (v_hbm, v_ref, 1), (k_hbm, k_ref, 1), (q_hbm, q_ref, 1), (state_hbm, state_ref, 0),
    ]
    stores = [(query_grad_ref, query_grad_hbm, 1)]
    each_head(heads, lambda h: start(head_copies(loads, in_sems, h)))
    wait(small)

    def one(h):
        within = within_ref[pl.ds(h, 1), :]
        column = as_column(within)
        grow = jnp.exp(column)
        at = lanes(h)
        q, k, v = q_ref[:, at], k_ref[:, at], v_ref[:, at]
        state = jnp.concatenate(halves(state_ref[h]), axis=0)
        grad = grad_ref[:, at]
        early = decayed(dot(grad, v[0:size], NT), 0, within, column)
        late = decayed(dot(grad[size:], v[size:], NT), size, within, column)
        query = dot(early, k[0:size], NN)
        query = jnp.concatenate([query[0:size], query[size:] + dot(late, k[size:], NN)], axis=0)
        inter = dot(jnp.concatenate([grad, grad], axis=1), state, NN)
        query_grad_ref[:, at] = (query + grow * inter).astype(BF16)
        key_ref[0:size, at] = dot(early, q, TN).astype(BF16)
        key_ref[size:tokens, at] = dot(late, q[size:], TN).astype(BF16)

    each_pair(
        heads, lambda h: wait(head_copies(loads, in_sems, h)), one,
        lambda h: start(head_copies(stores, out_sems, h)),
    )
    each_head(heads, lambda h: wait(head_copies(stores, out_sems, h)))


def value_gate_kernel(
    grad_ref, table_hbm, attn_hbm, gate_hbm, up_hbm, probs_hbm, output_hbm, gate_grad_hbm, value_ref,
    table_ref, attn_ref, gate_ref, up_ref, probs_ref, output_ref, gate_grad_ref,
    scale_ref, sem, in_sems, out_sems,
):
    heads = probs_ref.shape[0]
    tokens = grad_ref.shape[0]
    size = tokens // 2
    small = copies([(table_hbm, table_ref)], sem)
    start(small)

    def loads(h):
        upper, lower = pl.ds(0, size), pl.ds(size, size)
        pairs = [
            (probs_hbm.at[h, upper], probs_ref.at[h, upper]),
            (probs_hbm.at[h, lower, lower], probs_ref.at[h, lower, lower]),
        ]
        pairs += [
            (a.at[:, lanes(h)], b.at[:, lanes(h)])
            for a, b in (
                (attn_hbm, attn_ref), (gate_hbm, gate_ref), (up_hbm, up_ref)
            )
        ]
        return [pltpu.make_async_copy(a, b, in_sems.at[i, h]) for i, (a, b) in enumerate(pairs)]

    stores = [(output_ref, output_hbm, 1), (gate_grad_ref, gate_grad_hbm, 1)]
    each_head(heads, lambda h: start(loads(h)))
    wait(small)
    for i in range(4):
        scale_ref[i * HEAD : (i + 1) * HEAD] = as_column(table_ref[i : i + 1])

    def one(h):
        at = lanes(h)
        early = dot(probs_ref[h, 0:size, :], grad_ref[:, at], NN)
        late = dot(probs_ref[h, size:tokens, size:tokens], grad_ref[size:tokens, at], NN)
        normed = attn_ref[:, at] * scale_ref[...]
        sig = sigmoid(gate_ref[:, at].astype(F32))
        output_ref[:, at] = (normed * sig).astype(BF16)
        gate_grad_ref[:, at] = (up_ref[:, at].astype(F32) * normed * sig * (1.0 - sig)).astype(BF16)
        value_ref[0:size, at] = early.astype(BF16)
        value_ref[size:tokens, at] = late.astype(BF16)

    each_pair(
        heads, lambda h: wait(loads(h)), one, lambda h: start(head_copies(stores, out_sems, h)), 1
    )
    each_head(heads, lambda h: wait(head_copies(stores, out_sems, h)))


def final_head(core, head, i, within_ref, k_ref, v_ref, key_part_ref, value_part_ref, chip_ref, lead_ref):
    tokens = k_ref.shape[0]
    at = slice(i * HEAD, (i + 1) * HEAD)
    own = lanes(head)
    state = halves(pick_state(core == 0, chip_ref, lead_ref, i))
    within = within_ref[pl.ds(head, 1), :]
    tail = as_column(jnp.exp(within[:, tokens - 1 :] - within))
    k, v = k_ref[:, at], v_ref[:, at]
    key_inter = dot(jnp.concatenate([v, v], axis=1), jnp.concatenate(state, axis=0), NN)
    value_inter = dot(jnp.concatenate([k, k], axis=1), jnp.concatenate(state, axis=1), NT)
    return (
        (key_part_ref[:, own].astype(F32) + tail * key_inter).astype(BF16),
        (value_part_ref[:, own].astype(F32) + tail * value_inter).astype(BF16),
    )


def final_mine_kernel(
    core_ref, chip_ref, key_part_ref, value_part_ref, within_hbm, lead_hbm, k_hbm, v_hbm,
    key_grad_ref, value_grad_ref, k_far, v_far, within_ref, lead_ref, k_ref, v_ref, sems,
):
    core = core_ref[0]
    group = chip_ref.shape[0]
    near, far = half_of(core, group), half_of(1 - core, group)
    pairs = [(within_hbm, within_ref), (lead_hbm, lead_ref)]
    pairs += [(v_hbm.at[:, near], v_ref), (k_hbm.at[:, near], k_ref)]
    pairs += [(v_hbm.at[:, far], v_far), (k_hbm.at[:, far], k_far)]
    made = copies(pairs, sems)
    start(made)
    wait(made[:4])
    for i in range(group):
        cols = slice(i * HEAD, (i + 1) * HEAD)
        key_grad_ref[:, cols], value_grad_ref[:, cols] = final_head(
            core, core * group + i, i, within_ref, k_ref, v_ref, key_part_ref, value_part_ref,
            chip_ref, lead_ref,
        )
    wait(made[4:])


def final_other_kernel(
    core_ref, chip_ref, lead_ref, within_ref, k_ref, v_ref, key_part_ref, value_part_ref, key_near, value_near,
    key_grad_hbm, value_grad_hbm, key_grad_ref, value_grad_ref, near_sems, sems,
):
    core = core_ref[0]
    group = chip_ref.shape[0]
    near = half_of(core, group)
    made = copies(
        [(key_near, key_grad_hbm.at[:, near]), (value_near, value_grad_hbm.at[:, near])], near_sems
    )
    start(made)
    for i in range(group):
        cols = slice(i * HEAD, (i + 1) * HEAD)
        head = (1 - core) * group + i
        key_grad_ref[:, cols], value_grad_ref[:, cols] = final_head(
            core, head, i, within_ref, k_ref, v_ref, key_part_ref, value_part_ref, chip_ref, lead_ref
        )
        stores = [
            pltpu.make_async_copy(a.at[:, cols], b.at[:, lanes(head)], sems.at[j, i])
            for j, (a, b) in enumerate(((key_grad_ref, key_grad_hbm), (value_grad_ref, value_grad_hbm)))
        ]
        start(stores)
        made = made + stores
    wait(made)


def shape(dims, dtype=F32):
    return jax.ShapeDtypeStruct(dims, dtype)


def swap(x):
    return lax.ppermute(x, "c", [(0, 1), (1, 0)])


def spread(x):
    return lax.all_to_all(x, CHIPS, split_axis=0, concat_axis=0, tiled=True)


def call(kernel, name, near, far, near_out, far_out, buffers, sems, core=None, aliases=(), mib=16):
    scalars = () if core is None else (core,)
    vmem = pl.BlockSpec(memory_space=pltpu.VMEM)
    hbm = pl.BlockSpec(memory_space=pl.ANY)
    return pl.pallas_call(
        kernel,
        grid_spec=pltpu.PrefetchScalarGridSpec(
            num_scalar_prefetch=len(scalars),
            grid=(1,),
            in_specs=[vmem] * len(near) + [hbm] * len(far),
            out_specs=[hbm] * len(far_out) + [vmem] * len(near_out),
            scratch_shapes=[pltpu.VMEM(x.shape, x.dtype) for x in buffers]
            + [pltpu.SemaphoreType.DMA(dims) for dims in sems],
        ),
        out_shape=[pltpu.HBM(x.shape, x.dtype) for x in far_out]
        + [pltpu.VMEM(x.shape, x.dtype) for x in near_out],
        input_output_aliases=dict(aliases),
        compiler_params=pltpu.CompilerParams(
            dimension_semantics=("arbitrary",), vmem_limit_bytes=mib * 2**20
        ),
        name=name,
    )(*scalars, *near, *(pltpu.with_memory_space_constraint(x, pltpu.HBM) for x in far))


def shards(queries, keys, values, gate, log_decay, out_grad):
    tokens, flat = queries.shape
    heads = log_decay.shape[1]
    group = heads // 2
    chips = lax.axis_size("x") * lax.axis_size("y")
    rows = group * HEAD // chips
    core = lax.axis_index("c").astype(jnp.int32).reshape(1)
    packed = shape((group, HEAD + PAD, HEAD))
    sliced = shape((chips, rows, HEAD))
    carried = shape((chips, rows + PAD, HEAD))
    wide = shape((tokens, flat))
    narrow = shape((tokens, flat), BF16)
    double = shape((tokens, 2 * flat), BF16)
    half = shape((tokens, flat // 2))
    half_narrow = shape((tokens, flat // 2), BF16)
    column = shape((tokens, HEAD))
    states = shape((heads, HEAD, HEAD))
    table_rows = shape((8, HEAD))
    sums_rows = shape((8, 8, HEAD))
    rates = shape((heads, tokens))
    table_of = shape((heads, tokens, tokens), BF16)

    def combined(lead, mine, other, sent):
        return call(
            combine_kernel, "combine", (mine, other), (), (), (sent, packed, packed), (sent,), ((2 + group,),),
            lead,
        )

    def scanned(x, decays=None):
        if decays is None:
            return call(
                scan_kernel, "scan", (x,), (), (shape((chips, PAD, HEAD)),), (sliced,), (sliced,), ((1,),)
            )
        (out,) = call(scan_back_kernel, "scan_back", (x, decays), (), (), (sliced,), (sliced,), ((1,),))
        return out

    within, theirs, k_near, v_near = call(
        local_other_kernel, "local_other", (), (log_decay.T, keys, values),
        (rates, packed, half_narrow, half_narrow), (), (rates, half_narrow, half_narrow), ((5,),), core,
    )
    lead_mine = swap(theirs)
    (mine,) = call(
        local_mine_kernel, "local_mine", (within, k_near, v_near), (), (packed,), (), (), (), core
    )
    chip_state, mine, lead_mine = combined(1 - core, mine, lead_mine, carried)
    chip_state = spread(chip_state)
    lead_other = swap(mine)
    probs, intra = call(
        inside_kernel, "inside", (), (within, queries, keys, values), (), (table_of, wide),
        (rates, narrow, narrow, narrow, table_of, wide), ((1,), (3, heads), (3, heads)),
    )
    chip_state, probs, intra = lax.optimization_barrier((chip_state, probs, intra))
    chip_state, decays = scanned(chip_state)
    chip_state, out_grad = lax.optimization_barrier((chip_state, out_grad))
    chip_mine = spread(chip_state)
    (dnorm,) = call(
        prepare_kernel, "prepare", (), (gate, out_grad), (), (wide,), (narrow, narrow, wide),
        ((2, heads), (1, heads)),
    )
    chip_mine, dnorm = lax.optimization_barrier((chip_mine, dnorm))
    chip_mine = chip_mine.reshape(group, HEAD, HEAD)
    chip_other = swap(chip_mine)
    attn, dnorm, grown, state, square, inner, intra_far, within_near = call(
        attn_mine_kernel, "attn_mine", (chip_mine,), (within, lead_mine, queries, intra, dnorm),
        (wide, wide, double, states, column, column, half, rates), (), (packed, half, half_narrow, half_narrow),
        ((8,),), core,
    )
    attn, state, sums = call(
        attn_other_kernel, "attn_other",
        (chip_other, lead_other, intra_far, square, inner, dnorm, grown, attn, state), (),
        (wide, states, sums_rows), (), (), (), core, {8: 0, 9: 1},
    )
    sums = lax.all_to_all(sums, "tp", split_axis=0, concat_axis=0, tiled=True)
    grad, theirs, scale, center, table = call(
        grad_other_kernel, "grad_other", (sums, within_near, grown, attn, dnorm), (),
        (narrow, packed, column, column, table_rows), (), (), (), core,
    )
    lead_mine = swap(theirs)
    table, grad, mine = call(
        grad_mine_kernel, "grad_mine",
        (scale, center, table, within_near, grown, attn, dnorm, grad), (),
        (narrow, packed), (table_rows,), (), ((1,),), core, {8: 1},
    )
    chip_state, mine, lead_mine = combined(core, mine, lead_mine, sliced)
    chip_state = spread(chip_state)
    query_grad, key_part = call(
        back_kernel, "back", (grad,), (within, queries, keys, values, state), (narrow,), (narrow,),
        (rates, narrow, narrow, narrow, states, narrow), ((1,), (4, heads), (1, heads)),
    )
    chip_state, key_part, grad, table = lax.optimization_barrier((chip_state, key_part, grad, table))
    chip_state, grad, table = lax.optimization_barrier((scanned(chip_state, decays), grad, table))
    chip_mine = spread(chip_state)
    output, gate_grad, value_part = call(
        value_gate_kernel, "value_gate", (grad,), (table, attn, gate, out_grad, probs), (narrow,), (narrow, narrow),
        (table_rows, wide, narrow, narrow, table_of, narrow, narrow, column),
        ((1,), (5, heads), (2, heads)), mib=24,
    )
    chip_mine, value_part, output, gate_grad, mine = lax.optimization_barrier(
        (chip_mine, value_part, output, gate_grad, mine)
    )
    chip_mine = chip_mine.reshape(group, HEAD, HEAD)
    chip_other, lead_other = swap(chip_mine), swap(mine)
    key_near, value_near, k_far, v_far, within_near = call(
        final_mine_kernel, "final_mine", (chip_mine, key_part, value_part), (within, lead_mine, keys, values),
        (half_narrow,) * 4 + (rates,), (), (packed, half_narrow, half_narrow), ((6,),), core,
    )
    key_grad, value_grad = call(
        final_other_kernel, "final_other",
        (chip_other, lead_other, within_near, k_far, v_far, key_part, value_part, key_near, value_near), (),
        (), (narrow, narrow), (half_narrow, half_narrow), ((2,), (2, group)), core,
    )
    return output, query_grad, key_grad, value_grad, gate_grad


def solution(mesh):
    split = Mesh(mesh.devices.reshape(4, 4, 2, mesh.shape["tp"]), ("x", "y", "c", "tp"))
    return jax.shard_map(
        shards,
        mesh=split,
        in_specs=(P(SEQ, "tp"),) * 6,
        out_specs=(P(SEQ, "tp"),) * 5,
        check_vma=False,
    )
```
